128 devices in a mesh: ctx: 32 (over x_lo, y, z), shard: 4 (over x_hi, core).
Axes of the slice: x: 4 (x_hi: 2, x_lo: 2; x = x_hi * 2 + x_lo), y: 4, z: 4, core: 2. Of those that a mesh axis runs over, the one named last changes fastest.
Arguments:
- block_in: bfloat16 [2, 4096, 1024], P(None, 'ctx', 'shard'), may hold values from -6 to 6
- block_pairs: int32 [32, 2], replicated, may hold values from 0 to 63, as said below
- attn_gain: float32 [1024], replicated, may hold values from 0.1 to 1.9
- query_gain: float32 [64], replicated, may hold values from 0.1 to 1.9
- key_gain: float32 [64], replicated, may hold values from 0.1 to 1.9
- ffn_gain: float32 [1024], replicated, may hold values from 0.1 to 1.9
- w_query: bfloat16 [1024, 1024], P('ctx', 'shard'), may hold values from -0.1875 to 0.1875
- w_key: bfloat16 [1024, 512], P('ctx', 'shard'), may hold values from -0.1875 to 0.1875
- w_value: bfloat16 [1024, 512], P('ctx', 'shard'), may hold values from -0.1875 to 0.1875
- w_output: bfloat16 [1024, 1024], P('shard', 'ctx'), may hold values from -1.5 to 1.5
- w_gate: bfloat16 [1024, 4608], P('ctx', 'shard'), may hold values from -0.1875 to 0.1875
- w_up: bfloat16 [1024, 4608], P('ctx', 'shard'), may hold values from -0.1875 to 0.1875
- w_down: bfloat16 [4608, 1024], P('shard', 'ctx'), may hold values from -0.09375 to 0.09375
- grad_output: bfloat16 [2, 4096, 1024], P(None, 'ctx', 'shard'), may hold values from -6 to 6
Outputs:
- block_out: bfloat16 [2, 4096, 1024], P(None, 'ctx', 'shard')
- input_grad: float32 [2, 4096, 1024], P(None, 'ctx', 'shard')
- attn_gain_grad: float32 [1024], replicated
- query_gain_grad: float32 [64], replicated
- key_gain_grad: float32 [64], replicated
- ffn_gain_grad: float32 [1024], replicated
- query_grad: float32 [1024, 1024], P('ctx', 'shard')
- key_grad: float32 [1024, 512], P('ctx', 'shard')
- value_grad: float32 [1024, 512], P('ctx', 'shard')
- output_grad: float32 [1024, 1024], P('shard', 'ctx')
- gate_grad: float32 [1024, 4608], P('ctx', 'shard')
- up_grad: float32 [1024, 4608], P('ctx', 'shard')
- down_grad: float32 [4608, 1024], P('shard', 'ctx')
The draws below stay inside these ranges and needn't reach their ends.
Inputs may be any that keep to these rules, and one draw needn't show every extreme that they name: Row d of block_pairs is (p, 63 - p); the first column holds every number below 32 once.
All inputs are finite; a program needn't handle non-finite values.
Results may differ from the reference program's by a relative error of at most 0.033.
Values may be sent and summed in bfloat16 or wider, within the bound.
No kernel may reach another device: no remote copies, remote signals or barrier semaphores. Data moves between devices by JAX's collectives and lax.ppermute only.
A program may use at most 128 MiB of HBM per device.

```python
import math
import jax
import jax.numpy as jnp
from jax import lax

D = 1024
HEADS = 16
KV_HEADS = 8
HD = 64
FF = 4608
SEQS = 2
BLK = 64
SEQ = 4096
N_CTX = 32


def draw_block_pairs(key, part):
    order = jax.random.permutation(key, N_CTX).astype(jnp.int32)
    return jnp.stack([order, 2 * N_CTX - 1 - order], axis=1)


def block_scale(key, extent, pieces, least, top_value):
    factor_of = 1.0
    for axis_at, blocks in pieces:
        steps = jax.random.uniform(jax.random.fold_in(jax.random.fold_in(key, 6), axis_at), (blocks,), jnp.float32, least / len(pieces), top_value / len(pieces))
        factor_of = factor_of * jnp.repeat(jnp.exp(steps), extent[axis_at] // blocks).reshape((-1,) + (1,) * (len(extent) - 1 - axis_at))
    return factor_of


def noise(rng, extent, width, reach, shards=(), kind=jnp.bfloat16):
    drawn = jax.random.normal(rng, extent, jnp.float32) * width
    if len(shards) > 0:
        drawn = block_scale(rng, extent, shards, -0.22, 0.18) * drawn
    return jnp.clip(drawn, min=-reach, max=reach).astype(kind)


def setup_inputs(seed: int = 0) -> dict:
    streams_of = jax.random.split(jax.random.key(seed), 15)
    block_in = noise(streams_of[0], (SEQS, SEQ, D), 1.0, 6.0, ((1, 32), (2, 4)))
    block_pairs = draw_block_pairs(jax.random.fold_in(streams_of[14], 71), 0)
    attn_gain = jnp.clip(1.0 + 0.18 * jax.random.normal(streams_of[2], (D,), jnp.float32), 0.1, 1.9)
    query_gain = jnp.clip(1.0 + 0.18 * jax.random.normal(streams_of[3], (HD,), jnp.float32), 0.1, 1.9)
    key_gain = jnp.clip(1.0 + 0.18 * jax.random.normal(streams_of[4], (HD,), jnp.float32), 0.1, 1.9)
    ffn_gain = jnp.clip(1.0 + 0.18 * jax.random.normal(streams_of[5], (D,), jnp.float32), 0.1, 1.9)
    w_query = noise(streams_of[6], (D, HEADS * HD), D ** -0.5, 0.1875, ((0, 32), (1, 4)))
    w_key = noise(streams_of[7], (D, KV_HEADS * HD), D ** -0.5, 0.1875, ((0, 32), (1, 4)))
    w_value = noise(streams_of[8], (D, KV_HEADS * HD), D ** -0.5, 0.1875, ((0, 32), (1, 4)))
    w_output = noise(streams_of[9], (HEADS * HD, D), 16 ** -0.5, 1.5, ((0, 4), (1, 32)))
    w_gate = noise(streams_of[10], (D, FF), D ** -0.5, 0.1875, ((0, 32), (1, 4)))
    w_up = noise(streams_of[11], (D, FF), D ** -0.5, 0.1875, ((0, 32), (1, 4)))
    w_down = noise(streams_of[12], (FF, D), FF ** -0.5, 0.09375, ((0, 4), (1, 32)))
    grad_output = noise(streams_of[13], (SEQS, SEQ, D), 1.0, 6.0, ((1, 32), (2, 4)))
    return dict(block_in=block_in, block_pairs=block_pairs, attn_gain=attn_gain, query_gain=query_gain, key_gain=key_gain, ffn_gain=ffn_gain, w_query=w_query, w_key=w_key, w_value=w_value, w_output=w_output, w_gate=w_gate, w_up=w_up, w_down=w_down, grad_output=grad_output)


EPSILON = 1e-05
ROPE_BASE = 1000000.0

def wide_dot(left, right):
    return jnp.dot(left, right, preferred_element_type=jnp.float32)

def rounded(values):
    return lax.optimization_barrier(values.astype(jnp.bfloat16))

def token_positions(block_pairs):
    row_index = jnp.arange(SEQ, dtype=jnp.int32)
    owner = row_index // (2 * BLK)
    half = row_index // BLK % 2
    return (block_pairs[owner, half] * BLK + row_index % BLK).astype(jnp.int32)

def rope_tables(positions):
    index = jnp.arange(HD // 2, dtype=jnp.float32)
    inverse = jnp.exp(index * (-2.0 * math.log(ROPE_BASE) / HD))
    angle = positions.astype(jnp.float32)[:, None] * inverse[None, :]
    cosine = jnp.cos(angle)
    sine = jnp.sin(angle)
    return (jnp.concatenate([cosine, cosine], 1)[:, None, :], jnp.concatenate([sine, sine], 1)[:, None, :])

def rotate_half(values):
    middle = values.shape[-1] // 2
    return jnp.concatenate([-values[..., middle:], values[..., :middle]], -1)

def rms_parts(values):
    scale = lax.rsqrt(lax.optimization_barrier(jnp.mean(values * values, axis=-1, keepdims=True)) + EPSILON)
    return (scale, values * scale)

def norm_back(grad_normed, unit, scale, gain):
    scaled = grad_normed * gain
    inner = lax.optimization_barrier(jnp.mean(scaled * unit, axis=-1, keepdims=True))
    return scale * (scaled - unit * inner)

def reference(block_in, block_pairs, attn_gain, query_gain, key_gain, ffn_gain, w_query, w_key, w_value, w_output, w_gate, w_up, w_down, grad_output):
    group = HEADS // KV_HEADS
    qblock = min(SEQ, 512)
    blocks = SEQ // qblock
    total_rows = SEQS * SEQ
    factor = 1.0 / math.sqrt(HD)
    positions = token_positions(block_pairs)
    cosine_one, sine_one = rope_tables(positions)
    cosine = jnp.tile(cosine_one, (SEQS, 1, 1))
    sine = jnp.tile(sine_one, (SEQS, 1, 1))
    input_wide = block_in.reshape(total_rows, D).astype(jnp.float32)
    grad_flat = grad_output.reshape(total_rows, D)
    scale_attn, unit_attn = rms_parts(input_wide)
    normed_attn = (unit_attn * attn_gain).astype(jnp.bfloat16)
    query = wide_dot(normed_attn, w_query).reshape(total_rows, HEADS, HD)
    key_raw = wide_dot(normed_attn, w_key).reshape(total_rows, KV_HEADS, HD)
    value = rounded(wide_dot(normed_attn, w_value)).reshape(total_rows, KV_HEADS, HD)
    query_scale, query_unit = rms_parts(query)
    key_scale, key_unit = rms_parts(key_raw)
    query_norm = query_unit * query_gain
    key_norm = key_unit * key_gain
    query_rot = rounded(query_norm * cosine + rotate_half(query_norm) * sine)
    key_rot = rounded(key_norm * cosine + rotate_half(key_norm) * sine)
    query_blocks = query_rot.astype(jnp.float32).reshape(SEQS * blocks, qblock, KV_HEADS, group, HD)
    pos_blocks = jnp.tile(positions, SEQS).reshape(SEQS * blocks, qblock)
    seq_ids = (jnp.arange(SEQS * blocks, dtype=jnp.int32) // blocks).astype(jnp.int32)
    key_wide = key_rot.astype(jnp.float32).reshape(SEQS, SEQ, KV_HEADS, HD)
    value_wide = value.astype(jnp.float32).reshape(SEQS, SEQ, KV_HEADS, HD)

    def scores_of(query_block, pos_block, seq_id):
        keys = key_wide[seq_id]
        score = jnp.einsum('qkgd,skd->kgqs', query_block, keys) * factor
        mask = positions[None, None, None, :] <= pos_block[None, None, :, None]
        return (score, mask, keys)

    def forward_block(inputs):
        query_block, pos_block, seq_id = inputs
        score, mask, keys = scores_of(query_block, pos_block, seq_id)
        weights = jnp.where(mask, jnp.exp(score), 0.0)
        total = lax.optimization_barrier(jnp.sum(weights, axis=-1))
        summed = jnp.einsum('kgqs,skd->qkgd', rounded(weights).astype(jnp.float32), value_wide[seq_id])
        out = summed / jnp.transpose(total, (2, 0, 1))[..., None]
        return (rounded(out), jnp.log(total))
    attn_heads, log_total = lax.map(forward_block, (query_blocks, pos_blocks, seq_ids))
    attn_out = attn_heads.reshape(total_rows, HEADS * HD)
    middle = input_wide + wide_dot(attn_out, w_output)
    scale_ffn, unit_ffn = rms_parts(middle)
    normed_ffn = (unit_ffn * ffn_gain).astype(jnp.bfloat16)
    gate = wide_dot(normed_ffn, w_gate)
    up_proj = wide_dot(normed_ffn, w_up)
    sigmoid_gate = jax.nn.sigmoid(gate)
    activated = gate * sigmoid_gate
    mixed = (activated * up_proj).astype(jnp.bfloat16)
    block_out = (middle + wide_dot(mixed, w_down)).astype(jnp.bfloat16)
    grad_mixed = wide_dot(grad_flat, w_down.T)
    down_grad = wide_dot(mixed.T, grad_flat)
    grad_gate = (grad_mixed * up_proj * sigmoid_gate * (1.0 + gate * (1.0 - sigmoid_gate))).astype(jnp.bfloat16)
    grad_up = (grad_mixed * activated).astype(jnp.bfloat16)
    gate_grad = wide_dot(normed_ffn.T, grad_gate)
    up_grad = wide_dot(normed_ffn.T, grad_up)
    grad_normed_ffn = wide_dot(grad_gate, w_gate.T) + wide_dot(grad_up, w_up.T)
    ffn_gain_grad = lax.optimization_barrier(jnp.sum(grad_normed_ffn * unit_ffn, axis=0))
    grad_middle = grad_flat.astype(jnp.float32) + norm_back(grad_normed_ffn, unit_ffn, scale_ffn, ffn_gain)
    grad_middle_low = grad_middle.astype(jnp.bfloat16)
    grad_attn = wide_dot(grad_middle_low, w_output.T).reshape(SEQS * blocks, qblock, KV_HEADS, group, HD)
    output_grad = wide_dot(attn_out.T, grad_middle_low)
    delta = lax.optimization_barrier(jnp.sum(grad_attn * attn_heads.astype(jnp.float32), axis=-1))
    grad_attn_low = rounded(grad_attn)

    def backward_block(carry, inputs):
        key_sum, value_sum = carry
        query_block, pos_block, seq_id, log_block, grad_block, delta_block = inputs
        score, mask, keys = scores_of(query_block, pos_block, seq_id)
        prob = jnp.where(mask, jnp.exp(score - log_block[..., None]), 0.0)
        grad_wide = grad_block.astype(jnp.float32)
        grad_prob = jnp.einsum('qkgd,skd->kgqs', grad_wide, value_wide[seq_id])
        grad_score = rounded(prob * (grad_prob - jnp.transpose(delta_block, (1, 2, 0))[..., None]) * factor).astype(jnp.float32)
        grad_query_block = jnp.einsum('kgqs,skd->qkgd', grad_score, keys)
        key_sum = key_sum.at[seq_id].add(jnp.einsum('kgqs,qkgd->skd', grad_score, query_block))
        value_sum = value_sum.at[seq_id].add(jnp.einsum('kgqs,qkgd->skd', rounded(prob).astype(jnp.float32), grad_wide))
        return ((key_sum, value_sum), grad_query_block)
    start_sums = (jnp.zeros((SEQS, SEQ, KV_HEADS, HD), jnp.float32), jnp.zeros((SEQS, SEQ, KV_HEADS, HD), jnp.float32))
    (grad_key_rot, grad_value), grad_query_rot = lax.scan(backward_block, start_sums, (query_blocks, pos_blocks, seq_ids, log_total, grad_attn_low, delta))
    grad_key_rot = grad_key_rot.reshape(total_rows, KV_HEADS, HD)
    grad_value = grad_value.reshape(total_rows, KV_HEADS, HD)
    grad_query_rot = grad_query_rot.reshape(total_rows, HEADS, HD)
    grad_query_unit = grad_query_rot * cosine - rotate_half(grad_query_rot * sine)
    grad_key_unit = grad_key_rot * cosine - rotate_half(grad_key_rot * sine)
    query_gain_grad = lax.optimization_barrier(jnp.sum(grad_query_unit * query_unit, axis=(0, 1)))
    key_gain_grad = lax.optimization_barrier(jnp.sum(grad_key_unit * key_unit, axis=(0, 1)))
    grad_query = norm_back(grad_query_unit, query_unit, query_scale, query_gain).astype(jnp.bfloat16).reshape(total_rows, HEADS * HD)
    grad_key = norm_back(grad_key_unit, key_unit, key_scale, key_gain).astype(jnp.bfloat16).reshape(total_rows, KV_HEADS * HD)
    grad_value_low = grad_value.astype(jnp.bfloat16).reshape(total_rows, KV_HEADS * HD)
    query_grad = wide_dot(normed_attn.T, grad_query)
    key_grad = wide_dot(normed_attn.T, grad_key)
    value_grad = wide_dot(normed_attn.T, grad_value_low)
    grad_normed_attn = wide_dot(grad_query, w_query.T) + wide_dot(grad_key, w_key.T) + wide_dot(grad_value_low, w_value.T)
    attn_gain_grad = lax.optimization_barrier(jnp.sum(grad_normed_attn * unit_attn, axis=0))
    input_grad = grad_middle + norm_back(grad_normed_attn, unit_attn, scale_attn, attn_gain)
    block_out = block_out.reshape(SEQS, SEQ, D)
    input_grad = input_grad.reshape(SEQS, SEQ, D)
    return (block_out, input_grad, attn_gain_grad, query_gain_grad, key_gain_grad, ffn_gain_grad, query_grad, key_grad, value_grad, output_grad, gate_grad, up_grad, down_grad)
```

```python
import math

import jax
import jax.numpy as jnp
from jax import lax
from jax.sharding import Mesh, PartitionSpec as P

HD = 64
BLK = 64


EPSILON = 1e-05
ROPE_BASE = 1000000.0


def wide_dot(left, right):
    return jnp.dot(left, right, preferred_element_type=jnp.float32)


def token_positions(block_pairs, row_index):
    owner = row_index // (2 * BLK)
    half = row_index // BLK % 2
    devices = jnp.arange(block_pairs.shape[0], dtype=jnp.int32)
    chosen = jnp.where(half[:, None] == 0, block_pairs[None, :, 0], block_pairs[None, :, 1])
    number = jnp.sum(jnp.where(owner[:, None] == devices[None, :], chosen, 0), axis=1)
    return number * BLK + row_index % BLK


def rope_tables(positions):
    index = jnp.arange(HD // 2, dtype=jnp.float32)
    inverse = jnp.exp(index * (-2.0 * math.log(ROPE_BASE) / HD))
    angle = positions.astype(jnp.float32)[:, None] * inverse[None, :]
    cosine = jnp.cos(angle)
    sine = jnp.sin(angle)
    return (
        jnp.concatenate([cosine, cosine], 1)[:, None, :],
        jnp.concatenate([sine, sine], 1)[:, None, :],
    )


def rotate_half(values):
    middle = values.shape[-1] // 2
    return jnp.concatenate([-values[..., middle:], values[..., :middle]], -1)


def head_norm(values):
    scale = lax.rsqrt(jnp.mean(values * values, axis=-1, keepdims=True) + EPSILON)
    return (scale, values * scale)


def head_back(grad_normed, unit, scale, gain):
    scaled = grad_normed * gain
    inner = jnp.mean(scaled * unit, axis=-1, keepdims=True)
    return scale * (scaled - unit * inner)


CTX_AXES = ("cx", "cy", "cz")
SHARD = ("sx", "sc")
EVERY = CTX_AXES + SHARD


def ctx_gather(local, axis):
    for name in reversed(CTX_AXES):
        local = lax.all_gather(local, name, axis=axis, tiled=True)
    return local


def ctx_scatter(partial_value, axis):
    for name in CTX_AXES:
        partial_value = lax.psum_scatter(partial_value, name, scatter_dimension=axis, tiled=True)
    return partial_value


def rows_total(partial_value):
    return lax.psum(partial_value, SHARD)


def full_rows(local):
    return lax.all_gather(local, SHARD, axis=1, tiled=True)


def share_rows(partial_value):
    return lax.psum_scatter(
        partial_value.astype(jnp.bfloat16), SHARD, scatter_dimension=1, tiled=True
    ).astype(jnp.float32)


def row_norm(values, width):
    total = rows_total(jnp.sum(values * values, axis=1))
    scale = lax.rsqrt(total / width + EPSILON)[:, None]
    return (scale, values * scale)


def norm_back(grad_normed, unit, scale, gain, width):
    scaled = grad_normed * gain
    inner = rows_total(jnp.sum(scaled * unit, axis=1)) / width
    return (scale * (scaled - unit * inner[:, None]), jnp.sum(grad_normed * unit, axis=0))


def over_blocks(step_fn, carry, arrays):
    whole = arrays[0].shape[1]
    step = min(whole, 1024)

    def turn(index, state):
        start = index * step
        pieces = tuple((lax.dynamic_slice_in_dim(array, start, step, 1) for array in arrays))
        return step_fn(state, pieces, start)

    return lax.fori_loop(0, whole // step, turn, carry)


def per_device(
    block_in,
    block_pairs,
    attn_gain,
    query_gain,
    key_gain,
    ffn_gain,
    w_query,
    w_key,
    w_value,
    w_output,
    w_gate,
    w_up,
    w_down,
    grad_output,
):
    seqs, rows, local_width = block_in.shape
    flat = seqs * rows
    width = local_width * lax.axis_size(SHARD)
    offset = lax.axis_index(SHARD) * local_width
    pieces = (w_query, w_key, w_value, w_gate, w_up, w_output.T, w_down.T)
    widths = [piece.shape[1] for piece in pieces]
    cuts = [sum(widths[:i]) for i in range(len(widths) + 1)]
    every_weight = ctx_gather(jnp.concatenate(pieces, axis=1), 0)
    gathered = [every_weight[:, cuts[i] : cuts[i + 1]] for i in range(len(pieces))]
    query_all, key_all_w, value_all_w, gate_all, up_all, output_all, down_all = gathered
    output_all = output_all.T
    down_all = down_all.T
    heads = query_all.shape[1] // HD
    kv_heads = key_all_w.shape[1] // HD
    group = heads // kv_heads
    factor = 1.0 / math.sqrt(HD)
    pos_query = token_positions(
        block_pairs, lax.axis_index(CTX_AXES) * rows + jnp.arange(rows, dtype=jnp.int32)
    )
    cosine_one, sine_one = rope_tables(pos_query)
    cosine = jnp.tile(cosine_one, (seqs, 1, 1))
    sine = jnp.tile(sine_one, (seqs, 1, 1))
    attn_slice = lax.dynamic_slice_in_dim(attn_gain, offset, local_width)
    ffn_slice = lax.dynamic_slice_in_dim(ffn_gain, offset, local_width)
    input_wide = block_in.reshape(flat, local_width).astype(jnp.float32)
    scale_attn, unit_attn = row_norm(input_wide, width)
    normed_attn = full_rows((unit_attn * attn_slice).astype(jnp.bfloat16))
    query_raw = wide_dot(normed_attn, query_all).reshape(flat, heads, HD)
    key_raw = wide_dot(normed_attn, key_all_w).reshape(flat, kv_heads, HD)
    value_rows = (
        wide_dot(normed_attn, value_all_w).astype(jnp.bfloat16).reshape(seqs, rows, kv_heads * HD)
    )
    query_scale, query_unit = head_norm(query_raw)
    key_scale, key_unit = head_norm(key_raw)
    query_norm = query_unit * query_gain
    key_norm = key_unit * key_gain
    query_rot = (
        (query_norm * cosine + rotate_half(query_norm) * sine)
        .astype(jnp.bfloat16)
        .reshape(seqs, rows, kv_heads, group, HD)
    )
    key_rot = (
        (key_norm * cosine + rotate_half(key_norm) * sine)
        .astype(jnp.bfloat16)
        .reshape(seqs, rows, kv_heads * HD)
    )

    def scores_at(key_piece, start):
        count = key_piece.shape[1]
        pos_key = token_positions(block_pairs, start + jnp.arange(count, dtype=jnp.int32))
        keys = key_piece.reshape(seqs, count, kv_heads, HD)
        score = (
            jnp.einsum("bqkgd,bskd->bkgqs", query_rot, keys, preferred_element_type=jnp.float32)
            * factor
        )
        mask = pos_key[None, None, None, None, :] <= pos_query[None, None, None, :, None]
        return (score, mask, keys)

    def attend(carry, pieces, start):
        key_piece, value_piece = pieces
        count = key_piece.shape[1]
        score, mask, keys = scores_at(key_piece, start)
        weights = jnp.where(mask, jnp.exp(score), 0.0)
        total, summed = carry
        values = value_piece.reshape(seqs, count, kv_heads, HD)
        summed = summed + jnp.einsum(
            "bkgqs,bskd->bqkgd",
            weights.astype(jnp.bfloat16),
            values,
            preferred_element_type=jnp.float32,
        )
        return (total + jnp.sum(weights, axis=-1), summed)

    start_carry = (
        jnp.zeros((seqs, kv_heads, group, rows), jnp.float32),
        jnp.zeros((seqs, rows, kv_heads, group, HD), jnp.float32),
    )
    key_value = ctx_gather(jnp.concatenate([key_rot, value_rows], axis=2), 1)
    key_every = key_value[:, :, : kv_heads * HD]
    value_every = key_value[:, :, kv_heads * HD :]
    total, summed = over_blocks(attend, start_carry, (key_every, value_every))
    log_total = jnp.log(total)
    attn_heads = (summed / jnp.transpose(total, (0, 3, 1, 2))[..., None]).astype(jnp.bfloat16)
    attn_out = attn_heads.reshape(flat, heads * HD)
    middle = input_wide + share_rows(wide_dot(attn_out, output_all))
    scale_ffn, unit_ffn = row_norm(middle, width)
    normed_ffn = full_rows((unit_ffn * ffn_slice).astype(jnp.bfloat16))
    gate = wide_dot(normed_ffn, gate_all)
    up_proj = wide_dot(normed_ffn, up_all)
    sigmoid_gate = jax.nn.sigmoid(gate)
    activated = gate * sigmoid_gate
    mixed = (activated * up_proj).astype(jnp.bfloat16)
    block_out = (middle + share_rows(wide_dot(mixed, down_all))).astype(jnp.bfloat16)
    grad_flat = grad_output.reshape(flat, local_width)
    grad_full = full_rows(grad_flat)
    grad_mixed = wide_dot(grad_full, down_all.T)
    down_grad = wide_dot(mixed.T, grad_full)
    grad_gate = (grad_mixed * up_proj * sigmoid_gate * (1.0 + gate * (1.0 - sigmoid_gate))).astype(
        jnp.bfloat16
    )
    grad_up = (grad_mixed * activated).astype(jnp.bfloat16)
    gate_grad = wide_dot(normed_ffn.T, grad_gate)
    up_grad = wide_dot(normed_ffn.T, grad_up)
    grad_normed_ffn = share_rows(wide_dot(grad_gate, gate_all.T) + wide_dot(grad_up, up_all.T))
    back_ffn, ffn_part = norm_back(grad_normed_ffn, unit_ffn, scale_ffn, ffn_slice, width)
    grad_middle = grad_flat.astype(jnp.float32) + back_ffn
    grad_middle_all = full_rows(grad_middle.astype(jnp.bfloat16))
    grad_attn = wide_dot(grad_middle_all, output_all.T).reshape(seqs, rows, kv_heads, group, HD)
    output_grad = wide_dot(attn_out.T, grad_middle_all)
    delta = jnp.transpose(
        jnp.sum(grad_attn * attn_heads.astype(jnp.float32), axis=-1), (0, 2, 3, 1)
    )
    grad_attn_low = grad_attn.astype(jnp.bfloat16)

    def revisit(grad_query_sum, pieces, start):
        key_piece, value_piece = pieces
        count = key_piece.shape[1]
        score, mask, keys = scores_at(key_piece, start)
        values = value_piece.reshape(seqs, count, kv_heads, HD)
        prob = jnp.where(mask, jnp.exp(score - log_total[..., None]), 0.0)
        grad_prob = jnp.einsum(
            "bqkgd,bskd->bkgqs", grad_attn_low, values, preferred_element_type=jnp.float32
        )
        grad_score = (prob * (grad_prob - delta[..., None]) * factor).astype(jnp.bfloat16)
        grad_query_sum = grad_query_sum + jnp.einsum(
            "bkgqs,bskd->bqkgd", grad_score, keys, preferred_element_type=jnp.float32
        )
        key_term = jnp.einsum(
            "bkgqs,bqkgd->bskd", grad_score, query_rot, preferred_element_type=jnp.float32
        )
        value_term = jnp.einsum(
            "bkgqs,bqkgd->bskd",
            prob.astype(jnp.bfloat16),
            grad_attn_low,
            preferred_element_type=jnp.float32,
        )
        return (
            grad_query_sum,
            jnp.concatenate(
                [
                    key_term.reshape(seqs, count, kv_heads * HD),
                    value_term.reshape(seqs, count, kv_heads * HD),
                ],
                2,
            ),
        )

    whole = key_every.shape[1]
    step = min(whole, 1024)

    def back_turn(grad_query_sum, index):
        start = index * step
        pieces = (
            lax.dynamic_slice_in_dim(key_every, start, step, 1),
            lax.dynamic_slice_in_dim(value_every, start, step, 1),
        )
        return revisit(grad_query_sum, pieces, start)

    grad_query_rot, key_terms = lax.scan(
        back_turn,
        jnp.zeros((seqs, rows, kv_heads, group, HD), jnp.float32),
        jnp.arange(whole // step, dtype=jnp.int32),
    )
    key_terms = jnp.transpose(key_terms, (1, 0, 2, 3)).reshape(seqs, whole, 2 * kv_heads * HD)
    owned = (
        ctx_scatter(key_terms.astype(jnp.bfloat16), 1)
        .astype(jnp.float32)
        .reshape(flat, 2 * kv_heads * HD)
    )
    grad_key_rot = owned[:, : kv_heads * HD].reshape(flat, kv_heads, HD)
    grad_value_low = owned[:, kv_heads * HD :].astype(jnp.bfloat16)
    grad_query_rot = grad_query_rot.reshape(flat, heads, HD)
    grad_query_unit = grad_query_rot * cosine - rotate_half(grad_query_rot * sine)
    grad_key_unit = grad_key_rot * cosine - rotate_half(grad_key_rot * sine)
    query_gain_part = jnp.sum(grad_query_unit * query_unit, axis=(0, 1))
    key_gain_part = jnp.sum(grad_key_unit * key_unit, axis=(0, 1))
    grad_query = (
        head_back(grad_query_unit, query_unit, query_scale, query_gain)
        .astype(jnp.bfloat16)
        .reshape(flat, heads * HD)
    )
    grad_key = (
        head_back(grad_key_unit, key_unit, key_scale, key_gain)
        .astype(jnp.bfloat16)
        .reshape(flat, kv_heads * HD)
    )
    query_grad = wide_dot(normed_attn.T, grad_query)
    key_grad = wide_dot(normed_attn.T, grad_key)
    value_grad = wide_dot(normed_attn.T, grad_value_low)
    grad_normed_attn = share_rows(
        wide_dot(grad_query, query_all.T)
        + wide_dot(grad_key, key_all_w.T)
        + wide_dot(grad_value_low, value_all_w.T)
    )
    back_attn, attn_part = norm_back(grad_normed_attn, unit_attn, scale_attn, attn_slice, width)
    input_grad = grad_middle + back_attn
    grad_pieces = (query_grad, key_grad, value_grad, gate_grad, up_grad, output_grad.T, down_grad.T)
    summed = ctx_scatter(jnp.concatenate(grad_pieces, axis=1).astype(jnp.bfloat16), 0)
    summed = summed.astype(jnp.float32)
    summed_grads = [summed[:, cuts[i] : cuts[i + 1]] for i in range(len(grad_pieces))]
    query_grad, key_grad, value_grad, gate_grad, up_grad, output_grad, down_grad = summed_grads
    output_grad = output_grad.T
    down_grad = down_grad.T
    attn_placed = lax.dynamic_update_slice_in_dim(
        jnp.zeros((width,), jnp.float32), attn_part, offset, 0
    )
    ffn_placed = lax.dynamic_update_slice_in_dim(
        jnp.zeros((width,), jnp.float32), ffn_part, offset, 0
    )
    attn_gain_grad, query_gain_grad, key_gain_grad, ffn_gain_grad = lax.psum(
        (attn_placed, query_gain_part, key_gain_part, ffn_placed), EVERY
    )
    block_out = block_out.reshape(seqs, rows, local_width)
    input_grad = input_grad.reshape(seqs, rows, local_width)
    return (
        block_out,
        input_grad,
        attn_gain_grad,
        query_gain_grad,
        key_gain_grad,
        ffn_gain_grad,
        query_grad,
        key_grad,
        value_grad,
        output_grad,
        gate_grad,
        up_grad,
        down_grad,
    )


def solution(mesh):
    ctx_size, shard_size = mesh.devices.shape
    fine = Mesh(mesh.devices.reshape(2, 4, ctx_size // 8, 2, shard_size // 2), EVERY)
    ctx = CTX_AXES
    in_specs = (
        P(None, ctx, SHARD),
        P(),
        P(),
        P(),
        P(),
        P(),
        P(ctx, SHARD),
        P(ctx, SHARD),
        P(ctx, SHARD),
        P(SHARD, ctx),
        P(ctx, SHARD),
        P(ctx, SHARD),
        P(SHARD, ctx),
        P(None, ctx, SHARD),
    )
    out_specs = (
        P(None, ctx, SHARD),
        P(None, ctx, SHARD),
        P(),
        P(),
        P(),
        P(),
        P(ctx, SHARD),
        P(ctx, SHARD),
        P(ctx, SHARD),
        P(SHARD, ctx),
        P(ctx, SHARD),
        P(ctx, SHARD),
        P(SHARD, ctx),
    )
    return jax.shard_map(
        per_device, mesh=fine, in_specs=in_specs, out_specs=out_specs, check_vma=False
    )
```

```python
import math

import jax
import jax.numpy as jnp
from jax import lax
from jax.sharding import Mesh, PartitionSpec as P

HD = 64
BLK = 64


EPSILON = 1e-05
ROPE_BASE = 1000000.0


def wide_dot(left, right):
    return jnp.dot(left, right, preferred_element_type=jnp.float32)


def token_positions(block_pairs, row_index):
    owner = row_index // (2 * BLK)
    half = row_index // BLK % 2
    devices = jnp.arange(block_pairs.shape[0], dtype=jnp.int32)
    chosen = jnp.where(half[:, None] == 0, block_pairs[None, :, 0], block_pairs[None, :, 1])
    number = jnp.sum(jnp.where(owner[:, None] == devices[None, :], chosen, 0), axis=1)
    return number * BLK + row_index % BLK


def rope_tables(positions):
    index = jnp.arange(HD // 2, dtype=jnp.float32)
    inverse = jnp.exp(index * (-2.0 * math.log(ROPE_BASE) / HD))
    angle = positions.astype(jnp.float32)[:, None] * inverse[None, :]
    cosine = jnp.cos(angle)
    sine = jnp.sin(angle)
    return (
        jnp.concatenate([cosine, cosine], 1)[:, None, :],
        jnp.concatenate([sine, sine], 1)[:, None, :],
    )


def rotate_half(values):
    middle = values.shape[-1] // 2
    return jnp.concatenate([-values[..., middle:], values[..., :middle]], -1)


def head_norm(values):
    scale = lax.rsqrt(jnp.mean(values * values, axis=-1, keepdims=True) + EPSILON)
    return (scale, values * scale)


def head_back(grad_normed, unit, scale, gain):
    scaled = grad_normed * gain
    inner = jnp.mean(scaled * unit, axis=-1, keepdims=True)
    return scale * (scaled - unit * inner)


CTX_AXES = ("cx", "cy", "cz")
SHARD = ("sx", "sc")
EVERY = CTX_AXES + SHARD


def ctx_gather(local, axis):
    for name in reversed(CTX_AXES):
        local = lax.all_gather(local, name, axis=axis, tiled=True)
    return local


def ctx_scatter(partial_value, axis):
    for name in CTX_AXES:
        partial_value = lax.psum_scatter(partial_value, name, scatter_dimension=axis, tiled=True)
    return partial_value


def rows_total(partial_value):
    return lax.psum(partial_value, SHARD)


def full_rows(local):
    return lax.all_gather(local, SHARD, axis=1, tiled=True)


def share_rows(partial_value):
    shards = lax.axis_size(SHARD)
    rows, cols = partial_value.shape
    blocks = partial_value.astype(jnp.bfloat16).reshape(rows, shards, cols // shards)
    blocks = lax.all_to_all(blocks, SHARD, 1, 1, tiled=True)
    return jnp.sum(blocks.astype(jnp.float32), axis=1)


def add_rows(partial_value):
    pieces = lax.all_gather(partial_value.astype(jnp.bfloat16), SHARD, axis=0)
    return jnp.sum(pieces.astype(jnp.float32), axis=0)


def local_norm(values):
    scale = lax.rsqrt(jnp.mean(values * values, axis=1, keepdims=True) + EPSILON)
    return (scale, values * scale)


def local_back(grad_normed, unit, scale, gain):
    scaled = grad_normed * gain
    inner = jnp.mean(scaled * unit, axis=1, keepdims=True)
    return scale * (scaled - unit * inner)


def row_norm(values, width):
    total = rows_total(jnp.sum(values * values, axis=1))
    scale = lax.rsqrt(total / width + EPSILON)[:, None]
    return (scale, values * scale)


def norm_back(grad_normed, unit, scale, gain, width):
    scaled = grad_normed * gain
    inner = rows_total(jnp.sum(scaled * unit, axis=1)) / width
    return (scale * (scaled - unit * inner[:, None]), jnp.sum(grad_normed * unit, axis=0))


def over_blocks(step_fn, carry, arrays):
    whole = arrays[0].shape[1]
    step = min(whole, 1024)

    def turn(index, state):
        start = index * step
        pieces = tuple((lax.dynamic_slice_in_dim(array, start, step, 1) for array in arrays))
        return step_fn(state, pieces, start)

    return lax.fori_loop(0, whole // step, turn, carry)


def per_device(
    block_in,
    block_pairs,
    attn_gain,
    query_gain,
    key_gain,
    ffn_gain,
    w_query,
    w_key,
    w_value,
    w_output,
    w_gate,
    w_up,
    w_down,
    grad_output,
):
    seqs, rows, local_width = block_in.shape
    flat = seqs * rows
    width = local_width * lax.axis_size(SHARD)
    offset = lax.axis_index(SHARD) * local_width
    pieces = (w_query, w_key, w_value, w_gate, w_up, w_output.T, w_down.T)
    widths = [piece.shape[1] for piece in pieces]
    cuts = [sum(widths[:i]) for i in range(len(widths) + 1)]
    every_weight = ctx_gather(jnp.concatenate(pieces, axis=1), 0)
    gathered = [every_weight[:, cuts[i] : cuts[i + 1]] for i in range(len(pieces))]
    query_all, key_all_w, value_all_w, gate_all, up_all, output_all, down_all = gathered
    output_all = output_all.T
    down_all = down_all.T
    heads = query_all.shape[1] // HD
    kv_heads = key_all_w.shape[1] // HD
    group = heads // kv_heads
    factor = 1.0 / math.sqrt(HD)
    pos_query = token_positions(
        block_pairs, lax.axis_index(CTX_AXES) * rows + jnp.arange(rows, dtype=jnp.int32)
    )
    cosine_one, sine_one = rope_tables(pos_query)
    cosine = jnp.tile(cosine_one, (seqs, 1, 1))
    sine = jnp.tile(sine_one, (seqs, 1, 1))
    attn_slice = lax.dynamic_slice_in_dim(attn_gain, offset, local_width)
    ffn_slice = lax.dynamic_slice_in_dim(ffn_gain, offset, local_width)
    input_all = full_rows(block_in.reshape(flat, local_width)).astype(jnp.float32)
    scale_attn, unit_attn = local_norm(input_all)
    normed_attn = (unit_attn * attn_gain).astype(jnp.bfloat16)
    query_raw = wide_dot(normed_attn, query_all).reshape(flat, heads, HD)
    key_raw = wide_dot(normed_attn, key_all_w).reshape(flat, kv_heads, HD)
    value_rows = (
        wide_dot(normed_attn, value_all_w).astype(jnp.bfloat16).reshape(seqs, rows, kv_heads * HD)
    )
    query_scale, query_unit = head_norm(query_raw)
    key_scale, key_unit = head_norm(key_raw)
    query_norm = query_unit * query_gain
    key_norm = key_unit * key_gain
    query_rot = (
        (query_norm * cosine + rotate_half(query_norm) * sine)
        .astype(jnp.bfloat16)
        .reshape(seqs, rows, kv_heads, group, HD)
    )
    key_rot = (
        (key_norm * cosine + rotate_half(key_norm) * sine)
        .astype(jnp.bfloat16)
        .reshape(seqs, rows, kv_heads * HD)
    )

    def scores_at(key_piece, start):
        count = key_piece.shape[1]
        pos_key = token_positions(block_pairs, start + jnp.arange(count, dtype=jnp.int32))
        keys = key_piece.reshape(seqs, count, kv_heads, HD)
        score = (
            jnp.einsum("bqkgd,bskd->bkgqs", query_rot, keys, preferred_element_type=jnp.float32)
            * factor
        )
        mask = pos_key[None, None, None, None, :] <= pos_query[None, None, None, :, None]
        return (score, mask, keys)

    def attend(carry, pieces, start):
        key_piece, value_piece = pieces
        count = key_piece.shape[1]
        score, mask, keys = scores_at(key_piece, start)
        weights = jnp.where(mask, jnp.exp(score), 0.0)
        total, summed = carry
        values = value_piece.reshape(seqs, count, kv_heads, HD)
        summed = summed + jnp.einsum(
            "bkgqs,bskd->bqkgd",
            weights.astype(jnp.bfloat16),
            values,
            preferred_element_type=jnp.float32,
        )
        return (total + jnp.sum(weights, axis=-1), summed)

    start_carry = (
        jnp.zeros((seqs, kv_heads, group, rows), jnp.float32),
        jnp.zeros((seqs, rows, kv_heads, group, HD), jnp.float32),
    )
    key_value = ctx_gather(jnp.concatenate([key_rot, value_rows], axis=2), 1)
    key_every = key_value[:, :, : kv_heads * HD]
    value_every = key_value[:, :, kv_heads * HD :]
    total, summed = over_blocks(attend, start_carry, (key_every, value_every))
    log_total = jnp.log(total)
    attn_heads = (summed / jnp.transpose(total, (0, 3, 1, 2))[..., None]).astype(jnp.bfloat16)
    attn_out = attn_heads.reshape(flat, heads * HD)
    middle_all = input_all + add_rows(wide_dot(attn_out, output_all))
    middle = lax.dynamic_slice_in_dim(middle_all, offset, local_width, 1)
    scale_ffn, unit_ffn = local_norm(middle_all)
    normed_ffn = (unit_ffn * ffn_gain).astype(jnp.bfloat16)
    gate = wide_dot(normed_ffn, gate_all)
    up_proj = wide_dot(normed_ffn, up_all)
    sigmoid_gate = jax.nn.sigmoid(gate)
    activated = gate * sigmoid_gate
    mixed = (activated * up_proj).astype(jnp.bfloat16)
    block_out = (middle + share_rows(wide_dot(mixed, down_all))).astype(jnp.bfloat16)
    grad_flat = grad_output.reshape(flat, local_width)
    grad_full = full_rows(grad_flat)
    grad_mixed = wide_dot(grad_full, down_all.T)
    down_grad = wide_dot(mixed.T, grad_full)
    grad_gate = (grad_mixed * up_proj * sigmoid_gate * (1.0 + gate * (1.0 - sigmoid_gate))).astype(
        jnp.bfloat16
    )
    grad_up = (grad_mixed * activated).astype(jnp.bfloat16)
    gate_grad = wide_dot(normed_ffn.T, grad_gate)
    up_grad = wide_dot(normed_ffn.T, grad_up)
    grad_normed_ffn = add_rows(wide_dot(grad_gate, gate_all.T) + wide_dot(grad_up, up_all.T))
    back_ffn = local_back(grad_normed_ffn, unit_ffn, scale_ffn, ffn_gain)
    ffn_part = lax.dynamic_slice_in_dim(jnp.sum(grad_normed_ffn * unit_ffn, axis=0), offset, local_width)
    grad_middle_full = grad_full.astype(jnp.float32) + back_ffn
    grad_middle_all = grad_middle_full.astype(jnp.bfloat16)
    grad_attn = wide_dot(grad_middle_all, output_all.T).reshape(seqs, rows, kv_heads, group, HD)
    output_grad = wide_dot(attn_out.T, grad_middle_all)
    delta = jnp.transpose(
        jnp.sum(grad_attn * attn_heads.astype(jnp.float32), axis=-1), (0, 2, 3, 1)
    )
    grad_attn_low = grad_attn.astype(jnp.bfloat16)

    def revisit(grad_query_sum, pieces, start):
        key_piece, value_piece = pieces
        count = key_piece.shape[1]
        score, mask, keys = scores_at(key_piece, start)
        values = value_piece.reshape(seqs, count, kv_heads, HD)
        prob = jnp.where(mask, jnp.exp(score - log_total[..., None]), 0.0)
        grad_prob = jnp.einsum(
            "bqkgd,bskd->bkgqs", grad_attn_low, values, preferred_element_type=jnp.float32
        )
        grad_score = (prob * (grad_prob - delta[..., None]) * factor).astype(jnp.bfloat16)
        grad_query_sum = grad_query_sum + jnp.einsum(
            "bkgqs,bskd->bqkgd", grad_score, keys, preferred_element_type=jnp.float32
        )
        key_term = jnp.einsum(
            "bkgqs,bqkgd->bskd", grad_score, query_rot, preferred_element_type=jnp.float32
        )
        value_term = jnp.einsum(
            "bkgqs,bqkgd->bskd",
            prob.astype(jnp.bfloat16),
            grad_attn_low,
            preferred_element_type=jnp.float32,
        )
        return (
            grad_query_sum,
            jnp.concatenate(
                [
                    key_term.reshape(seqs, count, kv_heads * HD),
                    value_term.reshape(seqs, count, kv_heads * HD),
                ],
                2,
            ),
        )

    whole = key_every.shape[1]
    step = min(whole, 1024)

    def back_turn(grad_query_sum, index):
        start = index * step
        pieces = (
            lax.dynamic_slice_in_dim(key_every, start, step, 1),
            lax.dynamic_slice_in_dim(value_every, start, step, 1),
        )
        return revisit(grad_query_sum, pieces, start)

    grad_query_rot, key_terms = lax.scan(
        back_turn,
        jnp.zeros((seqs, rows, kv_heads, group, HD), jnp.float32),
        jnp.arange(whole // step, dtype=jnp.int32),
    )
    key_terms = jnp.transpose(key_terms, (1, 0, 2, 3)).reshape(seqs, whole, 2 * kv_heads * HD)
    owned = (
        ctx_scatter(key_terms.astype(jnp.bfloat16), 1)
        .astype(jnp.float32)
        .reshape(flat, 2 * kv_heads * HD)
    )
    grad_key_rot = owned[:, : kv_heads * HD].reshape(flat, kv_heads, HD)
    grad_value_low = owned[:, kv_heads * HD :].astype(jnp.bfloat16)
    grad_query_rot = grad_query_rot.reshape(flat, heads, HD)
    grad_query_unit = grad_query_rot * cosine - rotate_half(grad_query_rot * sine)
    grad_key_unit = grad_key_rot * cosine - rotate_half(grad_key_rot * sine)
    query_gain_part = jnp.sum(grad_query_unit * query_unit, axis=(0, 1))
    key_gain_part = jnp.sum(grad_key_unit * key_unit, axis=(0, 1))
    grad_query = (
        head_back(grad_query_unit, query_unit, query_scale, query_gain)
        .astype(jnp.bfloat16)
        .reshape(flat, heads * HD)
    )
    grad_key = (
        head_back(grad_key_unit, key_unit, key_scale, key_gain)
        .astype(jnp.bfloat16)
        .reshape(flat, kv_heads * HD)
    )
    query_grad = wide_dot(normed_attn.T, grad_query)
    key_grad = wide_dot(normed_attn.T, grad_key)
    value_grad = wide_dot(normed_attn.T, grad_value_low)
    grad_normed_attn = add_rows(
        wide_dot(grad_query, query_all.T)
        + wide_dot(grad_key, key_all_w.T)
        + wide_dot(grad_value_low, value_all_w.T)
    )
    back_attn = local_back(grad_normed_attn, unit_attn, scale_attn, attn_gain)
    attn_part = lax.dynamic_slice_in_dim(jnp.sum(grad_normed_attn * unit_attn, axis=0), offset, local_width)
    input_grad = lax.dynamic_slice_in_dim(grad_middle_full + back_attn, offset, local_width, 1)
    grad_pieces = (query_grad, key_grad, value_grad, gate_grad, up_grad, output_grad.T, down_grad.T)
    summed = ctx_scatter(jnp.concatenate(grad_pieces, axis=1).astype(jnp.bfloat16), 0)
    summed = summed.astype(jnp.float32)
    summed_grads = [summed[:, cuts[i] : cuts[i + 1]] for i in range(len(grad_pieces))]
    query_grad, key_grad, value_grad, gate_grad, up_grad, output_grad, down_grad = summed_grads
    output_grad = output_grad.T
    down_grad = down_grad.T
    attn_placed = lax.dynamic_update_slice_in_dim(
        jnp.zeros((width,), jnp.float32), attn_part, offset, 0
    )
    ffn_placed = lax.dynamic_update_slice_in_dim(
        jnp.zeros((width,), jnp.float32), ffn_part, offset, 0
    )
    gains = (attn_placed, query_gain_part, key_gain_part, ffn_placed)
    for names in (SHARD,) + tuple(reversed(CTX_AXES)):
        gains = lax.psum(gains, names)
    attn_gain_grad, query_gain_grad, key_gain_grad, ffn_gain_grad = gains
    block_out = block_out.reshape(seqs, rows, local_width)
    input_grad = input_grad.reshape(seqs, rows, local_width)
    return (
        block_out,
        input_grad,
        attn_gain_grad,
        query_gain_grad,
        key_gain_grad,
        ffn_gain_grad,
        query_grad,
        key_grad,
        value_grad,
        output_grad,
        gate_grad,
        up_grad,
        down_grad,
    )


def solution(mesh):
    ctx_size, shard_size = mesh.devices.shape
    fine = Mesh(mesh.devices.reshape(2, 4, ctx_size // 8, 2, shard_size // 2), EVERY)
    ctx = CTX_AXES
    in_specs = (
        P(None, ctx, SHARD),
        P(),
        P(),
        P(),
        P(),
        P(),
        P(ctx, SHARD),
        P(ctx, SHARD),
        P(ctx, SHARD),
        P(SHARD, ctx),
        P(ctx, SHARD),
        P(ctx, SHARD),
        P(SHARD, ctx),
        P(None, ctx, SHARD),
    )
    out_specs = (
        P(None, ctx, SHARD),
        P(None, ctx, SHARD),
        P(),
        P(),
        P(),
        P(),
        P(ctx, SHARD),
        P(ctx, SHARD),
        P(ctx, SHARD),
        P(SHARD, ctx),
        P(ctx, SHARD),
        P(ctx, SHARD),
        P(SHARD, ctx),
    )
    return jax.shard_map(
        per_device, mesh=fine, in_specs=in_specs, out_specs=out_specs, check_vma=False
    )
```

```python
import math

import jax
import jax.numpy as jnp
from jax import lax
from jax.sharding import Mesh, PartitionSpec as P

HD = 64
BLK = 64


EPSILON = 1e-05
ROPE_BASE = 1000000.0


def wide_dot(left, right):
    return jnp.dot(left, right, preferred_element_type=jnp.float32)


def token_positions(block_pairs, row_index):
    owner = row_index // (2 * BLK)
    half = row_index // BLK % 2
    devices = jnp.arange(block_pairs.shape[0], dtype=jnp.int32)
    chosen = jnp.where(half[:, None] == 0, block_pairs[None, :, 0], block_pairs[None, :, 1])
    number = jnp.sum(jnp.where(owner[:, None] == devices[None, :], chosen, 0), axis=1)
    return number * BLK + row_index % BLK


def rope_tables(positions):
    index = jnp.arange(HD // 2, dtype=jnp.float32)
    inverse = jnp.exp(index * (-2.0 * math.log(ROPE_BASE) / HD))
    angle = positions.astype(jnp.float32)[:, None] * inverse[None, :]
    cosine = jnp.cos(angle)
    sine = jnp.sin(angle)
    return (
        jnp.concatenate([cosine, cosine], 1)[:, None, :],
        jnp.concatenate([sine, sine], 1)[:, None, :],
    )


def rotate_half(values):
    middle = values.shape[-1] // 2
    return jnp.concatenate([-values[..., middle:], values[..., :middle]], -1)


def head_norm(values):
    scale = lax.rsqrt(jnp.mean(values * values, axis=-1, keepdims=True) + EPSILON)
    return (scale, values * scale)


def head_back(grad_normed, unit, scale, gain):
    scaled = grad_normed * gain
    inner = jnp.mean(scaled * unit, axis=-1, keepdims=True)
    return scale * (scaled - unit * inner)


CTX_AXES = ("cx", "cy", "cz")
SHARD = ("sx", "sc")
EVERY = CTX_AXES + SHARD


def ctx_gather(local, axis):
    for name in CTX_AXES:
        local = lax.all_gather(local, name, axis=axis, tiled=True)
    return local


def ctx_scatter(partial_value, axis):
    for name in reversed(CTX_AXES):
        partial_value = lax.psum_scatter(partial_value, name, scatter_dimension=axis, tiled=True)
    return partial_value


def gathered_to_ctx(values, axis, sizes):
    shape = values.shape
    block = shape[axis] // (sizes[0] * sizes[1] * sizes[2])
    split = shape[:axis] + (sizes[2], sizes[1], sizes[0], block) + shape[axis + 1 :]
    order = list(range(len(split)))
    order[axis], order[axis + 2] = axis + 2, axis
    return jnp.transpose(values.reshape(split), order).reshape(shape)


def natural_row(index, rows, sizes):
    device = index // rows
    cx = device % sizes[0]
    cy = device // sizes[0] % sizes[1]
    cz = device // (sizes[0] * sizes[1])
    return ((cx * sizes[1] + cy) * sizes[2] + cz) * rows + index % rows


def rows_total(partial_value):
    return lax.psum(partial_value, SHARD)


def full_rows(local):
    return lax.all_gather(local, SHARD, axis=1, tiled=True)


def share_rows(partial_value):
    shards = lax.axis_size(SHARD)
    rows, cols = partial_value.shape
    blocks = partial_value.astype(jnp.bfloat16).reshape(rows, shards, cols // shards)
    blocks = lax.all_to_all(blocks, SHARD, 1, 1, tiled=True)
    return jnp.sum(blocks.astype(jnp.float32), axis=1)


def add_rows(partial_value):
    pieces = lax.all_gather(partial_value.astype(jnp.bfloat16), SHARD, axis=0)
    return jnp.sum(pieces.astype(jnp.float32), axis=0)


def local_norm(values):
    scale = lax.rsqrt(jnp.mean(values * values, axis=1, keepdims=True) + EPSILON)
    return (scale, values * scale)


def local_back(grad_normed, unit, scale, gain):
    scaled = grad_normed * gain
    inner = jnp.mean(scaled * unit, axis=1, keepdims=True)
    return scale * (scaled - unit * inner)


def row_norm(values, width):
    total = rows_total(jnp.sum(values * values, axis=1))
    scale = lax.rsqrt(total / width + EPSILON)[:, None]
    return (scale, values * scale)


def norm_back(grad_normed, unit, scale, gain, width):
    scaled = grad_normed * gain
    inner = rows_total(jnp.sum(scaled * unit, axis=1)) / width
    return (scale * (scaled - unit * inner[:, None]), jnp.sum(grad_normed * unit, axis=0))


def over_blocks(step_fn, carry, arrays):
    whole = arrays[0].shape[1]
    step = min(whole, 1024)

    def turn(index, state):
        start = index * step
        pieces = tuple((lax.dynamic_slice_in_dim(array, start, step, 1) for array in arrays))
        return step_fn(state, pieces, start)

    return lax.fori_loop(0, whole // step, turn, carry)


def per_device(
    block_in,
    block_pairs,
    attn_gain,
    query_gain,
    key_gain,
    ffn_gain,
    w_query,
    w_key,
    w_value,
    w_output,
    w_gate,
    w_up,
    w_down,
    grad_output,
):
    seqs, rows, local_width = block_in.shape
    flat = seqs * rows
    width = local_width * lax.axis_size(SHARD)
    offset = lax.axis_index(SHARD) * local_width
    pieces = (w_query, w_key, w_value, w_gate, w_up, w_output.T, w_down.T)
    widths = [piece.shape[1] for piece in pieces]
    cuts = [sum(widths[:i]) for i in range(len(widths) + 1)]
    ctx_sizes = tuple(lax.axis_size(name) for name in CTX_AXES)
    every_weight = ctx_gather(jnp.concatenate(pieces, axis=1), 0)
    every_weight = gathered_to_ctx(every_weight, 0, ctx_sizes)
    gathered = [every_weight[:, cuts[i] : cuts[i + 1]] for i in range(len(pieces))]
    query_all, key_all_w, value_all_w, gate_all, up_all, output_all, down_all = gathered
    output_all = output_all.T
    down_all = down_all.T
    heads = query_all.shape[1] // HD
    kv_heads = key_all_w.shape[1] // HD
    group = heads // kv_heads
    factor = 1.0 / math.sqrt(HD)
    pos_query = token_positions(
        block_pairs, lax.axis_index(CTX_AXES) * rows + jnp.arange(rows, dtype=jnp.int32)
    )
    cosine_one, sine_one = rope_tables(pos_query)
    cosine = jnp.tile(cosine_one, (seqs, 1, 1))
    sine = jnp.tile(sine_one, (seqs, 1, 1))
    attn_slice = lax.dynamic_slice_in_dim(attn_gain, offset, local_width)
    ffn_slice = lax.dynamic_slice_in_dim(ffn_gain, offset, local_width)
    input_all = full_rows(block_in.reshape(flat, local_width)).astype(jnp.float32)
    scale_attn, unit_attn = local_norm(input_all)
    normed_attn = (unit_attn * attn_gain).astype(jnp.bfloat16)
    query_raw = wide_dot(normed_attn, query_all).reshape(flat, heads, HD)
    key_raw = wide_dot(normed_attn, key_all_w).reshape(flat, kv_heads, HD)
    value_rows = (
        wide_dot(normed_attn, value_all_w).astype(jnp.bfloat16).reshape(seqs, rows, kv_heads * HD)
    )
    query_scale, query_unit = head_norm(query_raw)
    key_scale, key_unit = head_norm(key_raw)
    query_norm = query_unit * query_gain
    key_norm = key_unit * key_gain
    query_rot = (
        (query_norm * cosine + rotate_half(query_norm) * sine)
        .astype(jnp.bfloat16)
        .reshape(seqs, rows, kv_heads, group, HD)
    )
    key_rot = (
        (key_norm * cosine + rotate_half(key_norm) * sine)
        .astype(jnp.bfloat16)
        .reshape(seqs, rows, kv_heads * HD)
    )

    def scores_at(key_piece, start):
        count = key_piece.shape[1]
        pos_key = token_positions(
            block_pairs, natural_row(start + jnp.arange(count, dtype=jnp.int32), rows, ctx_sizes)
        )
        keys = key_piece.reshape(seqs, count, kv_heads, HD)
        score = (
            jnp.einsum("bqkgd,bskd->bkgqs", query_rot, keys, preferred_element_type=jnp.float32)
            * factor
        )
        mask = pos_key[None, None, None, None, :] <= pos_query[None, None, None, :, None]
        return (score, mask, keys)

    def attend(carry, pieces, start):
        key_piece, value_piece = pieces
        count = key_piece.shape[1]
        score, mask, keys = scores_at(key_piece, start)
        weights = jnp.where(mask, jnp.exp(score), 0.0)
        total, summed = carry
        values = value_piece.reshape(seqs, count, kv_heads, HD)
        summed = summed + jnp.einsum(
            "bkgqs,bskd->bqkgd",
            weights.astype(jnp.bfloat16),
            values,
            preferred_element_type=jnp.float32,
        )
        return (total + jnp.sum(weights, axis=-1), summed)

    start_carry = (
        jnp.zeros((seqs, kv_heads, group, rows), jnp.float32),
        jnp.zeros((seqs, rows, kv_heads, group, HD), jnp.float32),
    )
    key_value = ctx_gather(jnp.concatenate([key_rot, value_rows], axis=2), 1)
    key_every = key_value[:, :, : kv_heads * HD]
    value_every = key_value[:, :, kv_heads * HD :]
    total, summed = over_blocks(attend, start_carry, (key_every, value_every))
    log_total = jnp.log(total)
    attn_heads = (summed / jnp.transpose(total, (0, 3, 1, 2))[..., None]).astype(jnp.bfloat16)
    attn_out = attn_heads.reshape(flat, heads * HD)
    middle_all = input_all + add_rows(wide_dot(attn_out, output_all))
    middle = lax.dynamic_slice_in_dim(middle_all, offset, local_width, 1)
    scale_ffn, unit_ffn = local_norm(middle_all)
    normed_ffn = (unit_ffn * ffn_gain).astype(jnp.bfloat16)
    gate = wide_dot(normed_ffn, gate_all)
    up_proj = wide_dot(normed_ffn, up_all)
    sigmoid_gate = jax.nn.sigmoid(gate)
    activated = gate * sigmoid_gate
    mixed = (activated * up_proj).astype(jnp.bfloat16)
    block_out = (middle + share_rows(wide_dot(mixed, down_all))).astype(jnp.bfloat16)
    grad_flat = grad_output.reshape(flat, local_width)
    grad_full = full_rows(grad_flat)
    grad_mixed = wide_dot(grad_full, down_all.T)
    down_grad = wide_dot(mixed.T, grad_full)
    grad_gate = (grad_mixed * up_proj * sigmoid_gate * (1.0 + gate * (1.0 - sigmoid_gate))).astype(
        jnp.bfloat16
    )
    grad_up = (grad_mixed * activated).astype(jnp.bfloat16)
    gate_grad = wide_dot(normed_ffn.T, grad_gate)
    up_grad = wide_dot(normed_ffn.T, grad_up)
    grad_normed_ffn = add_rows(wide_dot(grad_gate, gate_all.T) + wide_dot(grad_up, up_all.T))
    back_ffn = local_back(grad_normed_ffn, unit_ffn, scale_ffn, ffn_gain)
    ffn_part = lax.dynamic_slice_in_dim(jnp.sum(grad_normed_ffn * unit_ffn, axis=0), offset, local_width)
    grad_middle_full = grad_full.astype(jnp.float32) + back_ffn
    grad_middle_all = grad_middle_full.astype(jnp.bfloat16)
    grad_attn = wide_dot(grad_middle_all, output_all.T).reshape(seqs, rows, kv_heads, group, HD)
    output_grad = wide_dot(attn_out.T, grad_middle_all)
    delta = jnp.transpose(
        jnp.sum(grad_attn * attn_heads.astype(jnp.float32), axis=-1), (0, 2, 3, 1)
    )
    grad_attn_low = grad_attn.astype(jnp.bfloat16)

    def revisit(grad_query_sum, pieces, start):
        key_piece, value_piece = pieces
        count = key_piece.shape[1]
        score, mask, keys = scores_at(key_piece, start)
        values = value_piece.reshape(seqs, count, kv_heads, HD)
        prob = jnp.where(mask, jnp.exp(score - log_total[..., None]), 0.0)
        grad_prob = jnp.einsum(
            "bqkgd,bskd->bkgqs", grad_attn_low, values, preferred_element_type=jnp.float32
        )
        grad_score = (prob * (grad_prob - delta[..., None]) * factor).astype(jnp.bfloat16)
        grad_query_sum = grad_query_sum + jnp.einsum(
            "bkgqs,bskd->bqkgd", grad_score, keys, preferred_element_type=jnp.float32
        )
        key_term = jnp.einsum(
            "bkgqs,bqkgd->bskd", grad_score, query_rot, preferred_element_type=jnp.float32
        )
        value_term = jnp.einsum(
            "bkgqs,bqkgd->bskd",
            prob.astype(jnp.bfloat16),
            grad_attn_low,
            preferred_element_type=jnp.float32,
        )
        return (
            grad_query_sum,
            jnp.concatenate(
                [
                    key_term.reshape(seqs, count, kv_heads * HD),
                    value_term.reshape(seqs, count, kv_heads * HD),
                ],
                2,
            ),
        )

    whole = key_every.shape[1]
    step = min(whole, 1024)

    def back_turn(grad_query_sum, index):
        start = index * step
        pieces = (
            lax.dynamic_slice_in_dim(key_every, start, step, 1),
            lax.dynamic_slice_in_dim(value_every, start, step, 1),
        )
        return revisit(grad_query_sum, pieces, start)

    grad_query_rot, key_terms = lax.scan(
        back_turn,
        jnp.zeros((seqs, rows, kv_heads, group, HD), jnp.float32),
        jnp.arange(whole // step, dtype=jnp.int32),
    )
    key_terms = jnp.transpose(key_terms, (1, 0, 2, 3)).reshape(seqs, whole, 2 * kv_heads * HD)
    owned = (
        ctx_scatter(key_terms.astype(jnp.bfloat16), 1)
        .astype(jnp.float32)
        .reshape(flat, 2 * kv_heads * HD)
    )
    grad_key_rot = owned[:, : kv_heads * HD].reshape(flat, kv_heads, HD)
    grad_value_low = owned[:, kv_heads * HD :].astype(jnp.bfloat16)
    grad_query_rot = grad_query_rot.reshape(flat, heads, HD)
    grad_query_unit = grad_query_rot * cosine - rotate_half(grad_query_rot * sine)
    grad_key_unit = grad_key_rot * cosine - rotate_half(grad_key_rot * sine)
    query_gain_part = jnp.sum(grad_query_unit * query_unit, axis=(0, 1))
    key_gain_part = jnp.sum(grad_key_unit * key_unit, axis=(0, 1))
    grad_query = (
        head_back(grad_query_unit, query_unit, query_scale, query_gain)
        .astype(jnp.bfloat16)
        .reshape(flat, heads * HD)
    )
    grad_key = (
        head_back(grad_key_unit, key_unit, key_scale, key_gain)
        .astype(jnp.bfloat16)
        .reshape(flat, kv_heads * HD)
    )
    query_grad = wide_dot(normed_attn.T, grad_query)
    key_grad = wide_dot(normed_attn.T, grad_key)
    value_grad = wide_dot(normed_attn.T, grad_value_low)
    grad_normed_attn = add_rows(
        wide_dot(grad_query, query_all.T)
        + wide_dot(grad_key, key_all_w.T)
        + wide_dot(grad_value_low, value_all_w.T)
    )
    back_attn = local_back(grad_normed_attn, unit_attn, scale_attn, attn_gain)
    attn_part = lax.dynamic_slice_in_dim(jnp.sum(grad_normed_attn * unit_attn, axis=0), offset, local_width)
    input_grad = lax.dynamic_slice_in_dim(grad_middle_full + back_attn, offset, local_width, 1)
    grad_pieces = (query_grad, key_grad, value_grad, gate_grad, up_grad, output_grad.T, down_grad.T)
    grad_cat = jnp.concatenate(grad_pieces, axis=1).astype(jnp.bfloat16)
    summed = ctx_scatter(gathered_to_ctx(grad_cat, 0, ctx_sizes[::-1]), 0)
    summed = summed.astype(jnp.float32)
    summed_grads = [summed[:, cuts[i] : cuts[i + 1]] for i in range(len(grad_pieces))]
    query_grad, key_grad, value_grad, gate_grad, up_grad, output_grad, down_grad = summed_grads
    output_grad = output_grad.T
    down_grad = down_grad.T
    attn_placed = lax.dynamic_update_slice_in_dim(
        jnp.zeros((width,), jnp.float32), attn_part, offset, 0
    )
    ffn_placed = lax.dynamic_update_slice_in_dim(
        jnp.zeros((width,), jnp.float32), ffn_part, offset, 0
    )
    gains = (attn_placed, query_gain_part, key_gain_part, ffn_placed)
    for names in (SHARD,) + tuple(reversed(CTX_AXES)):
        gains = lax.psum(gains, names)
    attn_gain_grad, query_gain_grad, key_gain_grad, ffn_gain_grad = gains
    block_out = block_out.reshape(seqs, rows, local_width)
    input_grad = input_grad.reshape(seqs, rows, local_width)
    return (
        block_out,
        input_grad,
        attn_gain_grad,
        query_gain_grad,
        key_gain_grad,
        ffn_gain_grad,
        query_grad,
        key_grad,
        value_grad,
        output_grad,
        gate_grad,
        up_grad,
        down_grad,
    )


def solution(mesh):
    ctx_size, shard_size = mesh.devices.shape
    fine = Mesh(mesh.devices.reshape(2, 4, ctx_size // 8, 2, shard_size // 2), EVERY)
    ctx = CTX_AXES
    in_specs = (
        P(None, ctx, SHARD),
        P(),
        P(),
        P(),
        P(),
        P(),
        P(ctx, SHARD),
        P(ctx, SHARD),
        P(ctx, SHARD),
        P(SHARD, ctx),
        P(ctx, SHARD),
        P(ctx, SHARD),
        P(SHARD, ctx),
        P(None, ctx, SHARD),
    )
    out_specs = (
        P(None, ctx, SHARD),
        P(None, ctx, SHARD),
        P(),
        P(),
        P(),
        P(),
        P(ctx, SHARD),
        P(ctx, SHARD),
        P(ctx, SHARD),
        P(SHARD, ctx),
        P(ctx, SHARD),
        P(ctx, SHARD),
        P(SHARD, ctx),
    )
    return jax.shard_map(
        per_device, mesh=fine, in_specs=in_specs, out_specs=out_specs, check_vma=False
    )
```

```python
import math

import jax
import jax.numpy as jnp
from jax import lax
from jax.sharding import Mesh, PartitionSpec as P

HD = 64
BLK = 64


EPSILON = 1e-05
ROPE_BASE = 1000000.0


def wide_dot(left, right):
    return jnp.dot(left, right, preferred_element_type=jnp.float32)


def token_positions(block_pairs, row_index):
    owner = row_index // (2 * BLK)
    half = row_index // BLK % 2
    devices = jnp.arange(block_pairs.shape[0], dtype=jnp.int32)
    chosen = jnp.where(half[:, None] == 0, block_pairs[None, :, 0], block_pairs[None, :, 1])
    number = jnp.sum(jnp.where(owner[:, None] == devices[None, :], chosen, 0), axis=1)
    return number * BLK + row_index % BLK


def rope_tables(positions):
    index = jnp.arange(HD // 2, dtype=jnp.float32)
    inverse = jnp.exp(index * (-2.0 * math.log(ROPE_BASE) / HD))
    angle = positions.astype(jnp.float32)[:, None] * inverse[None, :]
    cosine = jnp.cos(angle)
    sine = jnp.sin(angle)
    return (
        jnp.concatenate([cosine, cosine], 1)[:, None, :],
        jnp.concatenate([sine, sine], 1)[:, None, :],
    )


def rotate_half(values):
    middle = values.shape[-1] // 2
    return jnp.concatenate([-values[..., middle:], values[..., :middle]], -1)


def head_norm(values):
    scale = lax.rsqrt(jnp.mean(values * values, axis=-1, keepdims=True) + EPSILON)
    return (scale, values * scale)


def head_back(grad_normed, unit, scale, gain):
    scaled = grad_normed * gain
    inner = jnp.mean(scaled * unit, axis=-1, keepdims=True)
    return scale * (scaled - unit * inner)


CTX_AXES = ("cx", "cy", "cz")
SHARD = ("sx", "sc")
EVERY = CTX_AXES + SHARD


GATHER_STAGES = (("cx",), ("cy", "cz"))
SCATTER_STAGES = tuple(reversed(GATHER_STAGES))
GATHERED_ORDER = tuple(name for stage in reversed(GATHER_STAGES) for name in stage)
SCATTER_ORDER = tuple(name for stage in SCATTER_STAGES for name in stage)


def ctx_gather(local, axis):
    for names in GATHER_STAGES:
        local = lax.all_gather(local, names, axis=axis, tiled=True)
    return local


def ctx_scatter(partial_value, axis):
    for names in SCATTER_STAGES:
        partial_value = lax.psum_scatter(partial_value, names, scatter_dimension=axis, tiled=True)
    return partial_value


def reorder_blocks(values, axis, source, target):
    sizes = [lax.axis_size(name) for name in source]
    shape = values.shape
    block = shape[axis] // math.prod(sizes)
    split = values.reshape(shape[:axis] + tuple(sizes) + (block,) + shape[axis + 1 :])
    order = list(range(axis)) + [axis + source.index(name) for name in target]
    order += list(range(axis + len(source), split.ndim))
    return jnp.transpose(split, order).reshape(shape)


def natural_row(index, rows):
    device = index // rows
    place = {}
    for name in reversed(GATHERED_ORDER):
        size = lax.axis_size(name)
        place[name] = device % size
        device = device // size
    natural = 0
    for name in CTX_AXES:
        natural = natural * lax.axis_size(name) + place[name]
    return natural * rows + index % rows


def rows_total(partial_value):
    return lax.psum(partial_value, SHARD)


def full_rows(local):
    return lax.all_gather(local, SHARD, axis=1, tiled=True)


def share_rows(partial_value):
    shards = lax.axis_size(SHARD)
    rows, cols = partial_value.shape
    blocks = partial_value.astype(jnp.bfloat16).reshape(rows, shards, cols // shards)
    blocks = lax.all_to_all(blocks, SHARD, 1, 1, tiled=True)
    return jnp.sum(blocks.astype(jnp.float32), axis=1)


def add_rows(partial_value):
    pieces = lax.all_gather(partial_value.astype(jnp.bfloat16), SHARD, axis=0)
    return jnp.sum(pieces.astype(jnp.float32), axis=0)


def local_norm(values):
    scale = lax.rsqrt(jnp.mean(values * values, axis=1, keepdims=True) + EPSILON)
    return (scale, values * scale)


def local_back(grad_normed, unit, scale, gain):
    scaled = grad_normed * gain
    inner = jnp.mean(scaled * unit, axis=1, keepdims=True)
    return scale * (scaled - unit * inner)


def row_norm(values, width):
    total = rows_total(jnp.sum(values * values, axis=1))
    scale = lax.rsqrt(total / width + EPSILON)[:, None]
    return (scale, values * scale)


def norm_back(grad_normed, unit, scale, gain, width):
    scaled = grad_normed * gain
    inner = rows_total(jnp.sum(scaled * unit, axis=1)) / width
    return (scale * (scaled - unit * inner[:, None]), jnp.sum(grad_normed * unit, axis=0))


def over_blocks(step_fn, carry, arrays):
    whole = arrays[0].shape[1]
    step = min(whole, 1024)

    def turn(index, state):
        start = index * step
        pieces = tuple((lax.dynamic_slice_in_dim(array, start, step, 1) for array in arrays))
        return step_fn(state, pieces, start)

    return lax.fori_loop(0, whole // step, turn, carry)


def per_device(
    block_in,
    block_pairs,
    attn_gain,
    query_gain,
    key_gain,
    ffn_gain,
    w_query,
    w_key,
    w_value,
    w_output,
    w_gate,
    w_up,
    w_down,
    grad_output,
):
    seqs, rows, local_width = block_in.shape
    flat = seqs * rows
    width = local_width * lax.axis_size(SHARD)
    offset = lax.axis_index(SHARD) * local_width
    pieces = (w_query, w_key, w_value, w_gate, w_up, w_output.T, w_down.T)
    widths = [piece.shape[1] for piece in pieces]
    cuts = [sum(widths[:i]) for i in range(len(widths) + 1)]
    every_weight = ctx_gather(jnp.concatenate(pieces, axis=1), 0)
    every_weight = reorder_blocks(every_weight, 0, GATHERED_ORDER, CTX_AXES)
    gathered = [every_weight[:, cuts[i] : cuts[i + 1]] for i in range(len(pieces))]
    query_all, key_all_w, value_all_w, gate_all, up_all, output_all, down_all = gathered
    output_all = output_all.T
    down_all = down_all.T
    heads = query_all.shape[1] // HD
    kv_heads = key_all_w.shape[1] // HD
    group = heads // kv_heads
    factor = 1.0 / math.sqrt(HD)
    pos_query = token_positions(
        block_pairs, lax.axis_index(CTX_AXES) * rows + jnp.arange(rows, dtype=jnp.int32)
    )
    cosine_one, sine_one = rope_tables(pos_query)
    cosine = jnp.tile(cosine_one, (seqs, 1, 1))
    sine = jnp.tile(sine_one, (seqs, 1, 1))
    attn_slice = lax.dynamic_slice_in_dim(attn_gain, offset, local_width)
    ffn_slice = lax.dynamic_slice_in_dim(ffn_gain, offset, local_width)
    input_all = full_rows(block_in.reshape(flat, local_width)).astype(jnp.float32)
    scale_attn, unit_attn = local_norm(input_all)
    normed_attn = (unit_attn * attn_gain).astype(jnp.bfloat16)
    query_raw = wide_dot(normed_attn, query_all).reshape(flat, heads, HD)
    key_raw = wide_dot(normed_attn, key_all_w).reshape(flat, kv_heads, HD)
    value_rows = (
        wide_dot(normed_attn, value_all_w).astype(jnp.bfloat16).reshape(seqs, rows, kv_heads * HD)
    )
    query_scale, query_unit = head_norm(query_raw)
    key_scale, key_unit = head_norm(key_raw)
    query_norm = query_unit * query_gain
    key_norm = key_unit * key_gain
    query_rot = (
        (query_norm * cosine + rotate_half(query_norm) * sine)
        .astype(jnp.bfloat16)
        .reshape(seqs, rows, kv_heads, group, HD)
    )
    key_rot = (
        (key_norm * cosine + rotate_half(key_norm) * sine)
        .astype(jnp.bfloat16)
        .reshape(seqs, rows, kv_heads * HD)
    )

    def scores_at(key_piece, start):
        count = key_piece.shape[1]
        pos_key = token_positions(
            block_pairs, natural_row(start + jnp.arange(count, dtype=jnp.int32), rows)
        )
        keys = key_piece.reshape(seqs, count, kv_heads, HD)
        score = (
            jnp.einsum("bqkgd,bskd->bkgqs", query_rot, keys, preferred_element_type=jnp.float32)
            * factor
        )
        mask = pos_key[None, None, None, None, :] <= pos_query[None, None, None, :, None]
        return (score, mask, keys)

    def attend(carry, pieces, start):
        key_piece, value_piece = pieces
        count = key_piece.shape[1]
        score, mask, keys = scores_at(key_piece, start)
        weights = jnp.where(mask, jnp.exp(score), 0.0)
        total, summed = carry
        values = value_piece.reshape(seqs, count, kv_heads, HD)
        summed = summed + jnp.einsum(
            "bkgqs,bskd->bqkgd",
            weights.astype(jnp.bfloat16),
            values,
            preferred_element_type=jnp.float32,
        )
        return (total + jnp.sum(weights, axis=-1), summed)

    start_carry = (
        jnp.zeros((seqs, kv_heads, group, rows), jnp.float32),
        jnp.zeros((seqs, rows, kv_heads, group, HD), jnp.float32),
    )
    key_value = ctx_gather(jnp.concatenate([key_rot, value_rows], axis=2), 1)
    key_every = key_value[:, :, : kv_heads * HD]
    value_every = key_value[:, :, kv_heads * HD :]
    total, summed = over_blocks(attend, start_carry, (key_every, value_every))
    log_total = jnp.log(total)
    attn_heads = (summed / jnp.transpose(total, (0, 3, 1, 2))[..., None]).astype(jnp.bfloat16)
    attn_out = attn_heads.reshape(flat, heads * HD)
    middle_all = input_all + add_rows(wide_dot(attn_out, output_all))
    middle = lax.dynamic_slice_in_dim(middle_all, offset, local_width, 1)
    scale_ffn, unit_ffn = local_norm(middle_all)
    normed_ffn = (unit_ffn * ffn_gain).astype(jnp.bfloat16)
    gate = wide_dot(normed_ffn, gate_all)
    up_proj = wide_dot(normed_ffn, up_all)
    sigmoid_gate = jax.nn.sigmoid(gate)
    activated = gate * sigmoid_gate
    mixed = (activated * up_proj).astype(jnp.bfloat16)
    block_out = (middle + share_rows(wide_dot(mixed, down_all))).astype(jnp.bfloat16)
    grad_flat = grad_output.reshape(flat, local_width)
    grad_full = full_rows(grad_flat)
    grad_mixed = wide_dot(grad_full, down_all.T)
    down_grad = wide_dot(mixed.T, grad_full)
    grad_gate = (grad_mixed * up_proj * sigmoid_gate * (1.0 + gate * (1.0 - sigmoid_gate))).astype(
        jnp.bfloat16
    )
    grad_up = (grad_mixed * activated).astype(jnp.bfloat16)
    gate_grad = wide_dot(normed_ffn.T, grad_gate)
    up_grad = wide_dot(normed_ffn.T, grad_up)
    grad_normed_ffn = add_rows(wide_dot(grad_gate, gate_all.T) + wide_dot(grad_up, up_all.T))
    back_ffn = local_back(grad_normed_ffn, unit_ffn, scale_ffn, ffn_gain)
    ffn_part = lax.dynamic_slice_in_dim(jnp.sum(grad_normed_ffn * unit_ffn, axis=0), offset, local_width)
    grad_middle_full = grad_full.astype(jnp.float32) + back_ffn
    grad_middle_all = grad_middle_full.astype(jnp.bfloat16)
    grad_attn = wide_dot(grad_middle_all, output_all.T).reshape(seqs, rows, kv_heads, group, HD)
    output_grad = wide_dot(attn_out.T, grad_middle_all)
    delta = jnp.transpose(
        jnp.sum(grad_attn * attn_heads.astype(jnp.float32), axis=-1), (0, 2, 3, 1)
    )
    grad_attn_low = grad_attn.astype(jnp.bfloat16)

    def revisit(grad_query_sum, pieces, start):
        key_piece, value_piece = pieces
        count = key_piece.shape[1]
        score, mask, keys = scores_at(key_piece, start)
        values = value_piece.reshape(seqs, count, kv_heads, HD)
        prob = jnp.where(mask, jnp.exp(score - log_total[..., None]), 0.0)
        grad_prob = jnp.einsum(
            "bqkgd,bskd->bkgqs", grad_attn_low, values, preferred_element_type=jnp.float32
        )
        grad_score = (prob * (grad_prob - delta[..., None]) * factor).astype(jnp.bfloat16)
        grad_query_sum = grad_query_sum + jnp.einsum(
            "bkgqs,bskd->bqkgd", grad_score, keys, preferred_element_type=jnp.float32
        )
        key_term = jnp.einsum(
            "bkgqs,bqkgd->bskd", grad_score, query_rot, preferred_element_type=jnp.float32
        )
        value_term = jnp.einsum(
            "bkgqs,bqkgd->bskd",
            prob.astype(jnp.bfloat16),
            grad_attn_low,
            preferred_element_type=jnp.float32,
        )
        return (
            grad_query_sum,
            jnp.concatenate(
                [
                    key_term.reshape(seqs, count, kv_heads * HD),
                    value_term.reshape(seqs, count, kv_heads * HD),
                ],
                2,
            ),
        )

    whole = key_every.shape[1]
    step = min(whole, 1024)

    def back_turn(grad_query_sum, index):
        start = index * step
        pieces = (
            lax.dynamic_slice_in_dim(key_every, start, step, 1),
            lax.dynamic_slice_in_dim(value_every, start, step, 1),
        )
        return revisit(grad_query_sum, pieces, start)

    grad_query_rot, key_terms = lax.scan(
        back_turn,
        jnp.zeros((seqs, rows, kv_heads, group, HD), jnp.float32),
        jnp.arange(whole // step, dtype=jnp.int32),
    )
    key_terms = jnp.transpose(key_terms, (1, 0, 2, 3)).reshape(seqs, whole, 2 * kv_heads * HD)
    owned = (
        ctx_scatter(key_terms.astype(jnp.bfloat16), 1)
        .astype(jnp.float32)
        .reshape(flat, 2 * kv_heads * HD)
    )
    grad_key_rot = owned[:, : kv_heads * HD].reshape(flat, kv_heads, HD)
    grad_value_low = owned[:, kv_heads * HD :].astype(jnp.bfloat16)
    grad_query_rot = grad_query_rot.reshape(flat, heads, HD)
    grad_query_unit = grad_query_rot * cosine - rotate_half(grad_query_rot * sine)
    grad_key_unit = grad_key_rot * cosine - rotate_half(grad_key_rot * sine)
    query_gain_part = jnp.sum(grad_query_unit * query_unit, axis=(0, 1))
    key_gain_part = jnp.sum(grad_key_unit * key_unit, axis=(0, 1))
    grad_query = (
        head_back(grad_query_unit, query_unit, query_scale, query_gain)
        .astype(jnp.bfloat16)
        .reshape(flat, heads * HD)
    )
    grad_key = (
        head_back(grad_key_unit, key_unit, key_scale, key_gain)
        .astype(jnp.bfloat16)
        .reshape(flat, kv_heads * HD)
    )
    query_grad = wide_dot(normed_attn.T, grad_query)
    key_grad = wide_dot(normed_attn.T, grad_key)
    value_grad = wide_dot(normed_attn.T, grad_value_low)
    grad_normed_attn = add_rows(
        wide_dot(grad_query, query_all.T)
        + wide_dot(grad_key, key_all_w.T)
        + wide_dot(grad_value_low, value_all_w.T)
    )
    back_attn = local_back(grad_normed_attn, unit_attn, scale_attn, attn_gain)
    attn_part = lax.dynamic_slice_in_dim(jnp.sum(grad_normed_attn * unit_attn, axis=0), offset, local_width)
    input_grad = lax.dynamic_slice_in_dim(grad_middle_full + back_attn, offset, local_width, 1)
    grad_pieces = (query_grad, key_grad, value_grad, gate_grad, up_grad, output_grad.T, down_grad.T)
    grad_cat = jnp.concatenate(grad_pieces, axis=1).astype(jnp.bfloat16)
    summed = ctx_scatter(reorder_blocks(grad_cat, 0, CTX_AXES, SCATTER_ORDER), 0)
    summed = summed.astype(jnp.float32)
    summed_grads = [summed[:, cuts[i] : cuts[i + 1]] for i in range(len(grad_pieces))]
    query_grad, key_grad, value_grad, gate_grad, up_grad, output_grad, down_grad = summed_grads
    output_grad = output_grad.T
    down_grad = down_grad.T
    attn_placed = lax.dynamic_update_slice_in_dim(
        jnp.zeros((width,), jnp.float32), attn_part, offset, 0
    )
    ffn_placed = lax.dynamic_update_slice_in_dim(
        jnp.zeros((width,), jnp.float32), ffn_part, offset, 0
    )
    gains = (attn_placed, query_gain_part, key_gain_part, ffn_placed)
    for names in (SHARD,) + tuple(reversed(CTX_AXES)):
        gains = lax.psum(gains, names)
    attn_gain_grad, query_gain_grad, key_gain_grad, ffn_gain_grad = gains
    block_out = block_out.reshape(seqs, rows, local_width)
    input_grad = input_grad.reshape(seqs, rows, local_width)
    return (
        block_out,
        input_grad,
        attn_gain_grad,
        query_gain_grad,
        key_gain_grad,
        ffn_gain_grad,
        query_grad,
        key_grad,
        value_grad,
        output_grad,
        gate_grad,
        up_grad,
        down_grad,
    )


def solution(mesh):
    ctx_size, shard_size = mesh.devices.shape
    fine = Mesh(mesh.devices.reshape(2, 4, ctx_size // 8, 2, shard_size // 2), EVERY)
    ctx = CTX_AXES
    in_specs = (
        P(None, ctx, SHARD),
        P(),
        P(),
        P(),
        P(),
        P(),
        P(ctx, SHARD),
        P(ctx, SHARD),
        P(ctx, SHARD),
        P(SHARD, ctx),
        P(ctx, SHARD),
        P(ctx, SHARD),
        P(SHARD, ctx),
        P(None, ctx, SHARD),
    )
    out_specs = (
        P(None, ctx, SHARD),
        P(None, ctx, SHARD),
        P(),
        P(),
        P(),
        P(),
        P(ctx, SHARD),
        P(ctx, SHARD),
        P(ctx, SHARD),
        P(SHARD, ctx),
        P(ctx, SHARD),
        P(ctx, SHARD),
        P(SHARD, ctx),
    )
    return jax.shard_map(
        per_device, mesh=fine, in_specs=in_specs, out_specs=out_specs, check_vma=False
    )
```

```python
import math

import jax
import jax.numpy as jnp
from jax import lax
from jax.sharding import Mesh, PartitionSpec as P

HD = 64
BLK = 64


EPSILON = 1e-05
ROPE_BASE = 1000000.0


def wide_dot(left, right):
    return jnp.dot(left, right, preferred_element_type=jnp.float32)


def token_positions(block_pairs, row_index):
    owner = row_index // (2 * BLK)
    half = row_index // BLK % 2
    devices = jnp.arange(block_pairs.shape[0], dtype=jnp.int32)
    chosen = jnp.where(half[:, None] == 0, block_pairs[None, :, 0], block_pairs[None, :, 1])
    number = jnp.sum(jnp.where(owner[:, None] == devices[None, :], chosen, 0), axis=1)
    return number * BLK + row_index % BLK


def rope_tables(positions):
    index = jnp.arange(HD // 2, dtype=jnp.float32)
    inverse = jnp.exp(index * (-2.0 * math.log(ROPE_BASE) / HD))
    angle = positions.astype(jnp.float32)[:, None] * inverse[None, :]
    cosine = jnp.cos(angle)
    sine = jnp.sin(angle)
    return (
        jnp.concatenate([cosine, cosine], 1)[:, None, :],
        jnp.concatenate([sine, sine], 1)[:, None, :],
    )


def rotate_half(values):
    middle = values.shape[-1] // 2
    return jnp.concatenate([-values[..., middle:], values[..., :middle]], -1)


def head_norm(values):
    scale = lax.rsqrt(jnp.mean(values * values, axis=-1, keepdims=True) + EPSILON)
    return (scale, values * scale)


def head_back(grad_normed, unit, scale, gain):
    scaled = grad_normed * gain
    inner = jnp.mean(scaled * unit, axis=-1, keepdims=True)
    return scale * (scaled - unit * inner)


CTX_AXES = ("cx", "cy", "cz")
SHARD = ("sx", "sc")
EVERY = CTX_AXES + SHARD


GATHER_STAGES = (("cx",), ("cy", "cz"))
SCATTER_STAGES = tuple(reversed(GATHER_STAGES))
GATHERED_ORDER = tuple(name for stage in reversed(GATHER_STAGES) for name in stage)
SCATTER_ORDER = tuple(name for stage in SCATTER_STAGES for name in stage)


def ctx_gather(local, axis):
    for names in GATHER_STAGES:
        local = lax.all_gather(local, names, axis=axis, tiled=True)
    return local


def ctx_scatter(partial_value, axis, stages=SCATTER_STAGES):
    for names in stages:
        partial_value = lax.psum_scatter(partial_value, names, scatter_dimension=axis, tiled=True)
    return partial_value


def reorder_blocks(values, axis, source, target):
    sizes = [lax.axis_size(name) for name in source]
    shape = values.shape
    block = shape[axis] // math.prod(sizes)
    split = values.reshape(shape[:axis] + tuple(sizes) + (block,) + shape[axis + 1 :])
    order = list(range(axis)) + [axis + source.index(name) for name in target]
    order += list(range(axis + len(source), split.ndim))
    return jnp.transpose(split, order).reshape(shape)


def natural_row(index, rows):
    device = index // rows
    place = {}
    for name in reversed(GATHERED_ORDER):
        size = lax.axis_size(name)
        place[name] = device % size
        device = device // size
    natural = 0
    for name in CTX_AXES:
        natural = natural * lax.axis_size(name) + place[name]
    return natural * rows + index % rows


def start_sum_over_ctx(pieces):
    joined = jnp.concatenate(pieces, axis=1).astype(jnp.bfloat16)
    joined = reorder_blocks(joined, 0, CTX_AXES, SCATTER_ORDER)
    return ctx_scatter(joined, 0, SCATTER_STAGES[:1])


def finish_sum_over_ctx(partial_value, pieces):
    widths = [piece.shape[1] for piece in pieces]
    cuts = [sum(widths[:i]) for i in range(len(widths) + 1)]
    summed = ctx_scatter(partial_value, 0, SCATTER_STAGES[1:]).astype(jnp.float32)
    return [summed[:, cuts[i] : cuts[i + 1]] for i in range(len(pieces))]


def sum_over_ctx(pieces):
    return finish_sum_over_ctx(start_sum_over_ctx(pieces), pieces)


def rows_total(partial_value):
    return lax.psum(partial_value, SHARD)


def full_rows(local):
    return lax.all_gather(local, SHARD, axis=1, tiled=True)


def share_rows(partial_value):
    shards = lax.axis_size(SHARD)
    rows, cols = partial_value.shape
    blocks = partial_value.astype(jnp.bfloat16).reshape(rows, shards, cols // shards)
    blocks = lax.all_to_all(blocks, SHARD, 1, 1, tiled=True)
    return jnp.sum(blocks.astype(jnp.float32), axis=1)


def add_rows(partial_value):
    pieces = lax.all_gather(partial_value.astype(jnp.bfloat16), SHARD, axis=0)
    return jnp.sum(pieces.astype(jnp.float32), axis=0)


def local_norm(values):
    scale = lax.rsqrt(jnp.mean(values * values, axis=1, keepdims=True) + EPSILON)
    return (scale, values * scale)


def local_back(grad_normed, unit, scale, gain):
    scaled = grad_normed * gain
    inner = jnp.mean(scaled * unit, axis=1, keepdims=True)
    return scale * (scaled - unit * inner)


def row_norm(values, width):
    total = rows_total(jnp.sum(values * values, axis=1))
    scale = lax.rsqrt(total / width + EPSILON)[:, None]
    return (scale, values * scale)


def norm_back(grad_normed, unit, scale, gain, width):
    scaled = grad_normed * gain
    inner = rows_total(jnp.sum(scaled * unit, axis=1)) / width
    return (scale * (scaled - unit * inner[:, None]), jnp.sum(grad_normed * unit, axis=0))


def over_blocks(step_fn, carry, arrays):
    whole = arrays[0].shape[1]
    step = min(whole, 1024)

    def turn(index, state):
        start = index * step
        pieces = tuple((lax.dynamic_slice_in_dim(array, start, step, 1) for array in arrays))
        return step_fn(state, pieces, start)

    return lax.fori_loop(0, whole // step, turn, carry)


def per_device(
    block_in,
    block_pairs,
    attn_gain,
    query_gain,
    key_gain,
    ffn_gain,
    w_query,
    w_key,
    w_value,
    w_output,
    w_gate,
    w_up,
    w_down,
    grad_output,
):
    seqs, rows, local_width = block_in.shape
    flat = seqs * rows
    width = local_width * lax.axis_size(SHARD)
    offset = lax.axis_index(SHARD) * local_width
    pieces = (w_query, w_key, w_value, w_gate, w_up, w_output.T, w_down.T)
    widths = [piece.shape[1] for piece in pieces]
    cuts = [sum(widths[:i]) for i in range(len(widths) + 1)]
    every_weight = ctx_gather(jnp.concatenate(pieces, axis=1), 0)
    every_weight = reorder_blocks(every_weight, 0, GATHERED_ORDER, CTX_AXES)
    gathered = [every_weight[:, cuts[i] : cuts[i + 1]] for i in range(len(pieces))]
    query_all, key_all_w, value_all_w, gate_all, up_all, output_all, down_all = gathered
    output_all = output_all.T
    down_all = down_all.T
    heads = query_all.shape[1] // HD
    kv_heads = key_all_w.shape[1] // HD
    group = heads // kv_heads
    factor = 1.0 / math.sqrt(HD)
    pos_query = token_positions(
        block_pairs, lax.axis_index(CTX_AXES) * rows + jnp.arange(rows, dtype=jnp.int32)
    )
    cosine_one, sine_one = rope_tables(pos_query)
    cosine = jnp.tile(cosine_one, (seqs, 1, 1))
    sine = jnp.tile(sine_one, (seqs, 1, 1))
    attn_slice = lax.dynamic_slice_in_dim(attn_gain, offset, local_width)
    ffn_slice = lax.dynamic_slice_in_dim(ffn_gain, offset, local_width)
    input_all = full_rows(block_in.reshape(flat, local_width)).astype(jnp.float32)
    scale_attn, unit_attn = local_norm(input_all)
    normed_attn = (unit_attn * attn_gain).astype(jnp.bfloat16)
    query_raw = wide_dot(normed_attn, query_all).reshape(flat, heads, HD)
    key_raw = wide_dot(normed_attn, key_all_w).reshape(flat, kv_heads, HD)
    value_rows = (
        wide_dot(normed_attn, value_all_w).astype(jnp.bfloat16).reshape(seqs, rows, kv_heads * HD)
    )
    query_scale, query_unit = head_norm(query_raw)
    key_scale, key_unit = head_norm(key_raw)
    query_norm = query_unit * query_gain
    key_norm = key_unit * key_gain
    query_rot = (
        (query_norm * cosine + rotate_half(query_norm) * sine)
        .astype(jnp.bfloat16)
        .reshape(seqs, rows, kv_heads, group, HD)
    )
    key_rot = (
        (key_norm * cosine + rotate_half(key_norm) * sine)
        .astype(jnp.bfloat16)
        .reshape(seqs, rows, kv_heads * HD)
    )

    def scores_at(key_piece, start):
        count = key_piece.shape[1]
        pos_key = token_positions(
            block_pairs, natural_row(start + jnp.arange(count, dtype=jnp.int32), rows)
        )
        keys = key_piece.reshape(seqs, count, kv_heads, HD)
        score = (
            jnp.einsum("bqkgd,bskd->bkgqs", query_rot, keys, preferred_element_type=jnp.float32)
            * factor
        )
        mask = pos_key[None, None, None, None, :] <= pos_query[None, None, None, :, None]
        return (score, mask, keys)

    def attend(carry, pieces, start):
        key_piece, value_piece = pieces
        count = key_piece.shape[1]
        score, mask, keys = scores_at(key_piece, start)
        weights = jnp.where(mask, jnp.exp(score), 0.0)
        total, summed = carry
        values = value_piece.reshape(seqs, count, kv_heads, HD)
        summed = summed + jnp.einsum(
            "bkgqs,bskd->bqkgd",
            weights.astype(jnp.bfloat16),
            values,
            preferred_element_type=jnp.float32,
        )
        return (total + jnp.sum(weights, axis=-1), summed)

    start_carry = (
        jnp.zeros((seqs, kv_heads, group, rows), jnp.float32),
        jnp.zeros((seqs, rows, kv_heads, group, HD), jnp.float32),
    )
    key_value = ctx_gather(jnp.concatenate([key_rot, value_rows], axis=2), 1)
    key_every = key_value[:, :, : kv_heads * HD]
    value_every = key_value[:, :, kv_heads * HD :]
    total, summed = over_blocks(attend, start_carry, (key_every, value_every))
    log_total = jnp.log(total)
    attn_heads = (summed / jnp.transpose(total, (0, 3, 1, 2))[..., None]).astype(jnp.bfloat16)
    attn_out = attn_heads.reshape(flat, heads * HD)
    middle_all = input_all + add_rows(wide_dot(attn_out, output_all))
    middle = lax.dynamic_slice_in_dim(middle_all, offset, local_width, 1)
    scale_ffn, unit_ffn = local_norm(middle_all)
    normed_ffn = (unit_ffn * ffn_gain).astype(jnp.bfloat16)
    gate = wide_dot(normed_ffn, gate_all)
    up_proj = wide_dot(normed_ffn, up_all)
    sigmoid_gate = jax.nn.sigmoid(gate)
    activated = gate * sigmoid_gate
    mixed = (activated * up_proj).astype(jnp.bfloat16)
    block_out = (middle + share_rows(wide_dot(mixed, down_all))).astype(jnp.bfloat16)
    grad_flat = grad_output.reshape(flat, local_width)
    grad_full = full_rows(grad_flat)
    grad_mixed = wide_dot(grad_full, down_all.T)
    down_grad = wide_dot(mixed.T, grad_full)
    grad_gate = (grad_mixed * up_proj * sigmoid_gate * (1.0 + gate * (1.0 - sigmoid_gate))).astype(
        jnp.bfloat16
    )
    grad_up = (grad_mixed * activated).astype(jnp.bfloat16)
    gate_grad = wide_dot(normed_ffn.T, grad_gate)
    up_grad = wide_dot(normed_ffn.T, grad_up)
    ffn_pieces = (gate_grad, up_grad, down_grad.T)
    ffn_partial = start_sum_over_ctx(ffn_pieces)
    grad_normed_ffn = add_rows(wide_dot(grad_gate, gate_all.T) + wide_dot(grad_up, up_all.T))
    back_ffn = local_back(grad_normed_ffn, unit_ffn, scale_ffn, ffn_gain)
    ffn_part = lax.dynamic_slice_in_dim(jnp.sum(grad_normed_ffn * unit_ffn, axis=0), offset, local_width)
    grad_middle_full = grad_full.astype(jnp.float32) + back_ffn
    grad_middle_all = grad_middle_full.astype(jnp.bfloat16)
    grad_attn = wide_dot(grad_middle_all, output_all.T).reshape(seqs, rows, kv_heads, group, HD)
    output_grad = wide_dot(attn_out.T, grad_middle_all)
    delta = jnp.transpose(
        jnp.sum(grad_attn * attn_heads.astype(jnp.float32), axis=-1), (0, 2, 3, 1)
    )
    grad_attn_low = grad_attn.astype(jnp.bfloat16)

    def revisit(grad_query_sum, pieces, start):
        key_piece, value_piece = pieces
        count = key_piece.shape[1]
        score, mask, keys = scores_at(key_piece, start)
        values = value_piece.reshape(seqs, count, kv_heads, HD)
        prob = jnp.where(mask, jnp.exp(score - log_total[..., None]), 0.0)
        grad_prob = jnp.einsum(
            "bqkgd,bskd->bkgqs", grad_attn_low, values, preferred_element_type=jnp.float32
        )
        grad_score = (prob * (grad_prob - delta[..., None]) * factor).astype(jnp.bfloat16)
        grad_query_sum = grad_query_sum + jnp.einsum(
            "bkgqs,bskd->bqkgd", grad_score, keys, preferred_element_type=jnp.float32
        )
        key_term = jnp.einsum(
            "bkgqs,bqkgd->bskd", grad_score, query_rot, preferred_element_type=jnp.float32
        )
        value_term = jnp.einsum(
            "bkgqs,bqkgd->bskd",
            prob.astype(jnp.bfloat16),
            grad_attn_low,
            preferred_element_type=jnp.float32,
        )
        return (
            grad_query_sum,
            jnp.concatenate(
                [
                    key_term.reshape(seqs, count, kv_heads * HD),
                    value_term.reshape(seqs, count, kv_heads * HD),
                ],
                2,
            ),
        )

    whole = key_every.shape[1]
    step = min(whole, 1024)

    def back_turn(grad_query_sum, index):
        start = index * step
        pieces = (
            lax.dynamic_slice_in_dim(key_every, start, step, 1),
            lax.dynamic_slice_in_dim(value_every, start, step, 1),
        )
        return revisit(grad_query_sum, pieces, start)

    grad_query_rot, key_terms = lax.scan(
        back_turn,
        jnp.zeros((seqs, rows, kv_heads, group, HD), jnp.float32),
        jnp.arange(whole // step, dtype=jnp.int32),
    )
    key_terms = jnp.transpose(key_terms, (1, 0, 2, 3)).reshape(seqs, whole, 2 * kv_heads * HD)
    key_terms, ffn_partial = lax.optimization_barrier((key_terms, ffn_partial))
    ffn_summed = finish_sum_over_ctx(ffn_partial, ffn_pieces)
    owned = (
        ctx_scatter(key_terms.astype(jnp.bfloat16), 1, tuple((name,) for name in GATHERED_ORDER))
        .astype(jnp.float32)
        .reshape(flat, 2 * kv_heads * HD)
    )
    grad_key_rot = owned[:, : kv_heads * HD].reshape(flat, kv_heads, HD)
    grad_value_low = owned[:, kv_heads * HD :].astype(jnp.bfloat16)
    grad_query_rot = grad_query_rot.reshape(flat, heads, HD)
    grad_query_unit = grad_query_rot * cosine - rotate_half(grad_query_rot * sine)
    grad_key_unit = grad_key_rot * cosine - rotate_half(grad_key_rot * sine)
    query_gain_part = jnp.sum(grad_query_unit * query_unit, axis=(0, 1))
    key_gain_part = jnp.sum(grad_key_unit * key_unit, axis=(0, 1))
    grad_query = (
        head_back(grad_query_unit, query_unit, query_scale, query_gain)
        .astype(jnp.bfloat16)
        .reshape(flat, heads * HD)
    )
    grad_key = (
        head_back(grad_key_unit, key_unit, key_scale, key_gain)
        .astype(jnp.bfloat16)
        .reshape(flat, kv_heads * HD)
    )
    query_grad = wide_dot(normed_attn.T, grad_query)
    key_grad = wide_dot(normed_attn.T, grad_key)
    value_grad = wide_dot(normed_attn.T, grad_value_low)
    grad_normed_attn = add_rows(
        wide_dot(grad_query, query_all.T)
        + wide_dot(grad_key, key_all_w.T)
        + wide_dot(grad_value_low, value_all_w.T)
    )
    back_attn = local_back(grad_normed_attn, unit_attn, scale_attn, attn_gain)
    attn_part = lax.dynamic_slice_in_dim(jnp.sum(grad_normed_attn * unit_attn, axis=0), offset, local_width)
    input_grad = lax.dynamic_slice_in_dim(grad_middle_full + back_attn, offset, local_width, 1)
    attn_pieces = (query_grad, key_grad, value_grad, output_grad.T)
    attn_pieces, grad_normed_attn = lax.optimization_barrier((attn_pieces, grad_normed_attn))
    query_grad, key_grad, value_grad, output_grad = sum_over_ctx(attn_pieces)
    gate_grad, up_grad, down_grad = ffn_summed
    output_grad = output_grad.T
    down_grad = down_grad.T
    attn_placed = lax.dynamic_update_slice_in_dim(
        jnp.zeros((width,), jnp.float32), attn_part, offset, 0
    )
    ffn_placed = lax.dynamic_update_slice_in_dim(
        jnp.zeros((width,), jnp.float32), ffn_part, offset, 0
    )
    gains = (attn_placed, query_gain_part, key_gain_part, ffn_placed)
    for names in (SHARD,) + tuple(reversed(CTX_AXES)):
        gains = lax.psum(gains, names)
    attn_gain_grad, query_gain_grad, key_gain_grad, ffn_gain_grad = gains
    block_out = block_out.reshape(seqs, rows, local_width)
    input_grad = input_grad.reshape(seqs, rows, local_width)
    return (
        block_out,
        input_grad,
        attn_gain_grad,
        query_gain_grad,
        key_gain_grad,
        ffn_gain_grad,
        query_grad,
        key_grad,
        value_grad,
        output_grad,
        gate_grad,
        up_grad,
        down_grad,
    )


def solution(mesh):
    ctx_size, shard_size = mesh.devices.shape
    fine = Mesh(mesh.devices.reshape(2, 4, ctx_size // 8, 2, shard_size // 2), EVERY)
    ctx = CTX_AXES
    in_specs = (
        P(None, ctx, SHARD),
        P(),
        P(),
        P(),
        P(),
        P(),
        P(ctx, SHARD),
        P(ctx, SHARD),
        P(ctx, SHARD),
        P(SHARD, ctx),
        P(ctx, SHARD),
        P(ctx, SHARD),
        P(SHARD, ctx),
        P(None, ctx, SHARD),
    )
    out_specs = (
        P(None, ctx, SHARD),
        P(None, ctx, SHARD),
        P(),
        P(),
        P(),
        P(),
        P(ctx, SHARD),
        P(ctx, SHARD),
        P(ctx, SHARD),
        P(SHARD, ctx),
        P(ctx, SHARD),
        P(ctx, SHARD),
        P(SHARD, ctx),
    )
    return jax.shard_map(
        per_device, mesh=fine, in_specs=in_specs, out_specs=out_specs, check_vma=False
    )
```

```python
import math

import jax
import jax.numpy as jnp
from jax import lax
from jax.sharding import Mesh, PartitionSpec as P

HD = 64
BLK = 64


EPSILON = 1e-05
ROPE_BASE = 1000000.0


def wide_dot(left, right):
    return jnp.dot(left, right, preferred_element_type=jnp.float32)


def token_positions(block_pairs, row_index):
    owner = row_index // (2 * BLK)
    half = row_index // BLK % 2
    devices = jnp.arange(block_pairs.shape[0], dtype=jnp.int32)
    chosen = jnp.where(half[:, None] == 0, block_pairs[None, :, 0], block_pairs[None, :, 1])
    number = jnp.sum(jnp.where(owner[:, None] == devices[None, :], chosen, 0), axis=1)
    return number * BLK + row_index % BLK


def rope_tables(positions):
    index = jnp.arange(HD // 2, dtype=jnp.float32)
    inverse = jnp.exp(index * (-2.0 * math.log(ROPE_BASE) / HD))
    angle = positions.astype(jnp.float32)[:, None] * inverse[None, :]
    cosine = jnp.cos(angle)
    sine = jnp.sin(angle)
    return (
        jnp.concatenate([cosine, cosine], 1)[:, None, :],
        jnp.concatenate([sine, sine], 1)[:, None, :],
    )


def rotate_half(values):
    middle = values.shape[-1] // 2
    return jnp.concatenate([-values[..., middle:], values[..., :middle]], -1)


def head_norm(values):
    scale = lax.rsqrt(jnp.mean(values * values, axis=-1, keepdims=True) + EPSILON)
    return (scale, values * scale)


def head_back(grad_normed, unit, scale, gain):
    scaled = grad_normed * gain
    inner = jnp.mean(scaled * unit, axis=-1, keepdims=True)
    return scale * (scaled - unit * inner)


CTX_AXES = ("cx", "cy", "cz")
SHARD = ("sx", "sc")
EVERY = CTX_AXES + SHARD


GATHER_STAGES = (("cx",), ("cy", "cz"))
SCATTER_STAGES = tuple(reversed(GATHER_STAGES))
GATHERED_ORDER = tuple(name for stage in reversed(GATHER_STAGES) for name in stage)
SCATTER_ORDER = tuple(name for stage in SCATTER_STAGES for name in stage)


def ctx_gather(local, axis):
    for names in GATHER_STAGES:
        local = lax.all_gather(local, names, axis=axis, tiled=True)
    return local


def ctx_scatter(partial_value, axis, stages=SCATTER_STAGES):
    for names in stages:
        partial_value = lax.psum_scatter(partial_value, names, scatter_dimension=axis, tiled=True)
    return partial_value


def reorder_blocks(values, axis, source, target):
    sizes = [lax.axis_size(name) for name in source]
    shape = values.shape
    block = shape[axis] // math.prod(sizes)
    split = values.reshape(shape[:axis] + tuple(sizes) + (block,) + shape[axis + 1 :])
    order = list(range(axis)) + [axis + source.index(name) for name in target]
    order += list(range(axis + len(source), split.ndim))
    return jnp.transpose(split, order).reshape(shape)


def natural_row(index, rows):
    device = index // rows
    place = {}
    for name in reversed(GATHERED_ORDER):
        size = lax.axis_size(name)
        place[name] = device % size
        device = device // size
    natural = 0
    for name in CTX_AXES:
        natural = natural * lax.axis_size(name) + place[name]
    return natural * rows + index % rows


AXIS_STAGES = tuple((name,) for name in SCATTER_ORDER)


def start_sum_over_ctx(pieces, stages=SCATTER_STAGES):
    joined = jnp.concatenate(pieces, axis=1).astype(jnp.bfloat16)
    joined = reorder_blocks(joined, 0, CTX_AXES, SCATTER_ORDER)
    return ctx_scatter(joined, 0, stages[:1])


def finish_sum_over_ctx(partial_value, pieces, stages=SCATTER_STAGES):
    widths = [piece.shape[1] for piece in pieces]
    cuts = [sum(widths[:i]) for i in range(len(widths) + 1)]
    summed = ctx_scatter(partial_value, 0, stages[1:]).astype(jnp.float32)
    return [summed[:, cuts[i] : cuts[i + 1]] for i in range(len(pieces))]


def sum_over_ctx(pieces, stages=SCATTER_STAGES):
    return finish_sum_over_ctx(start_sum_over_ctx(pieces, stages), pieces, stages)


def rows_total(partial_value):
    return lax.psum(partial_value, SHARD)


def full_rows(local):
    return lax.all_gather(local, SHARD, axis=1, tiled=True)


def share_rows(partial_value):
    shards = lax.axis_size(SHARD)
    rows, cols = partial_value.shape
    blocks = partial_value.astype(jnp.bfloat16).reshape(rows, shards, cols // shards)
    blocks = lax.all_to_all(blocks, SHARD, 1, 1, tiled=True)
    return jnp.sum(blocks.astype(jnp.float32), axis=1)


def add_rows(partial_value):
    pieces = lax.all_gather(partial_value.astype(jnp.bfloat16), SHARD, axis=0)
    return jnp.sum(pieces.astype(jnp.float32), axis=0)


def local_norm(values):
    scale = lax.rsqrt(jnp.mean(values * values, axis=1, keepdims=True) + EPSILON)
    return (scale, values * scale)


def local_back(grad_normed, unit, scale, gain):
    scaled = grad_normed * gain
    inner = jnp.mean(scaled * unit, axis=1, keepdims=True)
    return scale * (scaled - unit * inner)


def row_norm(values, width):
    total = rows_total(jnp.sum(values * values, axis=1))
    scale = lax.rsqrt(total / width + EPSILON)[:, None]
    return (scale, values * scale)


def norm_back(grad_normed, unit, scale, gain, width):
    scaled = grad_normed * gain
    inner = rows_total(jnp.sum(scaled * unit, axis=1)) / width
    return (scale * (scaled - unit * inner[:, None]), jnp.sum(grad_normed * unit, axis=0))


def over_blocks(step_fn, carry, arrays):
    whole = arrays[0].shape[1]
    step = min(whole, 1024)

    def turn(index, state):
        start = index * step
        pieces = tuple((lax.dynamic_slice_in_dim(array, start, step, 1) for array in arrays))
        return step_fn(state, pieces, start)

    return lax.fori_loop(0, whole // step, turn, carry)


def per_device(
    block_in,
    block_pairs,
    attn_gain,
    query_gain,
    key_gain,
    ffn_gain,
    w_query,
    w_key,
    w_value,
    w_output,
    w_gate,
    w_up,
    w_down,
    grad_output,
):
    seqs, rows, local_width = block_in.shape
    flat = seqs * rows
    width = local_width * lax.axis_size(SHARD)
    offset = lax.axis_index(SHARD) * local_width
    pieces = (w_query, w_key, w_value, w_gate, w_up, w_output.T, w_down.T)
    widths = [piece.shape[1] for piece in pieces]
    cuts = [sum(widths[:i]) for i in range(len(widths) + 1)]
    every_weight = ctx_gather(jnp.concatenate(pieces, axis=1), 0)
    every_weight = reorder_blocks(every_weight, 0, GATHERED_ORDER, CTX_AXES)
    gathered = [every_weight[:, cuts[i] : cuts[i + 1]] for i in range(len(pieces))]
    query_all, key_all_w, value_all_w, gate_all, up_all, output_all, down_all = gathered
    output_all = output_all.T
    down_all = down_all.T
    heads = query_all.shape[1] // HD
    kv_heads = key_all_w.shape[1] // HD
    group = heads // kv_heads
    factor = 1.0 / math.sqrt(HD)
    pos_query = token_positions(
        block_pairs, lax.axis_index(CTX_AXES) * rows + jnp.arange(rows, dtype=jnp.int32)
    )
    cosine_one, sine_one = rope_tables(pos_query)
    cosine = jnp.tile(cosine_one, (seqs, 1, 1))
    sine = jnp.tile(sine_one, (seqs, 1, 1))
    attn_slice = lax.dynamic_slice_in_dim(attn_gain, offset, local_width)
    ffn_slice = lax.dynamic_slice_in_dim(ffn_gain, offset, local_width)
    input_all = full_rows(block_in.reshape(flat, local_width)).astype(jnp.float32)
    scale_attn, unit_attn = local_norm(input_all)
    normed_attn = (unit_attn * attn_gain).astype(jnp.bfloat16)
    query_raw = wide_dot(normed_attn, query_all).reshape(flat, heads, HD)
    key_raw = wide_dot(normed_attn, key_all_w).reshape(flat, kv_heads, HD)
    value_rows = (
        wide_dot(normed_attn, value_all_w).astype(jnp.bfloat16).reshape(seqs, rows, kv_heads * HD)
    )
    query_scale, query_unit = head_norm(query_raw)
    key_scale, key_unit = head_norm(key_raw)
    query_norm = query_unit * query_gain
    key_norm = key_unit * key_gain
    query_rot = (
        (query_norm * cosine + rotate_half(query_norm) * sine)
        .astype(jnp.bfloat16)
        .reshape(seqs, rows, kv_heads, group, HD)
    )
    key_rot = (
        (key_norm * cosine + rotate_half(key_norm) * sine)
        .astype(jnp.bfloat16)
        .reshape(seqs, rows, kv_heads * HD)
    )

    def scores_at(key_piece, start):
        count = key_piece.shape[1]
        pos_key = token_positions(
            block_pairs, natural_row(start + jnp.arange(count, dtype=jnp.int32), rows)
        )
        keys = key_piece.reshape(seqs, count, kv_heads, HD)
        score = (
            jnp.einsum("bqkgd,bskd->bkgqs", query_rot, keys, preferred_element_type=jnp.float32)
            * factor
        )
        mask = pos_key[None, None, None, None, :] <= pos_query[None, None, None, :, None]
        return (score, mask, keys)

    def attend(carry, pieces, start):
        key_piece, value_piece = pieces
        count = key_piece.shape[1]
        score, mask, keys = scores_at(key_piece, start)
        weights = jnp.where(mask, jnp.exp(score), 0.0)
        total, summed = carry
        values = value_piece.reshape(seqs, count, kv_heads, HD)
        summed = summed + jnp.einsum(
            "bkgqs,bskd->bqkgd",
            weights.astype(jnp.bfloat16),
            values,
            preferred_element_type=jnp.float32,
        )
        return (total + jnp.sum(weights, axis=-1), summed)

    start_carry = (
        jnp.zeros((seqs, kv_heads, group, rows), jnp.float32),
        jnp.zeros((seqs, rows, kv_heads, group, HD), jnp.float32),
    )
    key_value = ctx_gather(jnp.concatenate([key_rot, value_rows], axis=2), 1)
    key_every = key_value[:, :, : kv_heads * HD]
    value_every = key_value[:, :, kv_heads * HD :]
    total, summed = over_blocks(attend, start_carry, (key_every, value_every))
    log_total = jnp.log(total)
    attn_heads = (summed / jnp.transpose(total, (0, 3, 1, 2))[..., None]).astype(jnp.bfloat16)
    attn_out = attn_heads.reshape(flat, heads * HD)
    middle_all = input_all + add_rows(wide_dot(attn_out, output_all))
    middle = lax.dynamic_slice_in_dim(middle_all, offset, local_width, 1)
    scale_ffn, unit_ffn = local_norm(middle_all)
    normed_ffn = (unit_ffn * ffn_gain).astype(jnp.bfloat16)
    gate = wide_dot(normed_ffn, gate_all)
    up_proj = wide_dot(normed_ffn, up_all)
    sigmoid_gate = jax.nn.sigmoid(gate)
    activated = gate * sigmoid_gate
    mixed = (activated * up_proj).astype(jnp.bfloat16)
    block_out = (middle + share_rows(wide_dot(mixed, down_all))).astype(jnp.bfloat16)
    grad_flat = grad_output.reshape(flat, local_width)
    grad_full = full_rows(grad_flat)
    grad_mixed = wide_dot(grad_full, down_all.T)
    down_grad = wide_dot(mixed.T, grad_full)
    grad_gate = (grad_mixed * up_proj * sigmoid_gate * (1.0 + gate * (1.0 - sigmoid_gate))).astype(
        jnp.bfloat16
    )
    grad_up = (grad_mixed * activated).astype(jnp.bfloat16)
    gate_grad = wide_dot(normed_ffn.T, grad_gate)
    up_grad = wide_dot(normed_ffn.T, grad_up)
    ffn_pieces = (gate_grad, up_grad, down_grad.T)
    ffn_partial = start_sum_over_ctx(ffn_pieces)
    grad_normed_ffn = add_rows(wide_dot(grad_gate, gate_all.T) + wide_dot(grad_up, up_all.T))
    back_ffn = local_back(grad_normed_ffn, unit_ffn, scale_ffn, ffn_gain)
    ffn_part = lax.dynamic_slice_in_dim(jnp.sum(grad_normed_ffn * unit_ffn, axis=0), offset, local_width)
    grad_middle_full = grad_full.astype(jnp.float32) + back_ffn
    grad_middle_all = grad_middle_full.astype(jnp.bfloat16)
    grad_attn = wide_dot(grad_middle_all, output_all.T).reshape(seqs, rows, kv_heads, group, HD)
    output_grad = wide_dot(attn_out.T, grad_middle_all)
    delta = jnp.transpose(
        jnp.sum(grad_attn * attn_heads.astype(jnp.float32), axis=-1), (0, 2, 3, 1)
    )
    grad_attn_low = grad_attn.astype(jnp.bfloat16)

    def revisit(grad_query_sum, pieces, start):
        key_piece, value_piece = pieces
        count = key_piece.shape[1]
        score, mask, keys = scores_at(key_piece, start)
        values = value_piece.reshape(seqs, count, kv_heads, HD)
        prob = jnp.where(mask, jnp.exp(score - log_total[..., None]), 0.0)
        grad_prob = jnp.einsum(
            "bqkgd,bskd->bkgqs", grad_attn_low, values, preferred_element_type=jnp.float32
        )
        grad_score = (prob * (grad_prob - delta[..., None]) * factor).astype(jnp.bfloat16)
        grad_query_sum = grad_query_sum + jnp.einsum(
            "bkgqs,bskd->bqkgd", grad_score, keys, preferred_element_type=jnp.float32
        )
        key_term = jnp.einsum(
            "bkgqs,bqkgd->bskd", grad_score, query_rot, preferred_element_type=jnp.float32
        )
        value_term = jnp.einsum(
            "bkgqs,bqkgd->bskd",
            prob.astype(jnp.bfloat16),
            grad_attn_low,
            preferred_element_type=jnp.float32,
        )
        return (
            grad_query_sum,
            jnp.concatenate(
                [
                    key_term.reshape(seqs, count, kv_heads * HD),
                    value_term.reshape(seqs, count, kv_heads * HD),
                ],
                2,
            ),
        )

    whole = key_every.shape[1]
    step = min(whole, 1024)

    def back_turn(grad_query_sum, index):
        start = index * step
        pieces = (
            lax.dynamic_slice_in_dim(key_every, start, step, 1),
            lax.dynamic_slice_in_dim(value_every, start, step, 1),
        )
        return revisit(grad_query_sum, pieces, start)

    grad_query_rot, key_terms = lax.scan(
        back_turn,
        jnp.zeros((seqs, rows, kv_heads, group, HD), jnp.float32),
        jnp.arange(whole // step, dtype=jnp.int32),
    )
    key_terms = jnp.transpose(key_terms, (1, 0, 2, 3)).reshape(seqs, whole, 2 * kv_heads * HD)
    key_terms, ffn_partial = lax.optimization_barrier((key_terms, ffn_partial))
    ffn_summed = finish_sum_over_ctx(ffn_partial, ffn_pieces)
    owned = (
        ctx_scatter(key_terms.astype(jnp.bfloat16), 1, AXIS_STAGES)
        .astype(jnp.float32)
        .reshape(flat, 2 * kv_heads * HD)
    )
    grad_key_rot = owned[:, : kv_heads * HD].reshape(flat, kv_heads, HD)
    grad_value_low = owned[:, kv_heads * HD :].astype(jnp.bfloat16)
    grad_query_rot = grad_query_rot.reshape(flat, heads, HD)
    grad_query_unit = grad_query_rot * cosine - rotate_half(grad_query_rot * sine)
    grad_key_unit = grad_key_rot * cosine - rotate_half(grad_key_rot * sine)
    query_gain_part = jnp.sum(grad_query_unit * query_unit, axis=(0, 1))
    key_gain_part = jnp.sum(grad_key_unit * key_unit, axis=(0, 1))
    grad_query = (
        head_back(grad_query_unit, query_unit, query_scale, query_gain)
        .astype(jnp.bfloat16)
        .reshape(flat, heads * HD)
    )
    grad_key = (
        head_back(grad_key_unit, key_unit, key_scale, key_gain)
        .astype(jnp.bfloat16)
        .reshape(flat, kv_heads * HD)
    )
    query_grad = wide_dot(normed_attn.T, grad_query)
    key_grad = wide_dot(normed_attn.T, grad_key)
    value_grad = wide_dot(normed_attn.T, grad_value_low)
    grad_normed_attn = add_rows(
        wide_dot(grad_query, query_all.T)
        + wide_dot(grad_key, key_all_w.T)
        + wide_dot(grad_value_low, value_all_w.T)
    )
    back_attn = local_back(grad_normed_attn, unit_attn, scale_attn, attn_gain)
    attn_part = lax.dynamic_slice_in_dim(jnp.sum(grad_normed_attn * unit_attn, axis=0), offset, local_width)
    input_grad = lax.dynamic_slice_in_dim(grad_middle_full + back_attn, offset, local_width, 1)
    attn_pieces = (query_grad, key_grad, value_grad, output_grad.T)
    attn_pieces, grad_normed_attn = lax.optimization_barrier((attn_pieces, grad_normed_attn))
    query_grad, key_grad, value_grad, output_grad = sum_over_ctx(attn_pieces, AXIS_STAGES)
    gate_grad, up_grad, down_grad = ffn_summed
    output_grad = output_grad.T
    down_grad = down_grad.T
    attn_placed = lax.dynamic_update_slice_in_dim(
        jnp.zeros((width,), jnp.float32), attn_part, offset, 0
    )
    ffn_placed = lax.dynamic_update_slice_in_dim(
        jnp.zeros((width,), jnp.float32), ffn_part, offset, 0
    )
    gains = (attn_placed, query_gain_part, key_gain_part, ffn_placed)
    for names in (SHARD,) + tuple(reversed(CTX_AXES)):
        gains = lax.psum(gains, names)
    attn_gain_grad, query_gain_grad, key_gain_grad, ffn_gain_grad = gains
    block_out = block_out.reshape(seqs, rows, local_width)
    input_grad = input_grad.reshape(seqs, rows, local_width)
    return (
        block_out,
        input_grad,
        attn_gain_grad,
        query_gain_grad,
        key_gain_grad,
        ffn_gain_grad,
        query_grad,
        key_grad,
        value_grad,
        output_grad,
        gate_grad,
        up_grad,
        down_grad,
    )


def solution(mesh):
    ctx_size, shard_size = mesh.devices.shape
    fine = Mesh(mesh.devices.reshape(2, 4, ctx_size // 8, 2, shard_size // 2), EVERY)
    ctx = CTX_AXES
    in_specs = (
        P(None, ctx, SHARD),
        P(),
        P(),
        P(),
        P(),
        P(),
        P(ctx, SHARD),
        P(ctx, SHARD),
        P(ctx, SHARD),
        P(SHARD, ctx),
        P(ctx, SHARD),
        P(ctx, SHARD),
        P(SHARD, ctx),
        P(None, ctx, SHARD),
    )
    out_specs = (
        P(None, ctx, SHARD),
        P(None, ctx, SHARD),
        P(),
        P(),
        P(),
        P(),
        P(ctx, SHARD),
        P(ctx, SHARD),
        P(ctx, SHARD),
        P(SHARD, ctx),
        P(ctx, SHARD),
        P(ctx, SHARD),
        P(SHARD, ctx),
    )
    return jax.shard_map(
        per_device, mesh=fine, in_specs=in_specs, out_specs=out_specs, check_vma=False
    )
```

```python
import math

import jax
import jax.numpy as jnp
from jax import lax
from jax.sharding import Mesh, PartitionSpec as P

HD = 64
BLK = 64


EPSILON = 1e-05
ROPE_BASE = 1000000.0


def wide_dot(left, right):
    return jnp.dot(left, right, preferred_element_type=jnp.float32)


def token_positions(block_pairs, row_index):
    owner = row_index // (2 * BLK)
    half = row_index // BLK % 2
    devices = jnp.arange(block_pairs.shape[0], dtype=jnp.int32)
    chosen = jnp.where(half[:, None] == 0, block_pairs[None, :, 0], block_pairs[None, :, 1])
    number = jnp.sum(jnp.where(owner[:, None] == devices[None, :], chosen, 0), axis=1)
    return number * BLK + row_index % BLK


def rope_tables(positions):
    index = jnp.arange(HD // 2, dtype=jnp.float32)
    inverse = jnp.exp(index * (-2.0 * math.log(ROPE_BASE) / HD))
    angle = positions.astype(jnp.float32)[:, None] * inverse[None, :]
    cosine = jnp.cos(angle)
    sine = jnp.sin(angle)
    return (
        jnp.concatenate([cosine, cosine], 1)[:, None, :],
        jnp.concatenate([sine, sine], 1)[:, None, :],
    )


def rotate_half(values):
    middle = values.shape[-1] // 2
    return jnp.concatenate([-values[..., middle:], values[..., :middle]], -1)


def head_norm(values):
    scale = lax.rsqrt(jnp.mean(values * values, axis=-1, keepdims=True) + EPSILON)
    return (scale, values * scale)


def head_back(grad_normed, unit, scale, gain):
    scaled = grad_normed * gain
    inner = jnp.mean(scaled * unit, axis=-1, keepdims=True)
    return scale * (scaled - unit * inner)


CTX_AXES = ("cx", "cy", "cz")
SHARD = ("sx", "sc")
EVERY = CTX_AXES + SHARD


GATHER_STAGES = (("cx",), ("cy", "cz"))
SCATTER_STAGES = tuple(reversed(GATHER_STAGES))
GATHERED_ORDER = tuple(name for stage in reversed(GATHER_STAGES) for name in stage)
SCATTER_ORDER = tuple(name for stage in SCATTER_STAGES for name in stage)


def ctx_gather(local, axis):
    for names in GATHER_STAGES:
        local = lax.all_gather(local, names, axis=axis, tiled=True)
    return local


def pair_scatter(partial_value, axis, name):
    half = partial_value.shape[axis] // 2
    me = lax.axis_index(name)
    keep = lax.dynamic_slice_in_dim(partial_value, me * half, half, axis)
    send = lax.dynamic_slice_in_dim(partial_value, (1 - me) * half, half, axis)
    got = lax.ppermute(send, name, perm=[(0, 1), (1, 0)])
    return (keep.astype(jnp.float32) + got.astype(jnp.float32)).astype(partial_value.dtype)


def ctx_scatter(partial_value, axis, stages=SCATTER_STAGES):
    for names in stages:
        if len(names) == 1 and lax.axis_size(names[0]) == 2:
            partial_value = pair_scatter(partial_value, axis, names[0])
        else:
            partial_value = lax.psum_scatter(partial_value, names, scatter_dimension=axis, tiled=True)
    return partial_value


def reorder_blocks(values, axis, source, target):
    sizes = [lax.axis_size(name) for name in source]
    shape = values.shape
    block = shape[axis] // math.prod(sizes)
    split = values.reshape(shape[:axis] + tuple(sizes) + (block,) + shape[axis + 1 :])
    order = list(range(axis)) + [axis + source.index(name) for name in target]
    order += list(range(axis + len(source), split.ndim))
    return jnp.transpose(split, order).reshape(shape)


def natural_row(index, rows):
    device = index // rows
    place = {}
    for name in reversed(GATHERED_ORDER):
        size = lax.axis_size(name)
        place[name] = device % size
        device = device // size
    natural = 0
    for name in CTX_AXES:
        natural = natural * lax.axis_size(name) + place[name]
    return natural * rows + index % rows


AXIS_STAGES = tuple((name,) for name in SCATTER_ORDER)


def start_sum_over_ctx(pieces, stages=SCATTER_STAGES):
    joined = jnp.concatenate(pieces, axis=1).astype(jnp.bfloat16)
    joined = reorder_blocks(joined, 0, CTX_AXES, SCATTER_ORDER)
    return ctx_scatter(joined, 0, stages[:1])


def finish_sum_over_ctx(partial_value, pieces, stages=SCATTER_STAGES):
    widths = [piece.shape[1] for piece in pieces]
    cuts = [sum(widths[:i]) for i in range(len(widths) + 1)]
    summed = ctx_scatter(partial_value, 0, stages[1:]).astype(jnp.float32)
    return [summed[:, cuts[i] : cuts[i + 1]] for i in range(len(pieces))]


def sum_over_ctx(pieces, stages=SCATTER_STAGES):
    return finish_sum_over_ctx(start_sum_over_ctx(pieces, stages), pieces, stages)


def rows_total(partial_value):
    return lax.psum(partial_value, SHARD)


def full_rows(local):
    return lax.all_gather(local, SHARD, axis=1, tiled=True)


def share_rows(partial_value):
    shards = lax.axis_size(SHARD)
    rows, cols = partial_value.shape
    blocks = partial_value.astype(jnp.bfloat16).reshape(rows, shards, cols // shards)
    blocks = lax.all_to_all(blocks, SHARD, 1, 1, tiled=True)
    return jnp.sum(blocks.astype(jnp.float32), axis=1)


def add_rows(partial_value):
    pieces = lax.all_gather(partial_value.astype(jnp.bfloat16), SHARD, axis=0)
    return jnp.sum(pieces.astype(jnp.float32), axis=0)


def local_norm(values):
    scale = lax.rsqrt(jnp.mean(values * values, axis=1, keepdims=True) + EPSILON)
    return (scale, values * scale)


def local_back(grad_normed, unit, scale, gain):
    scaled = grad_normed * gain
    inner = jnp.mean(scaled * unit, axis=1, keepdims=True)
    return scale * (scaled - unit * inner)


def row_norm(values, width):
    total = rows_total(jnp.sum(values * values, axis=1))
    scale = lax.rsqrt(total / width + EPSILON)[:, None]
    return (scale, values * scale)


def norm_back(grad_normed, unit, scale, gain, width):
    scaled = grad_normed * gain
    inner = rows_total(jnp.sum(scaled * unit, axis=1)) / width
    return (scale * (scaled - unit * inner[:, None]), jnp.sum(grad_normed * unit, axis=0))


def over_blocks(step_fn, carry, arrays):
    whole = arrays[0].shape[1]
    step = min(whole, 1024)

    def turn(index, state):
        start = index * step
        pieces = tuple((lax.dynamic_slice_in_dim(array, start, step, 1) for array in arrays))
        return step_fn(state, pieces, start)

    return lax.fori_loop(0, whole // step, turn, carry)


def per_device(
    block_in,
    block_pairs,
    attn_gain,
    query_gain,
    key_gain,
    ffn_gain,
    w_query,
    w_key,
    w_value,
    w_output,
    w_gate,
    w_up,
    w_down,
    grad_output,
):
    seqs, rows, local_width = block_in.shape
    flat = seqs * rows
    width = local_width * lax.axis_size(SHARD)
    offset = lax.axis_index(SHARD) * local_width
    pieces = (w_query, w_key, w_value, w_gate, w_up, w_output.T, w_down.T)
    widths = [piece.shape[1] for piece in pieces]
    cuts = [sum(widths[:i]) for i in range(len(widths) + 1)]
    every_weight = ctx_gather(jnp.concatenate(pieces, axis=1), 0)
    every_weight = reorder_blocks(every_weight, 0, GATHERED_ORDER, CTX_AXES)
    gathered = [every_weight[:, cuts[i] : cuts[i + 1]] for i in range(len(pieces))]
    query_all, key_all_w, value_all_w, gate_all, up_all, output_all, down_all = gathered
    output_all = output_all.T
    down_all = down_all.T
    heads = query_all.shape[1] // HD
    kv_heads = key_all_w.shape[1] // HD
    group = heads // kv_heads
    factor = 1.0 / math.sqrt(HD)
    pos_query = token_positions(
        block_pairs, lax.axis_index(CTX_AXES) * rows + jnp.arange(rows, dtype=jnp.int32)
    )
    cosine_one, sine_one = rope_tables(pos_query)
    cosine = jnp.tile(cosine_one, (seqs, 1, 1))
    sine = jnp.tile(sine_one, (seqs, 1, 1))
    attn_slice = lax.dynamic_slice_in_dim(attn_gain, offset, local_width)
    ffn_slice = lax.dynamic_slice_in_dim(ffn_gain, offset, local_width)
    input_all = full_rows(block_in.reshape(flat, local_width)).astype(jnp.float32)
    scale_attn, unit_attn = local_norm(input_all)
    normed_attn = (unit_attn * attn_gain).astype(jnp.bfloat16)
    query_raw = wide_dot(normed_attn, query_all).reshape(flat, heads, HD)
    key_raw = wide_dot(normed_attn, key_all_w).reshape(flat, kv_heads, HD)
    value_rows = (
        wide_dot(normed_attn, value_all_w).astype(jnp.bfloat16).reshape(seqs, rows, kv_heads * HD)
    )
    query_scale, query_unit = head_norm(query_raw)
    key_scale, key_unit = head_norm(key_raw)
    query_norm = query_unit * query_gain
    key_norm = key_unit * key_gain
    query_rot = (
        (query_norm * cosine + rotate_half(query_norm) * sine)
        .astype(jnp.bfloat16)
        .reshape(seqs, rows, kv_heads, group, HD)
    )
    key_rot = (
        (key_norm * cosine + rotate_half(key_norm) * sine)
        .astype(jnp.bfloat16)
        .reshape(seqs, rows, kv_heads * HD)
    )

    def scores_at(key_piece, start):
        count = key_piece.shape[1]
        pos_key = token_positions(
            block_pairs, natural_row(start + jnp.arange(count, dtype=jnp.int32), rows)
        )
        keys = key_piece.reshape(seqs, count, kv_heads, HD)
        score = (
            jnp.einsum("bqkgd,bskd->bkgqs", query_rot, keys, preferred_element_type=jnp.float32)
            * factor
        )
        mask = pos_key[None, None, None, None, :] <= pos_query[None, None, None, :, None]
        return (score, mask, keys)

    def attend(carry, pieces, start):
        key_piece, value_piece = pieces
        count = key_piece.shape[1]
        score, mask, keys = scores_at(key_piece, start)
        weights = jnp.where(mask, jnp.exp(score), 0.0)
        total, summed = carry
        values = value_piece.reshape(seqs, count, kv_heads, HD)
        summed = summed + jnp.einsum(
            "bkgqs,bskd->bqkgd",
            weights.astype(jnp.bfloat16),
            values,
            preferred_element_type=jnp.float32,
        )
        return (total + jnp.sum(weights, axis=-1), summed)

    start_carry = (
        jnp.zeros((seqs, kv_heads, group, rows), jnp.float32),
        jnp.zeros((seqs, rows, kv_heads, group, HD), jnp.float32),
    )
    key_value = ctx_gather(jnp.concatenate([key_rot, value_rows], axis=2), 1)
    key_every = key_value[:, :, : kv_heads * HD]
    value_every = key_value[:, :, kv_heads * HD :]
    total, summed = over_blocks(attend, start_carry, (key_every, value_every))
    log_total = jnp.log(total)
    attn_heads = (summed / jnp.transpose(total, (0, 3, 1, 2))[..., None]).astype(jnp.bfloat16)
    attn_out = attn_heads.reshape(flat, heads * HD)
    middle_all = input_all + add_rows(wide_dot(attn_out, output_all))
    middle = lax.dynamic_slice_in_dim(middle_all, offset, local_width, 1)
    scale_ffn, unit_ffn = local_norm(middle_all)
    normed_ffn = (unit_ffn * ffn_gain).astype(jnp.bfloat16)
    gate = wide_dot(normed_ffn, gate_all)
    up_proj = wide_dot(normed_ffn, up_all)
    sigmoid_gate = jax.nn.sigmoid(gate)
    activated = gate * sigmoid_gate
    mixed = (activated * up_proj).astype(jnp.bfloat16)
    block_out = (middle + share_rows(wide_dot(mixed, down_all))).astype(jnp.bfloat16)
    grad_flat = grad_output.reshape(flat, local_width)
    grad_full = full_rows(grad_flat)
    grad_mixed = wide_dot(grad_full, down_all.T)
    down_grad = wide_dot(mixed.T, grad_full)
    grad_gate = (grad_mixed * up_proj * sigmoid_gate * (1.0 + gate * (1.0 - sigmoid_gate))).astype(
        jnp.bfloat16
    )
    grad_up = (grad_mixed * activated).astype(jnp.bfloat16)
    gate_grad = wide_dot(normed_ffn.T, grad_gate)
    up_grad = wide_dot(normed_ffn.T, grad_up)
    ffn_pieces = (gate_grad, up_grad, down_grad.T)
    ffn_partial = start_sum_over_ctx(ffn_pieces)
    grad_normed_ffn = add_rows(wide_dot(grad_gate, gate_all.T) + wide_dot(grad_up, up_all.T))
    back_ffn = local_back(grad_normed_ffn, unit_ffn, scale_ffn, ffn_gain)
    ffn_part = lax.dynamic_slice_in_dim(jnp.sum(grad_normed_ffn * unit_ffn, axis=0), offset, local_width)
    grad_middle_full = grad_full.astype(jnp.float32) + back_ffn
    grad_middle_all = grad_middle_full.astype(jnp.bfloat16)
    grad_attn = wide_dot(grad_middle_all, output_all.T).reshape(seqs, rows, kv_heads, group, HD)
    output_grad = wide_dot(attn_out.T, grad_middle_all)
    delta = jnp.transpose(
        jnp.sum(grad_attn * attn_heads.astype(jnp.float32), axis=-1), (0, 2, 3, 1)
    )
    grad_attn_low = grad_attn.astype(jnp.bfloat16)

    def revisit(grad_query_sum, pieces, start):
        key_piece, value_piece = pieces
        count = key_piece.shape[1]
        score, mask, keys = scores_at(key_piece, start)
        values = value_piece.reshape(seqs, count, kv_heads, HD)
        prob = jnp.where(mask, jnp.exp(score - log_total[..., None]), 0.0)
        grad_prob = jnp.einsum(
            "bqkgd,bskd->bkgqs", grad_attn_low, values, preferred_element_type=jnp.float32
        )
        grad_score = (prob * (grad_prob - delta[..., None]) * factor).astype(jnp.bfloat16)
        grad_query_sum = grad_query_sum + jnp.einsum(
            "bkgqs,bskd->bqkgd", grad_score, keys, preferred_element_type=jnp.float32
        )
        key_term = jnp.einsum(
            "bkgqs,bqkgd->bskd", grad_score, query_rot, preferred_element_type=jnp.float32
        )
        value_term = jnp.einsum(
            "bkgqs,bqkgd->bskd",
            prob.astype(jnp.bfloat16),
            grad_attn_low,
            preferred_element_type=jnp.float32,
        )
        return (
            grad_query_sum,
            jnp.concatenate(
                [
                    key_term.reshape(seqs, count, kv_heads * HD),
                    value_term.reshape(seqs, count, kv_heads * HD),
                ],
                2,
            ),
        )

    whole = key_every.shape[1]
    step = min(whole, 1024)

    def back_turn(grad_query_sum, index):
        start = index * step
        pieces = (
            lax.dynamic_slice_in_dim(key_every, start, step, 1),
            lax.dynamic_slice_in_dim(value_every, start, step, 1),
        )
        return revisit(grad_query_sum, pieces, start)

    grad_query_rot, key_terms = lax.scan(
        back_turn,
        jnp.zeros((seqs, rows, kv_heads, group, HD), jnp.float32),
        jnp.arange(whole // step, dtype=jnp.int32),
    )
    key_terms = jnp.transpose(key_terms, (1, 0, 2, 3)).reshape(seqs, whole, 2 * kv_heads * HD)
    key_terms, ffn_partial = lax.optimization_barrier((key_terms, ffn_partial))
    ffn_summed = finish_sum_over_ctx(ffn_partial, ffn_pieces)
    owned = (
        ctx_scatter(key_terms.astype(jnp.bfloat16), 1, AXIS_STAGES)
        .astype(jnp.float32)
        .reshape(flat, 2 * kv_heads * HD)
    )
    grad_key_rot = owned[:, : kv_heads * HD].reshape(flat, kv_heads, HD)
    grad_value_low = owned[:, kv_heads * HD :].astype(jnp.bfloat16)
    grad_query_rot = grad_query_rot.reshape(flat, heads, HD)
    grad_query_unit = grad_query_rot * cosine - rotate_half(grad_query_rot * sine)
    grad_key_unit = grad_key_rot * cosine - rotate_half(grad_key_rot * sine)
    query_gain_part = jnp.sum(grad_query_unit * query_unit, axis=(0, 1))
    key_gain_part = jnp.sum(grad_key_unit * key_unit, axis=(0, 1))
    grad_query = (
        head_back(grad_query_unit, query_unit, query_scale, query_gain)
        .astype(jnp.bfloat16)
        .reshape(flat, heads * HD)
    )
    grad_key = (
        head_back(grad_key_unit, key_unit, key_scale, key_gain)
        .astype(jnp.bfloat16)
        .reshape(flat, kv_heads * HD)
    )
    query_grad = wide_dot(normed_attn.T, grad_query)
    key_grad = wide_dot(normed_attn.T, grad_key)
    value_grad = wide_dot(normed_attn.T, grad_value_low)
    grad_normed_attn = add_rows(
        wide_dot(grad_query, query_all.T)
        + wide_dot(grad_key, key_all_w.T)
        + wide_dot(grad_value_low, value_all_w.T)
    )
    back_attn = local_back(grad_normed_attn, unit_attn, scale_attn, attn_gain)
    attn_part = lax.dynamic_slice_in_dim(jnp.sum(grad_normed_attn * unit_attn, axis=0), offset, local_width)
    input_grad = lax.dynamic_slice_in_dim(grad_middle_full + back_attn, offset, local_width, 1)
    attn_pieces = (query_grad, key_grad, value_grad, output_grad.T)
    attn_pieces, grad_normed_attn = lax.optimization_barrier((attn_pieces, grad_normed_attn))
    query_grad, key_grad, value_grad, output_grad = sum_over_ctx(attn_pieces, AXIS_STAGES)
    gate_grad, up_grad, down_grad = ffn_summed
    output_grad = output_grad.T
    down_grad = down_grad.T
    attn_placed = lax.dynamic_update_slice_in_dim(
        jnp.zeros((width,), jnp.float32), attn_part, offset, 0
    )
    ffn_placed = lax.dynamic_update_slice_in_dim(
        jnp.zeros((width,), jnp.float32), ffn_part, offset, 0
    )
    gains = (attn_placed, query_gain_part, key_gain_part, ffn_placed)
    for names in (SHARD,) + tuple(reversed(CTX_AXES)):
        gains = lax.psum(gains, names)
    attn_gain_grad, query_gain_grad, key_gain_grad, ffn_gain_grad = gains
    block_out = block_out.reshape(seqs, rows, local_width)
    input_grad = input_grad.reshape(seqs, rows, local_width)
    return (
        block_out,
        input_grad,
        attn_gain_grad,
        query_gain_grad,
        key_gain_grad,
        ffn_gain_grad,
        query_grad,
        key_grad,
        value_grad,
        output_grad,
        gate_grad,
        up_grad,
        down_grad,
    )


def solution(mesh):
    ctx_size, shard_size = mesh.devices.shape
    fine = Mesh(mesh.devices.reshape(2, 4, ctx_size // 8, 2, shard_size // 2), EVERY)
    ctx = CTX_AXES
    in_specs = (
        P(None, ctx, SHARD),
        P(),
        P(),
        P(),
        P(),
        P(),
        P(ctx, SHARD),
        P(ctx, SHARD),
        P(ctx, SHARD),
        P(SHARD, ctx),
        P(ctx, SHARD),
        P(ctx, SHARD),
        P(SHARD, ctx),
        P(None, ctx, SHARD),
    )
    out_specs = (
        P(None, ctx, SHARD),
        P(None, ctx, SHARD),
        P(),
        P(),
        P(),
        P(),
        P(ctx, SHARD),
        P(ctx, SHARD),
        P(ctx, SHARD),
        P(SHARD, ctx),
        P(ctx, SHARD),
        P(ctx, SHARD),
        P(SHARD, ctx),
    )
    return jax.shard_map(
        per_device, mesh=fine, in_specs=in_specs, out_specs=out_specs, check_vma=False
    )
```

```python
import math

import jax
import jax.numpy as jnp
from jax import lax
from jax.sharding import Mesh, PartitionSpec as P

HD = 64
BLK = 64


EPSILON = 1e-05
ROPE_BASE = 1000000.0


def wide_dot(left, right):
    return jnp.dot(left, right, preferred_element_type=jnp.float32)


def token_positions(block_pairs, row_index):
    owner = row_index // (2 * BLK)
    half = row_index // BLK % 2
    devices = jnp.arange(block_pairs.shape[0], dtype=jnp.int32)
    chosen = jnp.where(half[:, None] == 0, block_pairs[None, :, 0], block_pairs[None, :, 1])
    number = jnp.sum(jnp.where(owner[:, None] == devices[None, :], chosen, 0), axis=1)
    return number * BLK + row_index % BLK


def rope_tables(positions):
    index = jnp.arange(HD // 2, dtype=jnp.float32)
    inverse = jnp.exp(index * (-2.0 * math.log(ROPE_BASE) / HD))
    angle = positions.astype(jnp.float32)[:, None] * inverse[None, :]
    cosine = jnp.cos(angle)
    sine = jnp.sin(angle)
    return (
        jnp.concatenate([cosine, cosine], 1)[:, None, :],
        jnp.concatenate([sine, sine], 1)[:, None, :],
    )


def rotate_half(values):
    middle = values.shape[-1] // 2
    return jnp.concatenate([-values[..., middle:], values[..., :middle]], -1)


def head_norm(values):
    scale = lax.rsqrt(jnp.mean(values * values, axis=-1, keepdims=True) + EPSILON)
    return (scale, values * scale)


def head_back(grad_normed, unit, scale, gain):
    scaled = grad_normed * gain
    inner = jnp.mean(scaled * unit, axis=-1, keepdims=True)
    return scale * (scaled - unit * inner)


CTX_AXES = ("cx", "cy", "cz")
SHARD = ("sx", "sc")
EVERY = CTX_AXES + SHARD


GATHER_STAGES = (("cx",), ("cy", "cz"))
SCATTER_STAGES = tuple(reversed(GATHER_STAGES))
GATHERED_ORDER = tuple(name for stage in reversed(GATHER_STAGES) for name in stage)
SCATTER_ORDER = tuple(name for stage in SCATTER_STAGES for name in stage)


def ctx_gather(local, axis):
    for names in GATHER_STAGES:
        local = lax.all_gather(local, names, axis=axis, tiled=True)
    return local


def pair_scatter(partial_value, axis, name):
    half = partial_value.shape[axis] // 2
    me = lax.axis_index(name)
    keep = lax.dynamic_slice_in_dim(partial_value, me * half, half, axis)
    send = lax.dynamic_slice_in_dim(partial_value, (1 - me) * half, half, axis)
    got = lax.ppermute(send, name, perm=[(0, 1), (1, 0)])
    return (keep.astype(jnp.float32) + got.astype(jnp.float32)).astype(partial_value.dtype)


def ctx_scatter(partial_value, axis, stages=SCATTER_STAGES):
    for names in stages:
        if len(names) == 1 and lax.axis_size(names[0]) == 2:
            partial_value = pair_scatter(partial_value, axis, names[0])
        else:
            partial_value = lax.psum_scatter(partial_value, names, scatter_dimension=axis, tiled=True)
    return partial_value


def reorder_blocks(values, axis, source, target):
    sizes = [lax.axis_size(name) for name in source]
    shape = values.shape
    block = shape[axis] // math.prod(sizes)
    split = values.reshape(shape[:axis] + tuple(sizes) + (block,) + shape[axis + 1 :])
    order = list(range(axis)) + [axis + source.index(name) for name in target]
    order += list(range(axis + len(source), split.ndim))
    return jnp.transpose(split, order).reshape(shape)


def natural_row(index, rows):
    device = index // rows
    place = {}
    for name in reversed(GATHERED_ORDER):
        size = lax.axis_size(name)
        place[name] = device % size
        device = device // size
    natural = 0
    for name in CTX_AXES:
        natural = natural * lax.axis_size(name) + place[name]
    return natural * rows + index % rows


AXIS_STAGES = tuple((name,) for name in SCATTER_ORDER)


def start_sum_over_ctx(pieces, stages=SCATTER_STAGES[:1]):
    joined = jnp.concatenate(pieces, axis=1).astype(jnp.bfloat16)
    joined = reorder_blocks(joined, 0, CTX_AXES, SCATTER_ORDER)
    return ctx_scatter(joined, 0, stages)


def finish_sum_over_ctx(partial_value, pieces, stages=SCATTER_STAGES[1:]):
    widths = [piece.shape[1] for piece in pieces]
    cuts = [sum(widths[:i]) for i in range(len(widths) + 1)]
    summed = ctx_scatter(partial_value, 0, stages).astype(jnp.float32)
    return [summed[:, cuts[i] : cuts[i + 1]] for i in range(len(pieces))]


def sum_over_ctx(pieces, stages=SCATTER_STAGES):
    return finish_sum_over_ctx(start_sum_over_ctx(pieces, stages[:1]), pieces, stages[1:])


def rows_total(partial_value):
    return lax.psum(partial_value, SHARD)


def full_rows(local):
    return lax.all_gather(local, SHARD, axis=1, tiled=True)


def share_rows(partial_value):
    shards = lax.axis_size(SHARD)
    rows, cols = partial_value.shape
    blocks = partial_value.astype(jnp.bfloat16).reshape(rows, shards, cols // shards)
    blocks = lax.all_to_all(blocks, SHARD, 1, 1, tiled=True)
    return jnp.sum(blocks.astype(jnp.float32), axis=1)


def add_rows(partial_value):
    pieces = lax.all_gather(partial_value.astype(jnp.bfloat16), SHARD, axis=0)
    return jnp.sum(pieces.astype(jnp.float32), axis=0)


def local_norm(values):
    scale = lax.rsqrt(jnp.mean(values * values, axis=1, keepdims=True) + EPSILON)
    return (scale, values * scale)


def local_back(grad_normed, unit, scale, gain):
    scaled = grad_normed * gain
    inner = jnp.mean(scaled * unit, axis=1, keepdims=True)
    return scale * (scaled - unit * inner)


def row_norm(values, width):
    total = rows_total(jnp.sum(values * values, axis=1))
    scale = lax.rsqrt(total / width + EPSILON)[:, None]
    return (scale, values * scale)


def norm_back(grad_normed, unit, scale, gain, width):
    scaled = grad_normed * gain
    inner = rows_total(jnp.sum(scaled * unit, axis=1)) / width
    return (scale * (scaled - unit * inner[:, None]), jnp.sum(grad_normed * unit, axis=0))


def over_blocks(step_fn, carry, arrays):
    whole = arrays[0].shape[1]
    step = min(whole, 1024)

    def turn(index, state):
        start = index * step
        pieces = tuple((lax.dynamic_slice_in_dim(array, start, step, 1) for array in arrays))
        return step_fn(state, pieces, start)

    return lax.fori_loop(0, whole // step, turn, carry)


def per_device(
    block_in,
    block_pairs,
    attn_gain,
    query_gain,
    key_gain,
    ffn_gain,
    w_query,
    w_key,
    w_value,
    w_output,
    w_gate,
    w_up,
    w_down,
    grad_output,
):
    seqs, rows, local_width = block_in.shape
    flat = seqs * rows
    width = local_width * lax.axis_size(SHARD)
    offset = lax.axis_index(SHARD) * local_width
    pieces = (w_query, w_key, w_value, w_gate, w_up, w_output.T, w_down.T)
    widths = [piece.shape[1] for piece in pieces]
    cuts = [sum(widths[:i]) for i in range(len(widths) + 1)]
    every_weight = ctx_gather(jnp.concatenate(pieces, axis=1), 0)
    every_weight = reorder_blocks(every_weight, 0, GATHERED_ORDER, CTX_AXES)
    gathered = [every_weight[:, cuts[i] : cuts[i + 1]] for i in range(len(pieces))]
    query_all, key_all_w, value_all_w, gate_all, up_all, output_all, down_all = gathered
    output_all = output_all.T
    down_all = down_all.T
    heads = query_all.shape[1] // HD
    kv_heads = key_all_w.shape[1] // HD
    group = heads // kv_heads
    factor = 1.0 / math.sqrt(HD)
    pos_query = token_positions(
        block_pairs, lax.axis_index(CTX_AXES) * rows + jnp.arange(rows, dtype=jnp.int32)
    )
    cosine_one, sine_one = rope_tables(pos_query)
    cosine = jnp.tile(cosine_one, (seqs, 1, 1))
    sine = jnp.tile(sine_one, (seqs, 1, 1))
    attn_slice = lax.dynamic_slice_in_dim(attn_gain, offset, local_width)
    ffn_slice = lax.dynamic_slice_in_dim(ffn_gain, offset, local_width)
    input_all = full_rows(block_in.reshape(flat, local_width)).astype(jnp.float32)
    scale_attn, unit_attn = local_norm(input_all)
    normed_attn = (unit_attn * attn_gain).astype(jnp.bfloat16)
    query_raw = wide_dot(normed_attn, query_all).reshape(flat, heads, HD)
    key_raw = wide_dot(normed_attn, key_all_w).reshape(flat, kv_heads, HD)
    value_rows = (
        wide_dot(normed_attn, value_all_w).astype(jnp.bfloat16).reshape(seqs, rows, kv_heads * HD)
    )
    query_scale, query_unit = head_norm(query_raw)
    key_scale, key_unit = head_norm(key_raw)
    query_norm = query_unit * query_gain
    key_norm = key_unit * key_gain
    query_rot = (
        (query_norm * cosine + rotate_half(query_norm) * sine)
        .astype(jnp.bfloat16)
        .reshape(seqs, rows, kv_heads, group, HD)
    )
    key_rot = (
        (key_norm * cosine + rotate_half(key_norm) * sine)
        .astype(jnp.bfloat16)
        .reshape(seqs, rows, kv_heads * HD)
    )

    def scores_at(key_piece, start):
        count = key_piece.shape[1]
        pos_key = token_positions(
            block_pairs, natural_row(start + jnp.arange(count, dtype=jnp.int32), rows)
        )
        keys = key_piece.reshape(seqs, count, kv_heads, HD)
        score = (
            jnp.einsum("bqkgd,bskd->bkgqs", query_rot, keys, preferred_element_type=jnp.float32)
            * factor
        )
        mask = pos_key[None, None, None, None, :] <= pos_query[None, None, None, :, None]
        return (score, mask, keys)

    def attend(carry, pieces, start):
        key_piece, value_piece = pieces
        count = key_piece.shape[1]
        score, mask, keys = scores_at(key_piece, start)
        weights = jnp.where(mask, jnp.exp(score), 0.0)
        total, summed = carry
        values = value_piece.reshape(seqs, count, kv_heads, HD)
        summed = summed + jnp.einsum(
            "bkgqs,bskd->bqkgd",
            weights.astype(jnp.bfloat16),
            values,
            preferred_element_type=jnp.float32,
        )
        return (total + jnp.sum(weights, axis=-1), summed)

    start_carry = (
        jnp.zeros((seqs, kv_heads, group, rows), jnp.float32),
        jnp.zeros((seqs, rows, kv_heads, group, HD), jnp.float32),
    )
    key_value = ctx_gather(jnp.concatenate([key_rot, value_rows], axis=2), 1)
    key_every = key_value[:, :, : kv_heads * HD]
    value_every = key_value[:, :, kv_heads * HD :]
    total, summed = over_blocks(attend, start_carry, (key_every, value_every))
    log_total = jnp.log(total)
    attn_heads = (summed / jnp.transpose(total, (0, 3, 1, 2))[..., None]).astype(jnp.bfloat16)
    attn_out = attn_heads.reshape(flat, heads * HD)
    middle_all = input_all + add_rows(wide_dot(attn_out, output_all))
    middle = lax.dynamic_slice_in_dim(middle_all, offset, local_width, 1)
    scale_ffn, unit_ffn = local_norm(middle_all)
    normed_ffn = (unit_ffn * ffn_gain).astype(jnp.bfloat16)
    gate = wide_dot(normed_ffn, gate_all)
    up_proj = wide_dot(normed_ffn, up_all)
    sigmoid_gate = jax.nn.sigmoid(gate)
    activated = gate * sigmoid_gate
    mixed = (activated * up_proj).astype(jnp.bfloat16)
    block_out = (middle + share_rows(wide_dot(mixed, down_all))).astype(jnp.bfloat16)
    grad_flat = grad_output.reshape(flat, local_width)
    grad_full = full_rows(grad_flat)
    grad_mixed = wide_dot(grad_full, down_all.T)
    down_grad = wide_dot(mixed.T, grad_full)
    grad_gate = (grad_mixed * up_proj * sigmoid_gate * (1.0 + gate * (1.0 - sigmoid_gate))).astype(
        jnp.bfloat16
    )
    grad_up = (grad_mixed * activated).astype(jnp.bfloat16)
    gate_grad = wide_dot(normed_ffn.T, grad_gate)
    up_grad = wide_dot(normed_ffn.T, grad_up)
    ffn_pieces = (gate_grad, up_grad, down_grad.T)
    ffn_partial = start_sum_over_ctx(ffn_pieces)
    grad_normed_ffn = add_rows(wide_dot(grad_gate, gate_all.T) + wide_dot(grad_up, up_all.T))
    back_ffn = local_back(grad_normed_ffn, unit_ffn, scale_ffn, ffn_gain)
    ffn_part = lax.dynamic_slice_in_dim(jnp.sum(grad_normed_ffn * unit_ffn, axis=0), offset, local_width)
    grad_middle_full = grad_full.astype(jnp.float32) + back_ffn
    grad_middle_all = grad_middle_full.astype(jnp.bfloat16)
    grad_attn = wide_dot(grad_middle_all, output_all.T).reshape(seqs, rows, kv_heads, group, HD)
    output_grad = wide_dot(attn_out.T, grad_middle_all)
    delta = jnp.transpose(
        jnp.sum(grad_attn * attn_heads.astype(jnp.float32), axis=-1), (0, 2, 3, 1)
    )
    grad_attn_low = grad_attn.astype(jnp.bfloat16)

    def revisit(grad_query_sum, pieces, start):
        key_piece, value_piece = pieces
        count = key_piece.shape[1]
        score, mask, keys = scores_at(key_piece, start)
        values = value_piece.reshape(seqs, count, kv_heads, HD)
        prob = jnp.where(mask, jnp.exp(score - log_total[..., None]), 0.0)
        grad_prob = jnp.einsum(
            "bqkgd,bskd->bkgqs", grad_attn_low, values, preferred_element_type=jnp.float32
        )
        grad_score = (prob * (grad_prob - delta[..., None]) * factor).astype(jnp.bfloat16)
        grad_query_sum = grad_query_sum + jnp.einsum(
            "bkgqs,bskd->bqkgd", grad_score, keys, preferred_element_type=jnp.float32
        )
        key_term = jnp.einsum(
            "bkgqs,bqkgd->bskd", grad_score, query_rot, preferred_element_type=jnp.float32
        )
        value_term = jnp.einsum(
            "bkgqs,bqkgd->bskd",
            prob.astype(jnp.bfloat16),
            grad_attn_low,
            preferred_element_type=jnp.float32,
        )
        return (
            grad_query_sum,
            jnp.concatenate(
                [
                    key_term.reshape(seqs, count, kv_heads * HD),
                    value_term.reshape(seqs, count, kv_heads * HD),
                ],
                2,
            ),
        )

    whole = key_every.shape[1]
    step = min(whole, 1024)

    def back_turn(grad_query_sum, index):
        start = index * step
        pieces = (
            lax.dynamic_slice_in_dim(key_every, start, step, 1),
            lax.dynamic_slice_in_dim(value_every, start, step, 1),
        )
        return revisit(grad_query_sum, pieces, start)

    grad_query_rot, key_terms = lax.scan(
        back_turn,
        jnp.zeros((seqs, rows, kv_heads, group, HD), jnp.float32),
        jnp.arange(whole // step, dtype=jnp.int32),
    )
    key_terms = jnp.transpose(key_terms, (1, 0, 2, 3)).reshape(seqs, whole, 2 * kv_heads * HD)
    key_terms, ffn_partial = lax.optimization_barrier((key_terms, ffn_partial))
    ffn_summed = finish_sum_over_ctx(ffn_partial, ffn_pieces)
    owned = (
        ctx_scatter(key_terms.astype(jnp.bfloat16), 1, AXIS_STAGES)
        .astype(jnp.float32)
        .reshape(flat, 2 * kv_heads * HD)
    )
    grad_key_rot = owned[:, : kv_heads * HD].reshape(flat, kv_heads, HD)
    grad_value_low = owned[:, kv_heads * HD :].astype(jnp.bfloat16)
    grad_query_rot = grad_query_rot.reshape(flat, heads, HD)
    grad_query_unit = grad_query_rot * cosine - rotate_half(grad_query_rot * sine)
    grad_key_unit = grad_key_rot * cosine - rotate_half(grad_key_rot * sine)
    query_gain_part = jnp.sum(grad_query_unit * query_unit, axis=(0, 1))
    key_gain_part = jnp.sum(grad_key_unit * key_unit, axis=(0, 1))
    grad_query = (
        head_back(grad_query_unit, query_unit, query_scale, query_gain)
        .astype(jnp.bfloat16)
        .reshape(flat, heads * HD)
    )
    grad_key = (
        head_back(grad_key_unit, key_unit, key_scale, key_gain)
        .astype(jnp.bfloat16)
        .reshape(flat, kv_heads * HD)
    )
    query_grad = wide_dot(normed_attn.T, grad_query)
    key_grad = wide_dot(normed_attn.T, grad_key)
    value_grad = wide_dot(normed_attn.T, grad_value_low)
    grad_normed_attn = add_rows(
        wide_dot(grad_query, query_all.T)
        + wide_dot(grad_key, key_all_w.T)
        + wide_dot(grad_value_low, value_all_w.T)
    )
    back_attn = local_back(grad_normed_attn, unit_attn, scale_attn, attn_gain)
    attn_part = lax.dynamic_slice_in_dim(jnp.sum(grad_normed_attn * unit_attn, axis=0), offset, local_width)
    input_grad = lax.dynamic_slice_in_dim(grad_middle_full + back_attn, offset, local_width, 1)
    attn_pieces = (query_grad, key_grad, value_grad, output_grad.T)
    attn_pieces, grad_normed_attn = lax.optimization_barrier((attn_pieces, grad_normed_attn))
    attn_partial = start_sum_over_ctx(attn_pieces, AXIS_STAGES[:2])
    attn_placed = lax.dynamic_update_slice_in_dim(
        jnp.zeros((width,), jnp.float32), attn_part, offset, 0
    )
    ffn_placed = lax.dynamic_update_slice_in_dim(
        jnp.zeros((width,), jnp.float32), ffn_part, offset, 0
    )
    gains = (attn_placed, query_gain_part, key_gain_part, ffn_placed)
    for names in (SHARD,) + tuple(reversed(CTX_AXES)):
        gains = lax.psum(gains, names)
    attn_partial, gains = lax.optimization_barrier((attn_partial, gains))
    query_grad, key_grad, value_grad, output_grad = finish_sum_over_ctx(
        attn_partial, attn_pieces, AXIS_STAGES[2:]
    )
    gate_grad, up_grad, down_grad = ffn_summed
    output_grad = output_grad.T
    down_grad = down_grad.T
    attn_gain_grad, query_gain_grad, key_gain_grad, ffn_gain_grad = gains
    block_out = block_out.reshape(seqs, rows, local_width)
    input_grad = input_grad.reshape(seqs, rows, local_width)
    return (
        block_out,
        input_grad,
        attn_gain_grad,
        query_gain_grad,
        key_gain_grad,
        ffn_gain_grad,
        query_grad,
        key_grad,
        value_grad,
        output_grad,
        gate_grad,
        up_grad,
        down_grad,
    )


def solution(mesh):
    ctx_size, shard_size = mesh.devices.shape
    fine = Mesh(mesh.devices.reshape(2, 4, ctx_size // 8, 2, shard_size // 2), EVERY)
    ctx = CTX_AXES
    in_specs = (
        P(None, ctx, SHARD),
        P(),
        P(),
        P(),
        P(),
        P(),
        P(ctx, SHARD),
        P(ctx, SHARD),
        P(ctx, SHARD),
        P(SHARD, ctx),
        P(ctx, SHARD),
        P(ctx, SHARD),
        P(SHARD, ctx),
        P(None, ctx, SHARD),
    )
    out_specs = (
        P(None, ctx, SHARD),
        P(None, ctx, SHARD),
        P(),
        P(),
        P(),
        P(),
        P(ctx, SHARD),
        P(ctx, SHARD),
        P(ctx, SHARD),
        P(SHARD, ctx),
        P(ctx, SHARD),
        P(ctx, SHARD),
        P(SHARD, ctx),
    )
    return jax.shard_map(
        per_device, mesh=fine, in_specs=in_specs, out_specs=out_specs, check_vma=False
    )
```

```python
import math

import jax
import jax.numpy as jnp
from jax import lax
from jax.sharding import Mesh, PartitionSpec as P

HD = 64
BLK = 64


EPSILON = 1e-05
ROPE_BASE = 1000000.0


def wide_dot(left, right):
    return jnp.dot(left, right, preferred_element_type=jnp.float32)


def token_positions(block_pairs, row_index):
    owner = row_index // (2 * BLK)
    half = row_index // BLK % 2
    devices = jnp.arange(block_pairs.shape[0], dtype=jnp.int32)
    chosen = jnp.where(half[:, None] == 0, block_pairs[None, :, 0], block_pairs[None, :, 1])
    number = jnp.sum(jnp.where(owner[:, None] == devices[None, :], chosen, 0), axis=1)
    return number * BLK + row_index % BLK


def rope_tables(positions):
    index = jnp.arange(HD // 2, dtype=jnp.float32)
    inverse = jnp.exp(index * (-2.0 * math.log(ROPE_BASE) / HD))
    angle = positions.astype(jnp.float32)[:, None] * inverse[None, :]
    cosine = jnp.cos(angle)
    sine = jnp.sin(angle)
    return (
        jnp.concatenate([cosine, cosine], 1)[:, None, :],
        jnp.concatenate([sine, sine], 1)[:, None, :],
    )


def rotate_half(values):
    middle = values.shape[-1] // 2
    return jnp.concatenate([-values[..., middle:], values[..., :middle]], -1)


def head_norm(values):
    scale = lax.rsqrt(jnp.mean(values * values, axis=-1, keepdims=True) + EPSILON)
    return (scale, values * scale)


def head_back(grad_normed, unit, scale, gain):
    scaled = grad_normed * gain
    inner = jnp.mean(scaled * unit, axis=-1, keepdims=True)
    return scale * (scaled - unit * inner)


CTX_AXES = ("cx", "cy", "cz")
SHARD = ("sx", "sc")
EVERY = CTX_AXES + SHARD


GATHER_STAGES = (("cx",), ("cy", "cz"))
SCATTER_STAGES = tuple(reversed(GATHER_STAGES))
GATHERED_ORDER = tuple(name for stage in reversed(GATHER_STAGES) for name in stage)
SCATTER_ORDER = tuple(name for stage in SCATTER_STAGES for name in stage)


def ctx_gather(local, axis):
    for names in GATHER_STAGES:
        local = lax.all_gather(local, names, axis=axis, tiled=True)
    return local


def pair_scatter(partial_value, axis, name):
    half = partial_value.shape[axis] // 2
    me = lax.axis_index(name)
    keep = lax.dynamic_slice_in_dim(partial_value, me * half, half, axis)
    send = lax.dynamic_slice_in_dim(partial_value, (1 - me) * half, half, axis)
    got = lax.ppermute(send, name, perm=[(0, 1), (1, 0)])
    return (keep.astype(jnp.float32) + got.astype(jnp.float32)).astype(partial_value.dtype)


def ctx_scatter(partial_value, axis, stages=SCATTER_STAGES):
    for names in stages:
        if len(names) == 1 and lax.axis_size(names[0]) == 2:
            partial_value = pair_scatter(partial_value, axis, names[0])
        else:
            partial_value = lax.psum_scatter(partial_value, names, scatter_dimension=axis, tiled=True)
    return partial_value


def reorder_blocks(values, axis, source, target):
    sizes = [lax.axis_size(name) for name in source]
    shape = values.shape
    block = shape[axis] // math.prod(sizes)
    split = values.reshape(shape[:axis] + tuple(sizes) + (block,) + shape[axis + 1 :])
    order = list(range(axis)) + [axis + source.index(name) for name in target]
    order += list(range(axis + len(source), split.ndim))
    return jnp.transpose(split, order).reshape(shape)


def natural_row(index, rows):
    device = index // rows
    place = {}
    for name in reversed(GATHERED_ORDER):
        size = lax.axis_size(name)
        place[name] = device % size
        device = device // size
    natural = 0
    for name in CTX_AXES:
        natural = natural * lax.axis_size(name) + place[name]
    return natural * rows + index % rows


AXIS_STAGES = tuple((name,) for name in SCATTER_ORDER)


def start_sum_over_ctx(pieces, stages=SCATTER_STAGES[:1]):
    joined = jnp.concatenate(pieces, axis=1).astype(jnp.bfloat16)
    joined = reorder_blocks(joined, 0, CTX_AXES, SCATTER_ORDER)
    return ctx_scatter(joined, 0, stages)


def finish_sum_over_ctx(partial_value, pieces, stages=SCATTER_STAGES[1:]):
    widths = [piece.shape[1] for piece in pieces]
    cuts = [sum(widths[:i]) for i in range(len(widths) + 1)]
    summed = ctx_scatter(partial_value, 0, stages).astype(jnp.float32)
    return [summed[:, cuts[i] : cuts[i + 1]] for i in range(len(pieces))]


def sum_over_ctx(pieces, stages=SCATTER_STAGES):
    return finish_sum_over_ctx(start_sum_over_ctx(pieces, stages[:1]), pieces, stages[1:])


def rows_total(partial_value):
    return lax.psum(partial_value, SHARD)


def full_rows(local):
    return lax.all_gather(local, SHARD, axis=1, tiled=True)


def share_rows(partial_value):
    shards = lax.axis_size(SHARD)
    rows, cols = partial_value.shape
    blocks = partial_value.astype(jnp.bfloat16).reshape(rows, shards, cols // shards)
    blocks = lax.all_to_all(blocks, SHARD, 1, 1, tiled=True)
    return jnp.sum(blocks.astype(jnp.float32), axis=1)


def add_rows(partial_value):
    pieces = lax.all_gather(partial_value.astype(jnp.bfloat16), SHARD, axis=0)
    return jnp.sum(pieces.astype(jnp.float32), axis=0)


def add_rows_direct(partial_value):
    owned = share_rows(partial_value)
    shards = lax.axis_size(SHARD)
    copies = jnp.broadcast_to(owned[None], (shards,) + owned.shape)
    blocks = lax.all_to_all(copies, SHARD, 0, 0, tiled=True)
    return jnp.transpose(blocks, (1, 0, 2)).reshape(owned.shape[0], shards * owned.shape[1])


def local_norm(values):
    scale = lax.rsqrt(jnp.mean(values * values, axis=1, keepdims=True) + EPSILON)
    return (scale, values * scale)


def local_back(grad_normed, unit, scale, gain):
    scaled = grad_normed * gain
    inner = jnp.mean(scaled * unit, axis=1, keepdims=True)
    return scale * (scaled - unit * inner)


def row_norm(values, width):
    total = rows_total(jnp.sum(values * values, axis=1))
    scale = lax.rsqrt(total / width + EPSILON)[:, None]
    return (scale, values * scale)


def norm_back(grad_normed, unit, scale, gain, width):
    scaled = grad_normed * gain
    inner = rows_total(jnp.sum(scaled * unit, axis=1)) / width
    return (scale * (scaled - unit * inner[:, None]), jnp.sum(grad_normed * unit, axis=0))


def over_blocks(step_fn, carry, arrays):
    whole = arrays[0].shape[1]
    step = min(whole, 1024)

    def turn(index, state):
        start = index * step
        pieces = tuple((lax.dynamic_slice_in_dim(array, start, step, 1) for array in arrays))
        return step_fn(state, pieces, start)

    return lax.fori_loop(0, whole // step, turn, carry)


def per_device(
    block_in,
    block_pairs,
    attn_gain,
    query_gain,
    key_gain,
    ffn_gain,
    w_query,
    w_key,
    w_value,
    w_output,
    w_gate,
    w_up,
    w_down,
    grad_output,
):
    seqs, rows, local_width = block_in.shape
    flat = seqs * rows
    width = local_width * lax.axis_size(SHARD)
    offset = lax.axis_index(SHARD) * local_width
    pieces = (w_query, w_key, w_value, w_gate, w_up, w_output.T, w_down.T)
    widths = [piece.shape[1] for piece in pieces]
    cuts = [sum(widths[:i]) for i in range(len(widths) + 1)]
    every_weight = ctx_gather(jnp.concatenate(pieces, axis=1), 0)
    every_weight = reorder_blocks(every_weight, 0, GATHERED_ORDER, CTX_AXES)
    gathered = [every_weight[:, cuts[i] : cuts[i + 1]] for i in range(len(pieces))]
    query_all, key_all_w, value_all_w, gate_all, up_all, output_all, down_all = gathered
    output_all = output_all.T
    down_all = down_all.T
    heads = query_all.shape[1] // HD
    kv_heads = key_all_w.shape[1] // HD
    group = heads // kv_heads
    factor = 1.0 / math.sqrt(HD)
    pos_query = token_positions(
        block_pairs, lax.axis_index(CTX_AXES) * rows + jnp.arange(rows, dtype=jnp.int32)
    )
    cosine_one, sine_one = rope_tables(pos_query)
    cosine = jnp.tile(cosine_one, (seqs, 1, 1))
    sine = jnp.tile(sine_one, (seqs, 1, 1))
    attn_slice = lax.dynamic_slice_in_dim(attn_gain, offset, local_width)
    ffn_slice = lax.dynamic_slice_in_dim(ffn_gain, offset, local_width)
    input_all = full_rows(block_in.reshape(flat, local_width)).astype(jnp.float32)
    scale_attn, unit_attn = local_norm(input_all)
    normed_attn = (unit_attn * attn_gain).astype(jnp.bfloat16)
    query_raw = wide_dot(normed_attn, query_all).reshape(flat, heads, HD)
    key_raw = wide_dot(normed_attn, key_all_w).reshape(flat, kv_heads, HD)
    value_rows = (
        wide_dot(normed_attn, value_all_w).astype(jnp.bfloat16).reshape(seqs, rows, kv_heads * HD)
    )
    query_scale, query_unit = head_norm(query_raw)
    key_scale, key_unit = head_norm(key_raw)
    query_norm = query_unit * query_gain
    key_norm = key_unit * key_gain
    query_rot = (
        (query_norm * cosine + rotate_half(query_norm) * sine)
        .astype(jnp.bfloat16)
        .reshape(seqs, rows, kv_heads, group, HD)
    )
    key_rot = (
        (key_norm * cosine + rotate_half(key_norm) * sine)
        .astype(jnp.bfloat16)
        .reshape(seqs, rows, kv_heads * HD)
    )

    def scores_at(key_piece, start):
        count = key_piece.shape[1]
        pos_key = token_positions(
            block_pairs, natural_row(start + jnp.arange(count, dtype=jnp.int32), rows)
        )
        keys = key_piece.reshape(seqs, count, kv_heads, HD)
        score = (
            jnp.einsum("bqkgd,bskd->bkgqs", query_rot, keys, preferred_element_type=jnp.float32)
            * factor
        )
        mask = pos_key[None, None, None, None, :] <= pos_query[None, None, None, :, None]
        return (score, mask, keys)

    def attend(carry, pieces, start):
        key_piece, value_piece = pieces
        count = key_piece.shape[1]
        score, mask, keys = scores_at(key_piece, start)
        weights = jnp.where(mask, jnp.exp(score), 0.0)
        total, summed = carry
        values = value_piece.reshape(seqs, count, kv_heads, HD)
        summed = summed + jnp.einsum(
            "bkgqs,bskd->bqkgd",
            weights.astype(jnp.bfloat16),
            values,
            preferred_element_type=jnp.float32,
        )
        return (total + jnp.sum(weights, axis=-1), summed)

    start_carry = (
        jnp.zeros((seqs, kv_heads, group, rows), jnp.float32),
        jnp.zeros((seqs, rows, kv_heads, group, HD), jnp.float32),
    )
    key_value = ctx_gather(jnp.concatenate([key_rot, value_rows], axis=2), 1)
    key_every = key_value[:, :, : kv_heads * HD]
    value_every = key_value[:, :, kv_heads * HD :]
    total, summed = over_blocks(attend, start_carry, (key_every, value_every))
    log_total = jnp.log(total)
    attn_heads = (summed / jnp.transpose(total, (0, 3, 1, 2))[..., None]).astype(jnp.bfloat16)
    attn_out = attn_heads.reshape(flat, heads * HD)
    middle_all = input_all + add_rows(wide_dot(attn_out, output_all))
    middle = lax.dynamic_slice_in_dim(middle_all, offset, local_width, 1)
    scale_ffn, unit_ffn = local_norm(middle_all)
    normed_ffn = (unit_ffn * ffn_gain).astype(jnp.bfloat16)
    gate = wide_dot(normed_ffn, gate_all)
    up_proj = wide_dot(normed_ffn, up_all)
    sigmoid_gate = jax.nn.sigmoid(gate)
    activated = gate * sigmoid_gate
    mixed = (activated * up_proj).astype(jnp.bfloat16)
    block_out = (middle + share_rows(wide_dot(mixed, down_all))).astype(jnp.bfloat16)
    grad_flat = grad_output.reshape(flat, local_width)
    grad_full = full_rows(grad_flat)
    grad_mixed = wide_dot(grad_full, down_all.T)
    down_grad = wide_dot(mixed.T, grad_full)
    grad_gate = (grad_mixed * up_proj * sigmoid_gate * (1.0 + gate * (1.0 - sigmoid_gate))).astype(
        jnp.bfloat16
    )
    grad_up = (grad_mixed * activated).astype(jnp.bfloat16)
    gate_grad = wide_dot(normed_ffn.T, grad_gate)
    up_grad = wide_dot(normed_ffn.T, grad_up)
    ffn_pieces = (gate_grad, up_grad, down_grad.T)
    ffn_partial = start_sum_over_ctx(ffn_pieces)
    grad_normed_ffn = add_rows(wide_dot(grad_gate, gate_all.T) + wide_dot(grad_up, up_all.T))
    back_ffn = local_back(grad_normed_ffn, unit_ffn, scale_ffn, ffn_gain)
    ffn_part = lax.dynamic_slice_in_dim(jnp.sum(grad_normed_ffn * unit_ffn, axis=0), offset, local_width)
    grad_middle_full = grad_full.astype(jnp.float32) + back_ffn
    grad_middle_all = grad_middle_full.astype(jnp.bfloat16)
    grad_attn = wide_dot(grad_middle_all, output_all.T).reshape(seqs, rows, kv_heads, group, HD)
    output_grad = wide_dot(attn_out.T, grad_middle_all)
    delta = jnp.transpose(
        jnp.sum(grad_attn * attn_heads.astype(jnp.float32), axis=-1), (0, 2, 3, 1)
    )
    grad_attn_low = grad_attn.astype(jnp.bfloat16)

    def revisit(grad_query_sum, pieces, start):
        key_piece, value_piece = pieces
        count = key_piece.shape[1]
        score, mask, keys = scores_at(key_piece, start)
        values = value_piece.reshape(seqs, count, kv_heads, HD)
        prob = jnp.where(mask, jnp.exp(score - log_total[..., None]), 0.0)
        grad_prob = jnp.einsum(
            "bqkgd,bskd->bkgqs", grad_attn_low, values, preferred_element_type=jnp.float32
        )
        grad_score = (prob * (grad_prob - delta[..., None]) * factor).astype(jnp.bfloat16)
        grad_query_sum = grad_query_sum + jnp.einsum(
            "bkgqs,bskd->bqkgd", grad_score, keys, preferred_element_type=jnp.float32
        )
        key_term = jnp.einsum(
            "bkgqs,bqkgd->bskd", grad_score, query_rot, preferred_element_type=jnp.float32
        )
        value_term = jnp.einsum(
            "bkgqs,bqkgd->bskd",
            prob.astype(jnp.bfloat16),
            grad_attn_low,
            preferred_element_type=jnp.float32,
        )
        return (
            grad_query_sum,
            jnp.concatenate(
                [
                    key_term.reshape(seqs, count, kv_heads * HD),
                    value_term.reshape(seqs, count, kv_heads * HD),
                ],
                2,
            ),
        )

    whole = key_every.shape[1]
    step = min(whole, 1024)

    def back_turn(grad_query_sum, index):
        start = index * step
        pieces = (
            lax.dynamic_slice_in_dim(key_every, start, step, 1),
            lax.dynamic_slice_in_dim(value_every, start, step, 1),
        )
        return revisit(grad_query_sum, pieces, start)

    grad_query_rot, key_terms = lax.scan(
        back_turn,
        jnp.zeros((seqs, rows, kv_heads, group, HD), jnp.float32),
        jnp.arange(whole // step, dtype=jnp.int32),
    )
    key_terms = jnp.transpose(key_terms, (1, 0, 2, 3)).reshape(seqs, whole, 2 * kv_heads * HD)
    key_terms, ffn_partial = lax.optimization_barrier((key_terms, ffn_partial))
    ffn_summed = finish_sum_over_ctx(ffn_partial, ffn_pieces)
    owned = (
        ctx_scatter(key_terms.astype(jnp.bfloat16), 1, AXIS_STAGES)
        .astype(jnp.float32)
        .reshape(flat, 2 * kv_heads * HD)
    )
    grad_key_rot = owned[:, : kv_heads * HD].reshape(flat, kv_heads, HD)
    grad_value_low = owned[:, kv_heads * HD :].astype(jnp.bfloat16)
    grad_query_rot = grad_query_rot.reshape(flat, heads, HD)
    grad_query_unit = grad_query_rot * cosine - rotate_half(grad_query_rot * sine)
    grad_key_unit = grad_key_rot * cosine - rotate_half(grad_key_rot * sine)
    query_gain_part = jnp.sum(grad_query_unit * query_unit, axis=(0, 1))
    key_gain_part = jnp.sum(grad_key_unit * key_unit, axis=(0, 1))
    grad_query = (
        head_back(grad_query_unit, query_unit, query_scale, query_gain)
        .astype(jnp.bfloat16)
        .reshape(flat, heads * HD)
    )
    grad_key = (
        head_back(grad_key_unit, key_unit, key_scale, key_gain)
        .astype(jnp.bfloat16)
        .reshape(flat, kv_heads * HD)
    )
    query_grad = wide_dot(normed_attn.T, grad_query)
    key_grad = wide_dot(normed_attn.T, grad_key)
    value_grad = wide_dot(normed_attn.T, grad_value_low)
    grad_normed_attn = add_rows_direct(
        wide_dot(grad_query, query_all.T)
        + wide_dot(grad_key, key_all_w.T)
        + wide_dot(grad_value_low, value_all_w.T)
    )
    back_attn = local_back(grad_normed_attn, unit_attn, scale_attn, attn_gain)
    attn_part = lax.dynamic_slice_in_dim(jnp.sum(grad_normed_attn * unit_attn, axis=0), offset, local_width)
    input_grad = lax.dynamic_slice_in_dim(grad_middle_full + back_attn, offset, local_width, 1)
    attn_pieces = (query_grad, key_grad, value_grad, output_grad.T)
    attn_partial = start_sum_over_ctx(attn_pieces, AXIS_STAGES[:2])
    attn_placed = lax.dynamic_update_slice_in_dim(
        jnp.zeros((width,), jnp.float32), attn_part, offset, 0
    )
    ffn_placed = lax.dynamic_update_slice_in_dim(
        jnp.zeros((width,), jnp.float32), ffn_part, offset, 0
    )
    gains = (attn_placed, query_gain_part, key_gain_part, ffn_placed)
    for names in (SHARD,) + tuple(reversed(CTX_AXES)):
        gains = lax.psum(gains, names)
    attn_partial, gains = lax.optimization_barrier((attn_partial, gains))
    query_grad, key_grad, value_grad, output_grad = finish_sum_over_ctx(
        attn_partial, attn_pieces, AXIS_STAGES[2:]
    )
    gate_grad, up_grad, down_grad = ffn_summed
    output_grad = output_grad.T
    down_grad = down_grad.T
    attn_gain_grad, query_gain_grad, key_gain_grad, ffn_gain_grad = gains
    block_out = block_out.reshape(seqs, rows, local_width)
    input_grad = input_grad.reshape(seqs, rows, local_width)
    return (
        block_out,
        input_grad,
        attn_gain_grad,
        query_gain_grad,
        key_gain_grad,
        ffn_gain_grad,
        query_grad,
        key_grad,
        value_grad,
        output_grad,
        gate_grad,
        up_grad,
        down_grad,
    )


def solution(mesh):
    ctx_size, shard_size = mesh.devices.shape
    fine = Mesh(mesh.devices.reshape(2, 4, ctx_size // 8, 2, shard_size // 2), EVERY)
    ctx = CTX_AXES
    in_specs = (
        P(None, ctx, SHARD),
        P(),
        P(),
        P(),
        P(),
        P(),
        P(ctx, SHARD),
        P(ctx, SHARD),
        P(ctx, SHARD),
        P(SHARD, ctx),
        P(ctx, SHARD),
        P(ctx, SHARD),
        P(SHARD, ctx),
        P(None, ctx, SHARD),
    )
    out_specs = (
        P(None, ctx, SHARD),
        P(None, ctx, SHARD),
        P(),
        P(),
        P(),
        P(),
        P(ctx, SHARD),
        P(ctx, SHARD),
        P(ctx, SHARD),
        P(SHARD, ctx),
        P(ctx, SHARD),
        P(ctx, SHARD),
        P(SHARD, ctx),
    )
    return jax.shard_map(
        per_device, mesh=fine, in_specs=in_specs, out_specs=out_specs, check_vma=False
    )
```

```python
import math

import jax
import jax.numpy as jnp
from jax import lax
from jax.sharding import Mesh, PartitionSpec as P

HD = 64
BLK = 64


EPSILON = 1e-05
ROPE_BASE = 1000000.0


def wide_dot(left, right):
    return jnp.dot(left, right, preferred_element_type=jnp.float32)


def token_positions(block_pairs, row_index):
    owner = row_index // (2 * BLK)
    half = row_index // BLK % 2
    devices = jnp.arange(block_pairs.shape[0], dtype=jnp.int32)
    chosen = jnp.where(half[:, None] == 0, block_pairs[None, :, 0], block_pairs[None, :, 1])
    number = jnp.sum(jnp.where(owner[:, None] == devices[None, :], chosen, 0), axis=1)
    return number * BLK + row_index % BLK


def rope_tables(positions):
    index = jnp.arange(HD // 2, dtype=jnp.float32)
    inverse = jnp.exp(index * (-2.0 * math.log(ROPE_BASE) / HD))
    angle = positions.astype(jnp.float32)[:, None] * inverse[None, :]
    cosine = jnp.cos(angle)
    sine = jnp.sin(angle)
    return (
        jnp.concatenate([cosine, cosine], 1)[:, None, :],
        jnp.concatenate([sine, sine], 1)[:, None, :],
    )


def rotate_half(values):
    middle = values.shape[-1] // 2
    return jnp.concatenate([-values[..., middle:], values[..., :middle]], -1)


def head_norm(values):
    scale = lax.rsqrt(jnp.mean(values * values, axis=-1, keepdims=True) + EPSILON)
    return (scale, values * scale)


def head_back(grad_normed, unit, scale, gain):
    scaled = grad_normed * gain
    inner = jnp.mean(scaled * unit, axis=-1, keepdims=True)
    return scale * (scaled - unit * inner)


CTX_AXES = ("cx", "cy", "cz")
SHARD = ("sx", "sc")
EVERY = CTX_AXES + SHARD


GATHER_STAGES = (("cx",), ("cy", "cz"))
SCATTER_STAGES = tuple(reversed(GATHER_STAGES))
GATHERED_ORDER = tuple(name for stage in reversed(GATHER_STAGES) for name in stage)
SCATTER_ORDER = tuple(name for stage in SCATTER_STAGES for name in stage)


def ctx_gather(local, axis):
    for names in GATHER_STAGES:
        local = lax.all_gather(local, names, axis=axis, tiled=True)
    return local


def pair_scatter(partial_value, axis, name):
    half = partial_value.shape[axis] // 2
    me = lax.axis_index(name)
    keep = lax.dynamic_slice_in_dim(partial_value, me * half, half, axis)
    send = lax.dynamic_slice_in_dim(partial_value, (1 - me) * half, half, axis)
    got = lax.ppermute(send, name, perm=[(0, 1), (1, 0)])
    return (keep.astype(jnp.float32) + got.astype(jnp.float32)).astype(partial_value.dtype)


def ctx_scatter(partial_value, axis, stages=SCATTER_STAGES):
    for names in stages:
        if len(names) == 1 and lax.axis_size(names[0]) == 2:
            partial_value = pair_scatter(partial_value, axis, names[0])
        else:
            partial_value = lax.psum_scatter(partial_value, names, scatter_dimension=axis, tiled=True)
    return partial_value


def reorder_blocks(values, axis, source, target):
    sizes = [lax.axis_size(name) for name in source]
    shape = values.shape
    block = shape[axis] // math.prod(sizes)
    split = values.reshape(shape[:axis] + tuple(sizes) + (block,) + shape[axis + 1 :])
    order = list(range(axis)) + [axis + source.index(name) for name in target]
    order += list(range(axis + len(source), split.ndim))
    return jnp.transpose(split, order).reshape(shape)


def natural_row(index, rows):
    device = index // rows
    place = {}
    for name in reversed(GATHERED_ORDER):
        size = lax.axis_size(name)
        place[name] = device % size
        device = device // size
    natural = 0
    for name in CTX_AXES:
        natural = natural * lax.axis_size(name) + place[name]
    return natural * rows + index % rows


AXIS_STAGES = tuple((name,) for name in SCATTER_ORDER)


def start_sum_over_ctx(pieces, stages=SCATTER_STAGES[:1]):
    joined = jnp.concatenate(pieces, axis=1).astype(jnp.bfloat16)
    joined = reorder_blocks(joined, 0, CTX_AXES, SCATTER_ORDER)
    return ctx_scatter(joined, 0, stages)


def finish_sum_over_ctx(partial_value, pieces, stages=SCATTER_STAGES[1:]):
    widths = [piece.shape[1] for piece in pieces]
    cuts = [sum(widths[:i]) for i in range(len(widths) + 1)]
    summed = ctx_scatter(partial_value, 0, stages).astype(jnp.float32)
    return [summed[:, cuts[i] : cuts[i + 1]] for i in range(len(pieces))]


def sum_over_ctx(pieces, stages=SCATTER_STAGES):
    return finish_sum_over_ctx(start_sum_over_ctx(pieces, stages[:1]), pieces, stages[1:])


def rows_total(partial_value):
    return lax.psum(partial_value, SHARD)


def full_rows(local):
    return lax.all_gather(local, SHARD, axis=1, tiled=True)


def share_rows(partial_value):
    shards = lax.axis_size(SHARD)
    rows, cols = partial_value.shape
    blocks = partial_value.astype(jnp.bfloat16).reshape(rows, shards, cols // shards)
    blocks = lax.all_to_all(blocks, SHARD, 1, 1, tiled=True)
    return jnp.sum(blocks.astype(jnp.float32), axis=1)


def add_rows(partial_value):
    pieces = lax.all_gather(partial_value.astype(jnp.bfloat16), SHARD, axis=0)
    return jnp.sum(pieces.astype(jnp.float32), axis=0)


def add_rows_direct(partial_value):
    owned = share_rows(partial_value)
    shards = lax.axis_size(SHARD)
    copies = jnp.broadcast_to(owned[None], (shards,) + owned.shape)
    blocks = lax.all_to_all(copies, SHARD, 0, 0, tiled=True)
    return jnp.transpose(blocks, (1, 0, 2)).reshape(owned.shape[0], shards * owned.shape[1])


def local_norm(values):
    scale = lax.rsqrt(jnp.mean(values * values, axis=1, keepdims=True) + EPSILON)
    return (scale, values * scale)


def local_back(grad_normed, unit, scale, gain):
    scaled = grad_normed * gain
    inner = jnp.mean(scaled * unit, axis=1, keepdims=True)
    return scale * (scaled - unit * inner)


def row_norm(values, width):
    total = rows_total(jnp.sum(values * values, axis=1))
    scale = lax.rsqrt(total / width + EPSILON)[:, None]
    return (scale, values * scale)


def norm_back(grad_normed, unit, scale, gain, width):
    scaled = grad_normed * gain
    inner = rows_total(jnp.sum(scaled * unit, axis=1)) / width
    return (scale * (scaled - unit * inner[:, None]), jnp.sum(grad_normed * unit, axis=0))


def over_blocks(step_fn, carry, arrays):
    whole = arrays[0].shape[1]
    step = min(whole, 1024)

    def turn(index, state):
        start = index * step
        pieces = tuple((lax.dynamic_slice_in_dim(array, start, step, 1) for array in arrays))
        return step_fn(state, pieces, start)

    return lax.fori_loop(0, whole // step, turn, carry)


def per_device(
    block_in,
    block_pairs,
    attn_gain,
    query_gain,
    key_gain,
    ffn_gain,
    w_query,
    w_key,
    w_value,
    w_output,
    w_gate,
    w_up,
    w_down,
    grad_output,
):
    seqs, rows, local_width = block_in.shape
    flat = seqs * rows
    width = local_width * lax.axis_size(SHARD)
    offset = lax.axis_index(SHARD) * local_width
    pieces = (w_query, w_key, w_value, w_gate, w_up, w_output.T, w_down.T)
    widths = [piece.shape[1] for piece in pieces]
    cuts = [sum(widths[:i]) for i in range(len(widths) + 1)]
    every_weight = ctx_gather(jnp.concatenate(pieces, axis=1), 0)
    every_weight = reorder_blocks(every_weight, 0, GATHERED_ORDER, CTX_AXES)
    gathered = [every_weight[:, cuts[i] : cuts[i + 1]] for i in range(len(pieces))]
    query_all, key_all_w, value_all_w, gate_all, up_all, output_all, down_all = gathered
    output_all = output_all.T
    down_all = down_all.T
    heads = query_all.shape[1] // HD
    kv_heads = key_all_w.shape[1] // HD
    group = heads // kv_heads
    factor = 1.0 / math.sqrt(HD)
    pos_query = token_positions(
        block_pairs, lax.axis_index(CTX_AXES) * rows + jnp.arange(rows, dtype=jnp.int32)
    )
    cosine_one, sine_one = rope_tables(pos_query)
    cosine = jnp.tile(cosine_one, (seqs, 1, 1))
    sine = jnp.tile(sine_one, (seqs, 1, 1))
    attn_slice = lax.dynamic_slice_in_dim(attn_gain, offset, local_width)
    ffn_slice = lax.dynamic_slice_in_dim(ffn_gain, offset, local_width)
    input_all = full_rows(block_in.reshape(flat, local_width)).astype(jnp.float32)
    scale_attn, unit_attn = local_norm(input_all)
    normed_attn = (unit_attn * attn_gain).astype(jnp.bfloat16)
    query_raw = wide_dot(normed_attn, query_all).reshape(flat, heads, HD)
    key_raw = wide_dot(normed_attn, key_all_w).reshape(flat, kv_heads, HD)
    value_rows = (
        wide_dot(normed_attn, value_all_w).astype(jnp.bfloat16).reshape(seqs, rows, kv_heads * HD)
    )
    query_scale, query_unit = head_norm(query_raw)
    key_scale, key_unit = head_norm(key_raw)
    query_norm = query_unit * query_gain
    key_norm = key_unit * key_gain
    query_rot = (
        (query_norm * cosine + rotate_half(query_norm) * sine)
        .astype(jnp.bfloat16)
        .reshape(seqs, rows, kv_heads, group, HD)
    )
    key_rot = (
        (key_norm * cosine + rotate_half(key_norm) * sine)
        .astype(jnp.bfloat16)
        .reshape(seqs, rows, kv_heads * HD)
    )

    def scores_at(key_piece, start):
        count = key_piece.shape[1]
        pos_key = token_positions(
            block_pairs, natural_row(start + jnp.arange(count, dtype=jnp.int32), rows)
        )
        keys = key_piece.reshape(seqs, count, kv_heads, HD)
        score = (
            jnp.einsum("bqkgd,bskd->bkgqs", query_rot, keys, preferred_element_type=jnp.float32)
            * factor
        )
        mask = pos_key[None, None, None, None, :] <= pos_query[None, None, None, :, None]
        return (score, mask, keys)

    def attend(carry, pieces, start):
        key_piece, value_piece = pieces
        count = key_piece.shape[1]
        score, mask, keys = scores_at(key_piece, start)
        weights = jnp.where(mask, jnp.exp(score), 0.0)
        total, summed = carry
        values = value_piece.reshape(seqs, count, kv_heads, HD)
        summed = summed + jnp.einsum(
            "bkgqs,bskd->bqkgd",
            weights.astype(jnp.bfloat16),
            values,
            preferred_element_type=jnp.float32,
        )
        return (total + jnp.sum(weights, axis=-1), summed)

    start_carry = (
        jnp.zeros((seqs, kv_heads, group, rows), jnp.float32),
        jnp.zeros((seqs, rows, kv_heads, group, HD), jnp.float32),
    )
    key_value = ctx_gather(jnp.concatenate([key_rot, value_rows], axis=2), 1)
    key_every = key_value[:, :, : kv_heads * HD]
    value_every = key_value[:, :, kv_heads * HD :]
    total, summed = over_blocks(attend, start_carry, (key_every, value_every))
    log_total = jnp.log(total)
    attn_heads = (summed / jnp.transpose(total, (0, 3, 1, 2))[..., None]).astype(jnp.bfloat16)
    attn_out = attn_heads.reshape(flat, heads * HD)
    middle_all = input_all + add_rows(wide_dot(attn_out, output_all))
    middle = lax.dynamic_slice_in_dim(middle_all, offset, local_width, 1)
    scale_ffn, unit_ffn = local_norm(middle_all)
    normed_ffn = (unit_ffn * ffn_gain).astype(jnp.bfloat16)
    gate = wide_dot(normed_ffn, gate_all)
    up_proj = wide_dot(normed_ffn, up_all)
    sigmoid_gate = jax.nn.sigmoid(gate)
    activated = gate * sigmoid_gate
    mixed = (activated * up_proj).astype(jnp.bfloat16)
    block_out = (middle + share_rows(wide_dot(mixed, down_all))).astype(jnp.bfloat16)
    grad_flat = grad_output.reshape(flat, local_width)
    grad_full = full_rows(grad_flat)
    grad_mixed = wide_dot(grad_full, down_all.T)
    down_grad = wide_dot(mixed.T, grad_full)
    grad_gate = (grad_mixed * up_proj * sigmoid_gate * (1.0 + gate * (1.0 - sigmoid_gate))).astype(
        jnp.bfloat16
    )
    grad_up = (grad_mixed * activated).astype(jnp.bfloat16)
    gate_grad = wide_dot(normed_ffn.T, grad_gate)
    up_grad = wide_dot(normed_ffn.T, grad_up)
    ffn_pieces = (gate_grad, up_grad, down_grad.T)
    ffn_partial = start_sum_over_ctx(ffn_pieces)
    grad_normed_ffn = add_rows_direct(wide_dot(grad_gate, gate_all.T) + wide_dot(grad_up, up_all.T))
    back_ffn = local_back(grad_normed_ffn, unit_ffn, scale_ffn, ffn_gain)
    ffn_part = lax.dynamic_slice_in_dim(jnp.sum(grad_normed_ffn * unit_ffn, axis=0), offset, local_width)
    grad_middle_full = grad_full.astype(jnp.float32) + back_ffn
    grad_middle_all = grad_middle_full.astype(jnp.bfloat16)
    grad_attn = wide_dot(grad_middle_all, output_all.T).reshape(seqs, rows, kv_heads, group, HD)
    output_grad = wide_dot(attn_out.T, grad_middle_all)
    delta = jnp.transpose(
        jnp.sum(grad_attn * attn_heads.astype(jnp.float32), axis=-1), (0, 2, 3, 1)
    )
    grad_attn_low = grad_attn.astype(jnp.bfloat16)

    def revisit(grad_query_sum, pieces, start):
        key_piece, value_piece = pieces
        count = key_piece.shape[1]
        score, mask, keys = scores_at(key_piece, start)
        values = value_piece.reshape(seqs, count, kv_heads, HD)
        prob = jnp.where(mask, jnp.exp(score - log_total[..., None]), 0.0)
        grad_prob = jnp.einsum(
            "bqkgd,bskd->bkgqs", grad_attn_low, values, preferred_element_type=jnp.float32
        )
        grad_score = (prob * (grad_prob - delta[..., None]) * factor).astype(jnp.bfloat16)
        grad_query_sum = grad_query_sum + jnp.einsum(
            "bkgqs,bskd->bqkgd", grad_score, keys, preferred_element_type=jnp.float32
        )
        key_term = jnp.einsum(
            "bkgqs,bqkgd->bskd", grad_score, query_rot, preferred_element_type=jnp.float32
        )
        value_term = jnp.einsum(
            "bkgqs,bqkgd->bskd",
            prob.astype(jnp.bfloat16),
            grad_attn_low,
            preferred_element_type=jnp.float32,
        )
        return (
            grad_query_sum,
            jnp.concatenate(
                [
                    key_term.reshape(seqs, count, kv_heads * HD),
                    value_term.reshape(seqs, count, kv_heads * HD),
                ],
                2,
            ),
        )

    whole = key_every.shape[1]
    step = min(whole, 1024)

    def back_turn(grad_query_sum, index):
        start = index * step
        pieces = (
            lax.dynamic_slice_in_dim(key_every, start, step, 1),
            lax.dynamic_slice_in_dim(value_every, start, step, 1),
        )
        return revisit(grad_query_sum, pieces, start)

    grad_query_rot, key_terms = lax.scan(
        back_turn,
        jnp.zeros((seqs, rows, kv_heads, group, HD), jnp.float32),
        jnp.arange(whole // step, dtype=jnp.int32),
    )
    key_terms = jnp.transpose(key_terms, (1, 0, 2, 3)).reshape(seqs, whole, 2 * kv_heads * HD)
    key_terms, ffn_partial = lax.optimization_barrier((key_terms, ffn_partial))
    ffn_summed = finish_sum_over_ctx(ffn_partial, ffn_pieces)
    owned = (
        ctx_scatter(key_terms.astype(jnp.bfloat16), 1, AXIS_STAGES)
        .astype(jnp.float32)
        .reshape(flat, 2 * kv_heads * HD)
    )
    grad_key_rot = owned[:, : kv_heads * HD].reshape(flat, kv_heads, HD)
    grad_value_low = owned[:, kv_heads * HD :].astype(jnp.bfloat16)
    grad_query_rot = grad_query_rot.reshape(flat, heads, HD)
    grad_query_unit = grad_query_rot * cosine - rotate_half(grad_query_rot * sine)
    grad_key_unit = grad_key_rot * cosine - rotate_half(grad_key_rot * sine)
    query_gain_part = jnp.sum(grad_query_unit * query_unit, axis=(0, 1))
    key_gain_part = jnp.sum(grad_key_unit * key_unit, axis=(0, 1))
    grad_query = (
        head_back(grad_query_unit, query_unit, query_scale, query_gain)
        .astype(jnp.bfloat16)
        .reshape(flat, heads * HD)
    )
    grad_key = (
        head_back(grad_key_unit, key_unit, key_scale, key_gain)
        .astype(jnp.bfloat16)
        .reshape(flat, kv_heads * HD)
    )
    query_grad = wide_dot(normed_attn.T, grad_query)
    key_grad = wide_dot(normed_attn.T, grad_key)
    value_grad = wide_dot(normed_attn.T, grad_value_low)
    grad_normed_attn = add_rows_direct(
        wide_dot(grad_query, query_all.T)
        + wide_dot(grad_key, key_all_w.T)
        + wide_dot(grad_value_low, value_all_w.T)
    )
    back_attn = local_back(grad_normed_attn, unit_attn, scale_attn, attn_gain)
    attn_part = lax.dynamic_slice_in_dim(jnp.sum(grad_normed_attn * unit_attn, axis=0), offset, local_width)
    input_grad = lax.dynamic_slice_in_dim(grad_middle_full + back_attn, offset, local_width, 1)
    attn_pieces = (query_grad, key_grad, value_grad, output_grad.T)
    attn_partial = start_sum_over_ctx(attn_pieces, AXIS_STAGES[:2])
    attn_placed = lax.dynamic_update_slice_in_dim(
        jnp.zeros((width,), jnp.float32), attn_part, offset, 0
    )
    ffn_placed = lax.dynamic_update_slice_in_dim(
        jnp.zeros((width,), jnp.float32), ffn_part, offset, 0
    )
    gains = (attn_placed, query_gain_part, key_gain_part, ffn_placed)
    for names in (SHARD,) + tuple(reversed(CTX_AXES)):
        gains = lax.psum(gains, names)
    attn_partial, gains = lax.optimization_barrier((attn_partial, gains))
    query_grad, key_grad, value_grad, output_grad = finish_sum_over_ctx(
        attn_partial, attn_pieces, AXIS_STAGES[2:]
    )
    gate_grad, up_grad, down_grad = ffn_summed
    output_grad = output_grad.T
    down_grad = down_grad.T
    attn_gain_grad, query_gain_grad, key_gain_grad, ffn_gain_grad = gains
    block_out = block_out.reshape(seqs, rows, local_width)
    input_grad = input_grad.reshape(seqs, rows, local_width)
    return (
        block_out,
        input_grad,
        attn_gain_grad,
        query_gain_grad,
        key_gain_grad,
        ffn_gain_grad,
        query_grad,
        key_grad,
        value_grad,
        output_grad,
        gate_grad,
        up_grad,
        down_grad,
    )


def solution(mesh):
    ctx_size, shard_size = mesh.devices.shape
    fine = Mesh(mesh.devices.reshape(2, 4, ctx_size // 8, 2, shard_size // 2), EVERY)
    ctx = CTX_AXES
    in_specs = (
        P(None, ctx, SHARD),
        P(),
        P(),
        P(),
        P(),
        P(),
        P(ctx, SHARD),
        P(ctx, SHARD),
        P(ctx, SHARD),
        P(SHARD, ctx),
        P(ctx, SHARD),
        P(ctx, SHARD),
        P(SHARD, ctx),
        P(None, ctx, SHARD),
    )
    out_specs = (
        P(None, ctx, SHARD),
        P(None, ctx, SHARD),
        P(),
        P(),
        P(),
        P(),
        P(ctx, SHARD),
        P(ctx, SHARD),
        P(ctx, SHARD),
        P(SHARD, ctx),
        P(ctx, SHARD),
        P(ctx, SHARD),
        P(SHARD, ctx),
    )
    return jax.shard_map(
        per_device, mesh=fine, in_specs=in_specs, out_specs=out_specs, check_vma=False
    )
```

```python
import math

import jax
import jax.numpy as jnp
from jax import lax
from jax.sharding import Mesh, PartitionSpec as P

HD = 64
BLK = 64


EPSILON = 1e-05
ROPE_BASE = 1000000.0


def wide_dot(left, right):
    return jnp.dot(left, right, preferred_element_type=jnp.float32)


def token_positions(block_pairs, row_index):
    owner = row_index // (2 * BLK)
    half = row_index // BLK % 2
    devices = jnp.arange(block_pairs.shape[0], dtype=jnp.int32)
    chosen = jnp.where(half[:, None] == 0, block_pairs[None, :, 0], block_pairs[None, :, 1])
    number = jnp.sum(jnp.where(owner[:, None] == devices[None, :], chosen, 0), axis=1)
    return number * BLK + row_index % BLK


def rope_tables(positions):
    index = jnp.arange(HD // 2, dtype=jnp.float32)
    inverse = jnp.exp(index * (-2.0 * math.log(ROPE_BASE) / HD))
    angle = positions.astype(jnp.float32)[:, None] * inverse[None, :]
    cosine = jnp.cos(angle)
    sine = jnp.sin(angle)
    return (
        jnp.concatenate([cosine, cosine], 1)[:, None, :],
        jnp.concatenate([sine, sine], 1)[:, None, :],
    )


def rotate_half(values):
    middle = values.shape[-1] // 2
    return jnp.concatenate([-values[..., middle:], values[..., :middle]], -1)


def head_norm(values):
    scale = lax.rsqrt(jnp.mean(values * values, axis=-1, keepdims=True) + EPSILON)
    return (scale, values * scale)


def head_back(grad_normed, unit, scale, gain):
    scaled = grad_normed * gain
    inner = jnp.mean(scaled * unit, axis=-1, keepdims=True)
    return scale * (scaled - unit * inner)


CTX_AXES = ("cx", "cy", "cz")
SHARD = ("sx", "sc")
EVERY = CTX_AXES + SHARD


GATHER_STAGES = (("cx",), ("cy", "cz"))
SCATTER_STAGES = tuple(reversed(GATHER_STAGES))
GATHERED_ORDER = tuple(name for stage in reversed(GATHER_STAGES) for name in stage)
SCATTER_ORDER = tuple(name for stage in SCATTER_STAGES for name in stage)


def ctx_gather(local, axis):
    for names in GATHER_STAGES:
        local = lax.all_gather(local, names, axis=axis, tiled=True)
    return local


def pair_scatter(partial_value, axis, name):
    half = partial_value.shape[axis] // 2
    me = lax.axis_index(name)
    keep = lax.dynamic_slice_in_dim(partial_value, me * half, half, axis)
    send = lax.dynamic_slice_in_dim(partial_value, (1 - me) * half, half, axis)
    got = lax.ppermute(send, name, perm=[(0, 1), (1, 0)])
    return (keep.astype(jnp.float32) + got.astype(jnp.float32)).astype(partial_value.dtype)


def ctx_scatter(partial_value, axis, stages=SCATTER_STAGES):
    for names in stages:
        if len(names) == 1 and lax.axis_size(names[0]) == 2:
            partial_value = pair_scatter(partial_value, axis, names[0])
        else:
            partial_value = lax.psum_scatter(partial_value, names, scatter_dimension=axis, tiled=True)
    return partial_value


def reorder_blocks(values, axis, source, target):
    sizes = [lax.axis_size(name) for name in source]
    shape = values.shape
    block = shape[axis] // math.prod(sizes)
    split = values.reshape(shape[:axis] + tuple(sizes) + (block,) + shape[axis + 1 :])
    order = list(range(axis)) + [axis + source.index(name) for name in target]
    order += list(range(axis + len(source), split.ndim))
    return jnp.transpose(split, order).reshape(shape)


def natural_row(index, rows):
    device = index // rows
    place = {}
    for name in reversed(GATHERED_ORDER):
        size = lax.axis_size(name)
        place[name] = device % size
        device = device // size
    natural = 0
    for name in CTX_AXES:
        natural = natural * lax.axis_size(name) + place[name]
    return natural * rows + index % rows


AXIS_STAGES = tuple((name,) for name in SCATTER_ORDER)


def start_sum_over_ctx(pieces, stages=SCATTER_STAGES[:1]):
    joined = jnp.concatenate(pieces, axis=1).astype(jnp.bfloat16)
    joined = reorder_blocks(joined, 0, CTX_AXES, SCATTER_ORDER)
    return ctx_scatter(joined, 0, stages)


def finish_sum_over_ctx(partial_value, pieces, stages=SCATTER_STAGES[1:]):
    widths = [piece.shape[1] for piece in pieces]
    cuts = [sum(widths[:i]) for i in range(len(widths) + 1)]
    summed = ctx_scatter(partial_value, 0, stages).astype(jnp.float32)
    return [summed[:, cuts[i] : cuts[i + 1]] for i in range(len(pieces))]


def sum_over_ctx(pieces, stages=SCATTER_STAGES):
    return finish_sum_over_ctx(start_sum_over_ctx(pieces, stages[:1]), pieces, stages[1:])


def rows_total(partial_value):
    return lax.psum(partial_value, SHARD)


def full_rows(local):
    return lax.all_gather(local, SHARD, axis=1, tiled=True)


def share_rows(partial_value):
    shards = lax.axis_size(SHARD)
    rows, cols = partial_value.shape
    blocks = partial_value.astype(jnp.bfloat16).reshape(rows, shards, cols // shards)
    blocks = lax.all_to_all(blocks, SHARD, 1, 1, tiled=True)
    return jnp.sum(blocks.astype(jnp.float32), axis=1)


def add_rows(partial_value):
    pieces = lax.all_gather(partial_value.astype(jnp.bfloat16), SHARD, axis=0)
    return jnp.sum(pieces.astype(jnp.float32), axis=0)


def add_rows_direct(partial_value):
    owned = share_rows(partial_value)
    shards = lax.axis_size(SHARD)
    copies = jnp.broadcast_to(owned[None], (shards,) + owned.shape)
    blocks = lax.all_to_all(copies, SHARD, 0, 0, tiled=True)
    return jnp.transpose(blocks, (1, 0, 2)).reshape(owned.shape[0], shards * owned.shape[1])


def local_norm(values):
    scale = lax.rsqrt(jnp.mean(values * values, axis=1, keepdims=True) + EPSILON)
    return (scale, values * scale)


def local_back(grad_normed, unit, scale, gain):
    scaled = grad_normed * gain
    inner = jnp.mean(scaled * unit, axis=1, keepdims=True)
    return scale * (scaled - unit * inner)


def row_norm(values, width):
    total = rows_total(jnp.sum(values * values, axis=1))
    scale = lax.rsqrt(total / width + EPSILON)[:, None]
    return (scale, values * scale)


def norm_back(grad_normed, unit, scale, gain, width):
    scaled = grad_normed * gain
    inner = rows_total(jnp.sum(scaled * unit, axis=1)) / width
    return (scale * (scaled - unit * inner[:, None]), jnp.sum(grad_normed * unit, axis=0))


def over_blocks(step_fn, carry, arrays):
    whole = arrays[0].shape[1]
    step = min(whole, 1024)

    def turn(index, state):
        start = index * step
        pieces = tuple((lax.dynamic_slice_in_dim(array, start, step, 1) for array in arrays))
        return step_fn(state, pieces, start)

    return lax.fori_loop(0, whole // step, turn, carry)


def per_device(
    block_in,
    block_pairs,
    attn_gain,
    query_gain,
    key_gain,
    ffn_gain,
    w_query,
    w_key,
    w_value,
    w_output,
    w_gate,
    w_up,
    w_down,
    grad_output,
):
    seqs, rows, local_width = block_in.shape
    flat = seqs * rows
    width = local_width * lax.axis_size(SHARD)
    offset = lax.axis_index(SHARD) * local_width
    pieces = (w_query, w_key, w_value, w_gate, w_up, w_output.T, w_down.T)
    widths = [piece.shape[1] for piece in pieces]
    cuts = [sum(widths[:i]) for i in range(len(widths) + 1)]
    every_weight = ctx_gather(jnp.concatenate(pieces, axis=1), 0)
    every_weight = reorder_blocks(every_weight, 0, GATHERED_ORDER, CTX_AXES)
    gathered = [every_weight[:, cuts[i] : cuts[i + 1]] for i in range(len(pieces))]
    query_all, key_all_w, value_all_w, gate_all, up_all, output_all, down_all = gathered
    output_all = output_all.T
    down_all = down_all.T
    heads = query_all.shape[1] // HD
    kv_heads = key_all_w.shape[1] // HD
    group = heads // kv_heads
    factor = 1.0 / math.sqrt(HD)
    pos_query = token_positions(
        block_pairs, lax.axis_index(CTX_AXES) * rows + jnp.arange(rows, dtype=jnp.int32)
    )
    cosine_one, sine_one = rope_tables(pos_query)
    cosine = jnp.tile(cosine_one, (seqs, 1, 1))
    sine = jnp.tile(sine_one, (seqs, 1, 1))
    attn_slice = lax.dynamic_slice_in_dim(attn_gain, offset, local_width)
    ffn_slice = lax.dynamic_slice_in_dim(ffn_gain, offset, local_width)
    input_all = full_rows(block_in.reshape(flat, local_width)).astype(jnp.float32)
    scale_attn, unit_attn = local_norm(input_all)
    normed_attn = (unit_attn * attn_gain).astype(jnp.bfloat16)
    query_raw = wide_dot(normed_attn, query_all).reshape(flat, heads, HD)
    key_raw = wide_dot(normed_attn, key_all_w).reshape(flat, kv_heads, HD)
    value_rows = (
        wide_dot(normed_attn, value_all_w).astype(jnp.bfloat16).reshape(seqs, rows, kv_heads * HD)
    )
    query_scale, query_unit = head_norm(query_raw)
    key_scale, key_unit = head_norm(key_raw)
    query_norm = query_unit * query_gain
    key_norm = key_unit * key_gain
    query_rot = (
        (query_norm * cosine + rotate_half(query_norm) * sine)
        .astype(jnp.bfloat16)
        .reshape(seqs, rows, kv_heads, group, HD)
    )
    key_rot = (
        (key_norm * cosine + rotate_half(key_norm) * sine)
        .astype(jnp.bfloat16)
        .reshape(seqs, rows, kv_heads * HD)
    )

    def scores_at(key_piece, start):
        count = key_piece.shape[1]
        pos_key = token_positions(
            block_pairs, natural_row(start + jnp.arange(count, dtype=jnp.int32), rows)
        )
        keys = key_piece.reshape(seqs, count, kv_heads, HD)
        score = (
            jnp.einsum("bqkgd,bskd->bkgqs", query_rot, keys, preferred_element_type=jnp.float32)
            * factor
        )
        mask = pos_key[None, None, None, None, :] <= pos_query[None, None, None, :, None]
        return (score, mask, keys)

    def attend(carry, pieces, start):
        key_piece, value_piece = pieces
        count = key_piece.shape[1]
        score, mask, keys = scores_at(key_piece, start)
        weights = jnp.where(mask, jnp.exp(score), 0.0)
        total, summed = carry
        values = value_piece.reshape(seqs, count, kv_heads, HD)
        summed = summed + jnp.einsum(
            "bkgqs,bskd->bqkgd",
            weights.astype(jnp.bfloat16),
            values,
            preferred_element_type=jnp.float32,
        )
        return (total + jnp.sum(weights, axis=-1), summed)

    start_carry = (
        jnp.zeros((seqs, kv_heads, group, rows), jnp.float32),
        jnp.zeros((seqs, rows, kv_heads, group, HD), jnp.float32),
    )
    key_value = ctx_gather(jnp.concatenate([key_rot, value_rows], axis=2), 1)
    key_every = key_value[:, :, : kv_heads * HD]
    value_every = key_value[:, :, kv_heads * HD :]
    total, summed = over_blocks(attend, start_carry, (key_every, value_every))
    log_total = jnp.log(total)
    attn_heads = (summed / jnp.transpose(total, (0, 3, 1, 2))[..., None]).astype(jnp.bfloat16)
    attn_out = attn_heads.reshape(flat, heads * HD)
    middle_all = input_all + add_rows(wide_dot(attn_out, output_all))
    middle = lax.dynamic_slice_in_dim(middle_all, offset, local_width, 1)
    scale_ffn, unit_ffn = local_norm(middle_all)
    normed_ffn = (unit_ffn * ffn_gain).astype(jnp.bfloat16)
    gate = wide_dot(normed_ffn, gate_all)
    up_proj = wide_dot(normed_ffn, up_all)
    sigmoid_gate = jax.nn.sigmoid(gate)
    activated = gate * sigmoid_gate
    mixed = (activated * up_proj).astype(jnp.bfloat16)
    block_out = (middle + share_rows(wide_dot(mixed, down_all))).astype(jnp.bfloat16)
    grad_flat = grad_output.reshape(flat, local_width)
    grad_full = full_rows(grad_flat)
    grad_mixed = wide_dot(grad_full, down_all.T)
    down_grad = wide_dot(mixed.T, grad_full)
    grad_gate = (grad_mixed * up_proj * sigmoid_gate * (1.0 + gate * (1.0 - sigmoid_gate))).astype(
        jnp.bfloat16
    )
    grad_up = (grad_mixed * activated).astype(jnp.bfloat16)
    gate_grad = wide_dot(normed_ffn.T, grad_gate)
    up_grad = wide_dot(normed_ffn.T, grad_up)
    ffn_pieces = (gate_grad, up_grad, down_grad.T)
    ffn_partial = start_sum_over_ctx(ffn_pieces)
    grad_normed_ffn = add_rows_direct(wide_dot(grad_gate, gate_all.T) + wide_dot(grad_up, up_all.T))
    back_ffn = local_back(grad_normed_ffn, unit_ffn, scale_ffn, ffn_gain)
    ffn_part = lax.dynamic_slice_in_dim(jnp.sum(grad_normed_ffn * unit_ffn, axis=0), offset, local_width)
    grad_middle_full = grad_full.astype(jnp.float32) + back_ffn
    grad_middle_all = grad_middle_full.astype(jnp.bfloat16)
    grad_attn = wide_dot(grad_middle_all, output_all.T).reshape(seqs, rows, kv_heads, group, HD)
    output_grad = wide_dot(attn_out.T, grad_middle_all)
    delta = jnp.transpose(
        jnp.sum(grad_attn * attn_heads.astype(jnp.float32), axis=-1), (0, 2, 3, 1)
    )
    grad_attn_low = grad_attn.astype(jnp.bfloat16)

    def revisit(grad_query_sum, pieces, start):
        key_piece, value_piece = pieces
        count = key_piece.shape[1]
        score, mask, keys = scores_at(key_piece, start)
        values = value_piece.reshape(seqs, count, kv_heads, HD)
        prob = jnp.where(mask, jnp.exp(score - log_total[..., None]), 0.0)
        grad_prob = jnp.einsum(
            "bqkgd,bskd->bkgqs", grad_attn_low, values, preferred_element_type=jnp.float32
        )
        grad_score = (prob * (grad_prob - delta[..., None]) * factor).astype(jnp.bfloat16)
        grad_query_sum = grad_query_sum + jnp.einsum(
            "bkgqs,bskd->bqkgd", grad_score, keys, preferred_element_type=jnp.float32
        )
        key_term = jnp.einsum(
            "bkgqs,bqkgd->bskd", grad_score, query_rot, preferred_element_type=jnp.float32
        )
        value_term = jnp.einsum(
            "bkgqs,bqkgd->bskd",
            prob.astype(jnp.bfloat16),
            grad_attn_low,
            preferred_element_type=jnp.float32,
        )
        return (
            grad_query_sum,
            jnp.concatenate(
                [
                    key_term.reshape(seqs, count, kv_heads * HD),
                    value_term.reshape(seqs, count, kv_heads * HD),
                ],
                2,
            ),
        )

    whole = key_every.shape[1]
    step = min(whole, 1024)

    def back_turn(grad_query_sum, index):
        start = index * step
        pieces = (
            lax.dynamic_slice_in_dim(key_every, start, step, 1),
            lax.dynamic_slice_in_dim(value_every, start, step, 1),
        )
        return revisit(grad_query_sum, pieces, start)

    grad_query_rot, key_terms = lax.scan(
        back_turn,
        jnp.zeros((seqs, rows, kv_heads, group, HD), jnp.float32),
        jnp.arange(whole // step, dtype=jnp.int32),
    )
    key_terms = jnp.transpose(key_terms, (1, 0, 2, 3)).reshape(seqs, whole, 2 * kv_heads * HD)
    key_terms, ffn_partial = lax.optimization_barrier((key_terms, ffn_partial))
    ffn_summed = finish_sum_over_ctx(ffn_partial, ffn_pieces)
    owned = (
        ctx_scatter(key_terms.astype(jnp.bfloat16), 1, AXIS_STAGES)
        .astype(jnp.float32)
        .reshape(flat, 2 * kv_heads * HD)
    )
    grad_key_rot = owned[:, : kv_heads * HD].reshape(flat, kv_heads, HD)
    grad_value_low = owned[:, kv_heads * HD :].astype(jnp.bfloat16)
    grad_query_rot = grad_query_rot.reshape(flat, heads, HD)
    grad_query_unit = grad_query_rot * cosine - rotate_half(grad_query_rot * sine)
    grad_key_unit = grad_key_rot * cosine - rotate_half(grad_key_rot * sine)
    query_gain_part = jnp.sum(grad_query_unit * query_unit, axis=(0, 1))
    key_gain_part = jnp.sum(grad_key_unit * key_unit, axis=(0, 1))
    grad_query = (
        head_back(grad_query_unit, query_unit, query_scale, query_gain)
        .astype(jnp.bfloat16)
        .reshape(flat, heads * HD)
    )
    grad_key = (
        head_back(grad_key_unit, key_unit, key_scale, key_gain)
        .astype(jnp.bfloat16)
        .reshape(flat, kv_heads * HD)
    )
    query_grad = wide_dot(normed_attn.T, grad_query)
    key_grad = wide_dot(normed_attn.T, grad_key)
    value_grad = wide_dot(normed_attn.T, grad_value_low)
    grad_normed_attn = add_rows_direct(
        wide_dot(grad_query, query_all.T)
        + wide_dot(grad_key, key_all_w.T)
        + wide_dot(grad_value_low, value_all_w.T)
    )
    back_attn = local_back(grad_normed_attn, unit_attn, scale_attn, attn_gain)
    attn_part = lax.dynamic_slice_in_dim(jnp.sum(grad_normed_attn * unit_attn, axis=0), offset, local_width)
    input_grad = lax.dynamic_slice_in_dim(grad_middle_full + back_attn, offset, local_width, 1)
    attn_pieces = (query_grad, key_grad, value_grad, output_grad.T)
    attn_partial = start_sum_over_ctx(attn_pieces, AXIS_STAGES[:2])
    whole_gains = (
        jnp.sum(grad_normed_attn * unit_attn, axis=0),
        jnp.sum(grad_normed_ffn * unit_ffn, axis=0),
    )
    head_gains = (query_gain_part, key_gain_part)
    for names in tuple(reversed(CTX_AXES)):
        whole_gains = lax.psum(whole_gains, names)
    for names in (SHARD,) + tuple(reversed(CTX_AXES)):
        head_gains = lax.psum(head_gains, names)
    gains = (whole_gains[0], head_gains[0], head_gains[1], whole_gains[1])
    attn_partial, gains = lax.optimization_barrier((attn_partial, gains))
    query_grad, key_grad, value_grad, output_grad = finish_sum_over_ctx(
        attn_partial, attn_pieces, AXIS_STAGES[2:]
    )
    gate_grad, up_grad, down_grad = ffn_summed
    output_grad = output_grad.T
    down_grad = down_grad.T
    attn_gain_grad, query_gain_grad, key_gain_grad, ffn_gain_grad = gains
    block_out = block_out.reshape(seqs, rows, local_width)
    input_grad = input_grad.reshape(seqs, rows, local_width)
    return (
        block_out,
        input_grad,
        attn_gain_grad,
        query_gain_grad,
        key_gain_grad,
        ffn_gain_grad,
        query_grad,
        key_grad,
        value_grad,
        output_grad,
        gate_grad,
        up_grad,
        down_grad,
    )


def solution(mesh):
    ctx_size, shard_size = mesh.devices.shape
    fine = Mesh(mesh.devices.reshape(2, 4, ctx_size // 8, 2, shard_size // 2), EVERY)
    ctx = CTX_AXES
    in_specs = (
        P(None, ctx, SHARD),
        P(),
        P(),
        P(),
        P(),
        P(),
        P(ctx, SHARD),
        P(ctx, SHARD),
        P(ctx, SHARD),
        P(SHARD, ctx),
        P(ctx, SHARD),
        P(ctx, SHARD),
        P(SHARD, ctx),
        P(None, ctx, SHARD),
    )
    out_specs = (
        P(None, ctx, SHARD),
        P(None, ctx, SHARD),
        P(),
        P(),
        P(),
        P(),
        P(ctx, SHARD),
        P(ctx, SHARD),
        P(ctx, SHARD),
        P(SHARD, ctx),
        P(ctx, SHARD),
        P(ctx, SHARD),
        P(SHARD, ctx),
    )
    return jax.shard_map(
        per_device, mesh=fine, in_specs=in_specs, out_specs=out_specs, check_vma=False
    )
```

```python
import math

import jax
import jax.numpy as jnp
from jax import lax
from jax.sharding import Mesh, PartitionSpec as P

HD = 64
BLK = 64


EPSILON = 1e-05
ROPE_BASE = 1000000.0


def wide_dot(left, right):
    return jnp.dot(left, right, preferred_element_type=jnp.float32)


def token_positions(block_pairs, row_index):
    owner = row_index // (2 * BLK)
    half = row_index // BLK % 2
    devices = jnp.arange(block_pairs.shape[0], dtype=jnp.int32)
    chosen = jnp.where(half[:, None] == 0, block_pairs[None, :, 0], block_pairs[None, :, 1])
    number = jnp.sum(jnp.where(owner[:, None] == devices[None, :], chosen, 0), axis=1)
    return number * BLK + row_index % BLK


def rope_tables(positions):
    index = jnp.arange(HD // 2, dtype=jnp.float32)
    inverse = jnp.exp(index * (-2.0 * math.log(ROPE_BASE) / HD))
    angle = positions.astype(jnp.float32)[:, None] * inverse[None, :]
    cosine = jnp.cos(angle)
    sine = jnp.sin(angle)
    return (
        jnp.concatenate([cosine, cosine], 1)[:, None, :],
        jnp.concatenate([sine, sine], 1)[:, None, :],
    )


def rotate_half(values):
    middle = values.shape[-1] // 2
    return jnp.concatenate([-values[..., middle:], values[..., :middle]], -1)


def head_norm(values):
    scale = lax.rsqrt(jnp.mean(values * values, axis=-1, keepdims=True) + EPSILON)
    return (scale, values * scale)


def head_back(grad_normed, unit, scale, gain):
    scaled = grad_normed * gain
    inner = jnp.mean(scaled * unit, axis=-1, keepdims=True)
    return scale * (scaled - unit * inner)


CTX_AXES = ("cx", "cy", "cz")
SHARD = ("sx", "sc")
EVERY = CTX_AXES + SHARD


GATHER_STAGES = (("cx",), ("cy", "cz"))
SCATTER_STAGES = tuple(reversed(GATHER_STAGES))
GATHERED_ORDER = tuple(name for stage in reversed(GATHER_STAGES) for name in stage)
SCATTER_ORDER = tuple(name for stage in SCATTER_STAGES for name in stage)


def ctx_gather(local, axis):
    for names in GATHER_STAGES:
        local = lax.all_gather(local, names, axis=axis, tiled=True)
    return local


def pair_scatter(partial_value, axis, name):
    half = partial_value.shape[axis] // 2
    me = lax.axis_index(name)
    keep = lax.dynamic_slice_in_dim(partial_value, me * half, half, axis)
    send = lax.dynamic_slice_in_dim(partial_value, (1 - me) * half, half, axis)
    got = lax.ppermute(send, name, perm=[(0, 1), (1, 0)])
    return (keep.astype(jnp.float32) + got.astype(jnp.float32)).astype(partial_value.dtype)


def ctx_scatter(partial_value, axis, stages=SCATTER_STAGES):
    for names in stages:
        if len(names) == 1 and lax.axis_size(names[0]) == 2:
            partial_value = pair_scatter(partial_value, axis, names[0])
        else:
            partial_value = lax.psum_scatter(partial_value, names, scatter_dimension=axis, tiled=True)
    return partial_value


def reorder_blocks(values, axis, source, target):
    sizes = [lax.axis_size(name) for name in source]
    shape = values.shape
    block = shape[axis] // math.prod(sizes)
    split = values.reshape(shape[:axis] + tuple(sizes) + (block,) + shape[axis + 1 :])
    order = list(range(axis)) + [axis + source.index(name) for name in target]
    order += list(range(axis + len(source), split.ndim))
    return jnp.transpose(split, order).reshape(shape)


def natural_row(index, rows):
    device = index // rows
    place = {}
    for name in reversed(GATHERED_ORDER):
        size = lax.axis_size(name)
        place[name] = device % size
        device = device // size
    natural = 0
    for name in CTX_AXES:
        natural = natural * lax.axis_size(name) + place[name]
    return natural * rows + index % rows


AXIS_STAGES = tuple((name,) for name in SCATTER_ORDER)


def start_sum_over_ctx(pieces, stages=SCATTER_STAGES[:1]):
    joined = jnp.concatenate(pieces, axis=1).astype(jnp.bfloat16)
    return ctx_scatter(joined, 0, stages)


def finish_sum_over_ctx(partial_value, pieces, stages=SCATTER_STAGES[1:]):
    widths = [piece.shape[1] for piece in pieces]
    cuts = [sum(widths[:i]) for i in range(len(widths) + 1)]
    summed = ctx_scatter(partial_value, 0, stages).astype(jnp.float32)
    return [summed[:, cuts[i] : cuts[i + 1]] for i in range(len(pieces))]


def sum_over_ctx(pieces, stages=SCATTER_STAGES):
    return finish_sum_over_ctx(start_sum_over_ctx(pieces, stages[:1]), pieces, stages[1:])


def rows_total(partial_value):
    return lax.psum(partial_value, SHARD)


def full_rows(local):
    return lax.all_gather(local, SHARD, axis=1, tiled=True)


def share_rows(partial_value):
    shards = lax.axis_size(SHARD)
    rows, cols = partial_value.shape
    blocks = partial_value.astype(jnp.bfloat16).reshape(rows, shards, cols // shards)
    blocks = lax.all_to_all(blocks, SHARD, 1, 1, tiled=True)
    return jnp.sum(blocks.astype(jnp.float32), axis=1)


def add_rows(partial_value):
    pieces = lax.all_gather(partial_value.astype(jnp.bfloat16), SHARD, axis=0)
    return jnp.sum(pieces.astype(jnp.float32), axis=0)


def add_rows_direct(partial_value):
    owned = share_rows(partial_value)
    shards = lax.axis_size(SHARD)
    copies = jnp.broadcast_to(owned[None], (shards,) + owned.shape)
    blocks = lax.all_to_all(copies, SHARD, 0, 0, tiled=True)
    return jnp.transpose(blocks, (1, 0, 2)).reshape(owned.shape[0], shards * owned.shape[1])


def local_norm(values):
    scale = lax.rsqrt(jnp.mean(values * values, axis=1, keepdims=True) + EPSILON)
    return (scale, values * scale)


def local_back(grad_normed, unit, scale, gain):
    scaled = grad_normed * gain
    inner = jnp.mean(scaled * unit, axis=1, keepdims=True)
    return scale * (scaled - unit * inner)


def row_norm(values, width):
    total = rows_total(jnp.sum(values * values, axis=1))
    scale = lax.rsqrt(total / width + EPSILON)[:, None]
    return (scale, values * scale)


def norm_back(grad_normed, unit, scale, gain, width):
    scaled = grad_normed * gain
    inner = rows_total(jnp.sum(scaled * unit, axis=1)) / width
    return (scale * (scaled - unit * inner[:, None]), jnp.sum(grad_normed * unit, axis=0))


def over_blocks(step_fn, carry, arrays):
    whole = arrays[0].shape[1]
    step = min(whole, 1024)

    def turn(index, state):
        start = index * step
        pieces = tuple((lax.dynamic_slice_in_dim(array, start, step, 1) for array in arrays))
        return step_fn(state, pieces, start)

    return lax.fori_loop(0, whole // step, turn, carry)


def per_device(
    block_in,
    block_pairs,
    attn_gain,
    query_gain,
    key_gain,
    ffn_gain,
    w_query,
    w_key,
    w_value,
    w_output,
    w_gate,
    w_up,
    w_down,
    grad_output,
):
    seqs, rows, local_width = block_in.shape
    flat = seqs * rows
    width = local_width * lax.axis_size(SHARD)
    offset = lax.axis_index(SHARD) * local_width
    pieces = (w_query, w_key, w_value, w_gate, w_up, w_output.T, w_down.T)
    widths = [piece.shape[1] for piece in pieces]
    cuts = [sum(widths[:i]) for i in range(len(widths) + 1)]
    every_weight = ctx_gather(jnp.concatenate(pieces, axis=1), 0)

    def to_gathered(values):
        return reorder_blocks(values, 1, CTX_AXES, GATHERED_ORDER)

    def to_natural(values):
        return reorder_blocks(values, 1, GATHERED_ORDER, CTX_AXES)
    gathered = [every_weight[:, cuts[i] : cuts[i + 1]] for i in range(len(pieces))]
    query_all, key_all_w, value_all_w, gate_all, up_all, output_all, down_all = gathered
    output_all = output_all.T
    down_all = down_all.T
    heads = query_all.shape[1] // HD
    kv_heads = key_all_w.shape[1] // HD
    group = heads // kv_heads
    factor = 1.0 / math.sqrt(HD)
    pos_query = token_positions(
        block_pairs, lax.axis_index(CTX_AXES) * rows + jnp.arange(rows, dtype=jnp.int32)
    )
    cosine_one, sine_one = rope_tables(pos_query)
    cosine = jnp.tile(cosine_one, (seqs, 1, 1))
    sine = jnp.tile(sine_one, (seqs, 1, 1))
    attn_slice = lax.dynamic_slice_in_dim(attn_gain, offset, local_width)
    ffn_slice = lax.dynamic_slice_in_dim(ffn_gain, offset, local_width)
    input_all = full_rows(block_in.reshape(flat, local_width)).astype(jnp.float32)
    scale_attn, unit_attn = local_norm(input_all)
    normed_attn = to_gathered((unit_attn * attn_gain).astype(jnp.bfloat16))
    query_raw = wide_dot(normed_attn, query_all).reshape(flat, heads, HD)
    key_raw = wide_dot(normed_attn, key_all_w).reshape(flat, kv_heads, HD)
    value_rows = (
        wide_dot(normed_attn, value_all_w).astype(jnp.bfloat16).reshape(seqs, rows, kv_heads * HD)
    )
    query_scale, query_unit = head_norm(query_raw)
    key_scale, key_unit = head_norm(key_raw)
    query_norm = query_unit * query_gain
    key_norm = key_unit * key_gain
    query_rot = (
        (query_norm * cosine + rotate_half(query_norm) * sine)
        .astype(jnp.bfloat16)
        .reshape(seqs, rows, kv_heads, group, HD)
    )
    key_rot = (
        (key_norm * cosine + rotate_half(key_norm) * sine)
        .astype(jnp.bfloat16)
        .reshape(seqs, rows, kv_heads * HD)
    )

    def scores_at(key_piece, start):
        count = key_piece.shape[1]
        pos_key = token_positions(
            block_pairs, natural_row(start + jnp.arange(count, dtype=jnp.int32), rows)
        )
        keys = key_piece.reshape(seqs, count, kv_heads, HD)
        score = (
            jnp.einsum("bqkgd,bskd->bkgqs", query_rot, keys, preferred_element_type=jnp.float32)
            * factor
        )
        mask = pos_key[None, None, None, None, :] <= pos_query[None, None, None, :, None]
        return (score, mask, keys)

    def attend(carry, pieces, start):
        key_piece, value_piece = pieces
        count = key_piece.shape[1]
        score, mask, keys = scores_at(key_piece, start)
        weights = jnp.where(mask, jnp.exp(score), 0.0)
        total, summed = carry
        values = value_piece.reshape(seqs, count, kv_heads, HD)
        summed = summed + jnp.einsum(
            "bkgqs,bskd->bqkgd",
            weights.astype(jnp.bfloat16),
            values,
            preferred_element_type=jnp.float32,
        )
        return (total + jnp.sum(weights, axis=-1), summed)

    start_carry = (
        jnp.zeros((seqs, kv_heads, group, rows), jnp.float32),
        jnp.zeros((seqs, rows, kv_heads, group, HD), jnp.float32),
    )
    key_value = ctx_gather(jnp.concatenate([key_rot, value_rows], axis=2), 1)
    key_every = key_value[:, :, : kv_heads * HD]
    value_every = key_value[:, :, kv_heads * HD :]
    total, summed = over_blocks(attend, start_carry, (key_every, value_every))
    log_total = jnp.log(total)
    attn_heads = (summed / jnp.transpose(total, (0, 3, 1, 2))[..., None]).astype(jnp.bfloat16)
    attn_out = attn_heads.reshape(flat, heads * HD)
    middle_all = input_all + to_natural(add_rows(wide_dot(attn_out, output_all)))
    middle = lax.dynamic_slice_in_dim(middle_all, offset, local_width, 1)
    scale_ffn, unit_ffn = local_norm(middle_all)
    normed_ffn = to_gathered((unit_ffn * ffn_gain).astype(jnp.bfloat16))
    gate = wide_dot(normed_ffn, gate_all)
    up_proj = wide_dot(normed_ffn, up_all)
    sigmoid_gate = jax.nn.sigmoid(gate)
    activated = gate * sigmoid_gate
    mixed = (activated * up_proj).astype(jnp.bfloat16)
    block_out = (middle + share_rows(to_natural(wide_dot(mixed, down_all)))).astype(jnp.bfloat16)
    grad_flat = grad_output.reshape(flat, local_width)
    grad_full = full_rows(grad_flat)
    grad_full_gathered = to_gathered(grad_full)
    grad_mixed = wide_dot(grad_full_gathered, down_all.T)
    down_grad = wide_dot(mixed.T, grad_full_gathered)
    grad_gate = (grad_mixed * up_proj * sigmoid_gate * (1.0 + gate * (1.0 - sigmoid_gate))).astype(
        jnp.bfloat16
    )
    grad_up = (grad_mixed * activated).astype(jnp.bfloat16)
    gate_grad = wide_dot(normed_ffn.T, grad_gate)
    up_grad = wide_dot(normed_ffn.T, grad_up)
    ffn_pieces = (gate_grad, up_grad, down_grad.T)
    ffn_partial = start_sum_over_ctx(ffn_pieces)
    grad_normed_ffn = to_natural(
        add_rows_direct(wide_dot(grad_gate, gate_all.T) + wide_dot(grad_up, up_all.T))
    )
    back_ffn = local_back(grad_normed_ffn, unit_ffn, scale_ffn, ffn_gain)
    ffn_part = lax.dynamic_slice_in_dim(jnp.sum(grad_normed_ffn * unit_ffn, axis=0), offset, local_width)
    grad_middle_full = grad_full.astype(jnp.float32) + back_ffn
    grad_middle_all = to_gathered(grad_middle_full.astype(jnp.bfloat16))
    grad_attn = wide_dot(grad_middle_all, output_all.T).reshape(seqs, rows, kv_heads, group, HD)
    output_grad = wide_dot(attn_out.T, grad_middle_all)
    delta = jnp.transpose(
        jnp.sum(grad_attn * attn_heads.astype(jnp.float32), axis=-1), (0, 2, 3, 1)
    )
    grad_attn_low = grad_attn.astype(jnp.bfloat16)

    def revisit(grad_query_sum, pieces, start):
        key_piece, value_piece = pieces
        count = key_piece.shape[1]
        score, mask, keys = scores_at(key_piece, start)
        values = value_piece.reshape(seqs, count, kv_heads, HD)
        prob = jnp.where(mask, jnp.exp(score - log_total[..., None]), 0.0)
        grad_prob = jnp.einsum(
            "bqkgd,bskd->bkgqs", grad_attn_low, values, preferred_element_type=jnp.float32
        )
        grad_score = (prob * (grad_prob - delta[..., None]) * factor).astype(jnp.bfloat16)
        grad_query_sum = grad_query_sum + jnp.einsum(
            "bkgqs,bskd->bqkgd", grad_score, keys, preferred_element_type=jnp.float32
        )
        key_term = jnp.einsum(
            "bkgqs,bqkgd->bskd", grad_score, query_rot, preferred_element_type=jnp.float32
        )
        value_term = jnp.einsum(
            "bkgqs,bqkgd->bskd",
            prob.astype(jnp.bfloat16),
            grad_attn_low,
            preferred_element_type=jnp.float32,
        )
        return (
            grad_query_sum,
            jnp.concatenate(
                [
                    key_term.reshape(seqs, count, kv_heads * HD),
                    value_term.reshape(seqs, count, kv_heads * HD),
                ],
                2,
            ),
        )

    whole = key_every.shape[1]
    step = min(whole, 1024)

    def back_turn(grad_query_sum, index):
        start = index * step
        pieces = (
            lax.dynamic_slice_in_dim(key_every, start, step, 1),
            lax.dynamic_slice_in_dim(value_every, start, step, 1),
        )
        return revisit(grad_query_sum, pieces, start)

    grad_query_rot, key_terms = lax.scan(
        back_turn,
        jnp.zeros((seqs, rows, kv_heads, group, HD), jnp.float32),
        jnp.arange(whole // step, dtype=jnp.int32),
    )
    key_terms = jnp.transpose(key_terms, (1, 0, 2, 3)).reshape(seqs, whole, 2 * kv_heads * HD)
    key_terms, ffn_partial = lax.optimization_barrier((key_terms, ffn_partial))
    ffn_summed = finish_sum_over_ctx(ffn_partial, ffn_pieces)
    owned = (
        ctx_scatter(key_terms.astype(jnp.bfloat16), 1, AXIS_STAGES)
        .astype(jnp.float32)
        .reshape(flat, 2 * kv_heads * HD)
    )
    grad_key_rot = owned[:, : kv_heads * HD].reshape(flat, kv_heads, HD)
    grad_value_low = owned[:, kv_heads * HD :].astype(jnp.bfloat16)
    grad_query_rot = grad_query_rot.reshape(flat, heads, HD)
    grad_query_unit = grad_query_rot * cosine - rotate_half(grad_query_rot * sine)
    grad_key_unit = grad_key_rot * cosine - rotate_half(grad_key_rot * sine)
    query_gain_part = jnp.sum(grad_query_unit * query_unit, axis=(0, 1))
    key_gain_part = jnp.sum(grad_key_unit * key_unit, axis=(0, 1))
    grad_query = (
        head_back(grad_query_unit, query_unit, query_scale, query_gain)
        .astype(jnp.bfloat16)
        .reshape(flat, heads * HD)
    )
    grad_key = (
        head_back(grad_key_unit, key_unit, key_scale, key_gain)
        .astype(jnp.bfloat16)
        .reshape(flat, kv_heads * HD)
    )
    query_grad = wide_dot(normed_attn.T, grad_query)
    key_grad = wide_dot(normed_attn.T, grad_key)
    value_grad = wide_dot(normed_attn.T, grad_value_low)
    grad_normed_attn = to_natural(add_rows_direct(
        wide_dot(grad_query, query_all.T)
        + wide_dot(grad_key, key_all_w.T)
        + wide_dot(grad_value_low, value_all_w.T)
    ))
    back_attn = local_back(grad_normed_attn, unit_attn, scale_attn, attn_gain)
    attn_part = lax.dynamic_slice_in_dim(jnp.sum(grad_normed_attn * unit_attn, axis=0), offset, local_width)
    input_grad = lax.dynamic_slice_in_dim(grad_middle_full + back_attn, offset, local_width, 1)
    attn_pieces = (query_grad, key_grad, value_grad, output_grad.T)
    attn_partial = start_sum_over_ctx(attn_pieces, AXIS_STAGES[:2])
    attn_placed = lax.dynamic_update_slice_in_dim(
        jnp.zeros((width,), jnp.float32), attn_part, offset, 0
    )
    ffn_placed = lax.dynamic_update_slice_in_dim(
        jnp.zeros((width,), jnp.float32), ffn_part, offset, 0
    )
    gains = (attn_placed, query_gain_part, key_gain_part, ffn_placed)
    for names in (SHARD,) + tuple(reversed(CTX_AXES)):
        gains = lax.psum(gains, names)
    attn_partial, gains = lax.optimization_barrier((attn_partial, gains))
    query_grad, key_grad, value_grad, output_grad = finish_sum_over_ctx(
        attn_partial, attn_pieces, AXIS_STAGES[2:]
    )
    gate_grad, up_grad, down_grad = ffn_summed
    output_grad = output_grad.T
    down_grad = down_grad.T
    attn_gain_grad, query_gain_grad, key_gain_grad, ffn_gain_grad = gains
    block_out = block_out.reshape(seqs, rows, local_width)
    input_grad = input_grad.reshape(seqs, rows, local_width)
    return (
        block_out,
        input_grad,
        attn_gain_grad,
        query_gain_grad,
        key_gain_grad,
        ffn_gain_grad,
        query_grad,
        key_grad,
        value_grad,
        output_grad,
        gate_grad,
        up_grad,
        down_grad,
    )


def solution(mesh):
    ctx_size, shard_size = mesh.devices.shape
    fine = Mesh(mesh.devices.reshape(2, 4, ctx_size // 8, 2, shard_size // 2), EVERY)
    ctx = CTX_AXES
    in_specs = (
        P(None, ctx, SHARD),
        P(),
        P(),
        P(),
        P(),
        P(),
        P(ctx, SHARD),
        P(ctx, SHARD),
        P(ctx, SHARD),
        P(SHARD, ctx),
        P(ctx, SHARD),
        P(ctx, SHARD),
        P(SHARD, ctx),
        P(None, ctx, SHARD),
    )
    out_specs = (
        P(None, ctx, SHARD),
        P(None, ctx, SHARD),
        P(),
        P(),
        P(),
        P(),
        P(ctx, SHARD),
        P(ctx, SHARD),
        P(ctx, SHARD),
        P(SHARD, ctx),
        P(ctx, SHARD),
        P(ctx, SHARD),
        P(SHARD, ctx),
    )
    return jax.shard_map(
        per_device, mesh=fine, in_specs=in_specs, out_specs=out_specs, check_vma=False
    )
```

```python
import math

import jax
import jax.numpy as jnp
from jax import lax
from jax.sharding import Mesh, PartitionSpec as P

HD = 64
BLK = 64


EPSILON = 1e-05
ROPE_BASE = 1000000.0


def wide_dot(left, right):
    return jnp.dot(left, right, preferred_element_type=jnp.float32)


def token_positions(block_pairs, row_index):
    owner = row_index // (2 * BLK)
    half = row_index // BLK % 2
    devices = jnp.arange(block_pairs.shape[0], dtype=jnp.int32)
    chosen = jnp.where(half[:, None] == 0, block_pairs[None, :, 0], block_pairs[None, :, 1])
    number = jnp.sum(jnp.where(owner[:, None] == devices[None, :], chosen, 0), axis=1)
    return number * BLK + row_index % BLK


def rope_tables(positions):
    index = jnp.arange(HD // 2, dtype=jnp.float32)
    inverse = jnp.exp(index * (-2.0 * math.log(ROPE_BASE) / HD))
    angle = positions.astype(jnp.float32)[:, None] * inverse[None, :]
    cosine = jnp.cos(angle)
    sine = jnp.sin(angle)
    return (
        jnp.concatenate([cosine, cosine], 1)[:, None, :],
        jnp.concatenate([sine, sine], 1)[:, None, :],
    )


def rotate_half(values):
    middle = values.shape[-1] // 2
    return jnp.concatenate([-values[..., middle:], values[..., :middle]], -1)


def head_norm(values):
    scale = lax.rsqrt(jnp.mean(values * values, axis=-1, keepdims=True) + EPSILON)
    return (scale, values * scale)


def head_back(grad_normed, unit, scale, gain):
    scaled = grad_normed * gain
    inner = jnp.mean(scaled * unit, axis=-1, keepdims=True)
    return scale * (scaled - unit * inner)


CTX_AXES = ("cx", "cy", "cz")
SHARD = ("sx", "sc")
EVERY = CTX_AXES + SHARD


GATHER_STAGES = (("cx",), ("cy", "cz"))
SCATTER_STAGES = tuple(reversed(GATHER_STAGES))
GATHERED_ORDER = tuple(name for stage in reversed(GATHER_STAGES) for name in stage)
SCATTER_ORDER = tuple(name for stage in SCATTER_STAGES for name in stage)


def ctx_gather(local, axis):
    for names in GATHER_STAGES:
        local = lax.all_gather(local, names, axis=axis, tiled=True)
    return local


def pair_scatter(partial_value, axis, name):
    half = partial_value.shape[axis] // 2
    me = lax.axis_index(name)
    keep = lax.dynamic_slice_in_dim(partial_value, me * half, half, axis)
    send = lax.dynamic_slice_in_dim(partial_value, (1 - me) * half, half, axis)
    got = lax.ppermute(send, name, perm=[(0, 1), (1, 0)])
    return (keep.astype(jnp.float32) + got.astype(jnp.float32)).astype(partial_value.dtype)


def ctx_scatter(partial_value, axis, stages=SCATTER_STAGES):
    for names in stages:
        if len(names) == 1 and lax.axis_size(names[0]) == 2:
            partial_value = pair_scatter(partial_value, axis, names[0])
        else:
            partial_value = lax.psum_scatter(partial_value, names, scatter_dimension=axis, tiled=True)
    return partial_value


def reorder_blocks(values, axis, source, target):
    sizes = [lax.axis_size(name) for name in source]
    shape = values.shape
    block = shape[axis] // math.prod(sizes)
    split = values.reshape(shape[:axis] + tuple(sizes) + (block,) + shape[axis + 1 :])
    order = list(range(axis)) + [axis + source.index(name) for name in target]
    order += list(range(axis + len(source), split.ndim))
    return jnp.transpose(split, order).reshape(shape)


def natural_row(index, rows):
    device = index // rows
    place = {}
    for name in reversed(GATHERED_ORDER):
        size = lax.axis_size(name)
        place[name] = device % size
        device = device // size
    natural = 0
    for name in CTX_AXES:
        natural = natural * lax.axis_size(name) + place[name]
    return natural * rows + index % rows


AXIS_STAGES = tuple((name,) for name in SCATTER_ORDER)


def start_sum_over_ctx(pieces, stages=SCATTER_STAGES[:1]):
    joined = jnp.concatenate(pieces, axis=1).astype(jnp.bfloat16)
    return ctx_scatter(joined, 0, stages)


def finish_sum_over_ctx(partial_value, pieces, stages=SCATTER_STAGES[1:]):
    widths = [piece.shape[1] for piece in pieces]
    cuts = [sum(widths[:i]) for i in range(len(widths) + 1)]
    summed = ctx_scatter(partial_value, 0, stages).astype(jnp.float32)
    return [summed[:, cuts[i] : cuts[i + 1]] for i in range(len(pieces))]


def sum_over_ctx(pieces, stages=SCATTER_STAGES):
    return finish_sum_over_ctx(start_sum_over_ctx(pieces, stages[:1]), pieces, stages[1:])


def rows_total(partial_value):
    return lax.psum(partial_value, SHARD)


def full_rows(local):
    return lax.all_gather(local, SHARD, axis=1, tiled=True)


def share_rows(partial_value):
    shards = lax.axis_size(SHARD)
    rows, cols = partial_value.shape
    blocks = partial_value.astype(jnp.bfloat16).reshape(rows, shards, cols // shards)
    blocks = lax.all_to_all(blocks, SHARD, 1, 1, tiled=True)
    return jnp.sum(blocks.astype(jnp.float32), axis=1)


def add_rows(partial_value):
    pieces = lax.all_gather(partial_value.astype(jnp.bfloat16), SHARD, axis=0)
    return jnp.sum(pieces.astype(jnp.float32), axis=0)


def add_rows_direct(partial_value):
    owned = share_rows(partial_value)
    shards = lax.axis_size(SHARD)
    copies = jnp.broadcast_to(owned[None], (shards,) + owned.shape)
    blocks = lax.all_to_all(copies, SHARD, 0, 0, tiled=True)
    return jnp.transpose(blocks, (1, 0, 2)).reshape(owned.shape[0], shards * owned.shape[1])


def local_norm(values):
    scale = lax.rsqrt(jnp.mean(values * values, axis=1, keepdims=True) + EPSILON)
    return (scale, values * scale)


def local_back(grad_normed, unit, scale, gain):
    scaled = grad_normed * gain
    inner = jnp.mean(scaled * unit, axis=1, keepdims=True)
    return scale * (scaled - unit * inner)


def row_norm(values, width):
    total = rows_total(jnp.sum(values * values, axis=1))
    scale = lax.rsqrt(total / width + EPSILON)[:, None]
    return (scale, values * scale)


def norm_back(grad_normed, unit, scale, gain, width):
    scaled = grad_normed * gain
    inner = rows_total(jnp.sum(scaled * unit, axis=1)) / width
    return (scale * (scaled - unit * inner[:, None]), jnp.sum(grad_normed * unit, axis=0))


def over_blocks(step_fn, carry, arrays):
    whole = arrays[0].shape[1]
    step = min(whole, 512)

    def turn(index, state):
        start = index * step
        pieces = tuple((lax.dynamic_slice_in_dim(array, start, step, 1) for array in arrays))
        return step_fn(state, pieces, start)

    return lax.fori_loop(0, whole // step, turn, carry)


def per_device(
    block_in,
    block_pairs,
    attn_gain,
    query_gain,
    key_gain,
    ffn_gain,
    w_query,
    w_key,
    w_value,
    w_output,
    w_gate,
    w_up,
    w_down,
    grad_output,
):
    seqs, rows, local_width = block_in.shape
    flat = seqs * rows
    width = local_width * lax.axis_size(SHARD)
    offset = lax.axis_index(SHARD) * local_width
    pieces = (w_query, w_key, w_value, w_gate, w_up, w_output.T, w_down.T)
    widths = [piece.shape[1] for piece in pieces]
    cuts = [sum(widths[:i]) for i in range(len(widths) + 1)]
    every_weight = ctx_gather(jnp.concatenate(pieces, axis=1), 0)

    def to_gathered(values):
        return reorder_blocks(values, 1, CTX_AXES, GATHERED_ORDER)

    def to_natural(values):
        return reorder_blocks(values, 1, GATHERED_ORDER, CTX_AXES)
    gathered = [every_weight[:, cuts[i] : cuts[i + 1]] for i in range(len(pieces))]
    query_all, key_all_w, value_all_w, gate_all, up_all, output_all, down_all = gathered
    output_all = output_all.T
    down_all = down_all.T
    heads = query_all.shape[1] // HD
    kv_heads = key_all_w.shape[1] // HD
    group = heads // kv_heads
    factor = 1.0 / math.sqrt(HD)
    pos_query = token_positions(
        block_pairs, lax.axis_index(CTX_AXES) * rows + jnp.arange(rows, dtype=jnp.int32)
    )
    cosine_one, sine_one = rope_tables(pos_query)
    cosine = jnp.tile(cosine_one, (seqs, 1, 1))
    sine = jnp.tile(sine_one, (seqs, 1, 1))
    attn_slice = lax.dynamic_slice_in_dim(attn_gain, offset, local_width)
    ffn_slice = lax.dynamic_slice_in_dim(ffn_gain, offset, local_width)
    input_all = full_rows(block_in.reshape(flat, local_width)).astype(jnp.float32)
    scale_attn, unit_attn = local_norm(input_all)
    normed_attn = to_gathered((unit_attn * attn_gain).astype(jnp.bfloat16))
    query_raw = wide_dot(normed_attn, query_all).reshape(flat, heads, HD)
    key_raw = wide_dot(normed_attn, key_all_w).reshape(flat, kv_heads, HD)
    value_rows = (
        wide_dot(normed_attn, value_all_w).astype(jnp.bfloat16).reshape(seqs, rows, kv_heads * HD)
    )
    query_scale, query_unit = head_norm(query_raw)
    key_scale, key_unit = head_norm(key_raw)
    query_norm = query_unit * query_gain
    key_norm = key_unit * key_gain
    query_rot = (
        (query_norm * cosine + rotate_half(query_norm) * sine)
        .astype(jnp.bfloat16)
        .reshape(seqs, rows, kv_heads, group, HD)
    )
    key_rot = (
        (key_norm * cosine + rotate_half(key_norm) * sine)
        .astype(jnp.bfloat16)
        .reshape(seqs, rows, kv_heads * HD)
    )

    def scores_at(key_piece, start):
        count = key_piece.shape[1]
        pos_key = token_positions(
            block_pairs, natural_row(start + jnp.arange(count, dtype=jnp.int32), rows)
        )
        keys = key_piece.reshape(seqs, count, kv_heads, HD)
        score = (
            jnp.einsum("bqkgd,bskd->bkgqs", query_rot, keys, preferred_element_type=jnp.float32)
            * factor
        )
        mask = pos_key[None, None, None, None, :] <= pos_query[None, None, None, :, None]
        return (score, mask, keys)

    def attend(carry, pieces, start):
        key_piece, value_piece = pieces
        count = key_piece.shape[1]
        score, mask, keys = scores_at(key_piece, start)
        weights = jnp.where(mask, jnp.exp(score), 0.0)
        total, summed = carry
        values = value_piece.reshape(seqs, count, kv_heads, HD)
        summed = summed + jnp.einsum(
            "bkgqs,bskd->bqkgd",
            weights.astype(jnp.bfloat16),
            values,
            preferred_element_type=jnp.float32,
        )
        return (total + jnp.sum(weights, axis=-1), summed)

    start_carry = (
        jnp.zeros((seqs, kv_heads, group, rows), jnp.float32),
        jnp.zeros((seqs, rows, kv_heads, group, HD), jnp.float32),
    )
    key_value = ctx_gather(jnp.concatenate([key_rot, value_rows], axis=2), 1)
    key_every = key_value[:, :, : kv_heads * HD]
    value_every = key_value[:, :, kv_heads * HD :]
    total, summed = over_blocks(attend, start_carry, (key_every, value_every))
    log_total = jnp.log(total)
    attn_heads = (summed / jnp.transpose(total, (0, 3, 1, 2))[..., None]).astype(jnp.bfloat16)
    attn_out = attn_heads.reshape(flat, heads * HD)
    middle_all = input_all + to_natural(add_rows(wide_dot(attn_out, output_all)))
    middle = lax.dynamic_slice_in_dim(middle_all, offset, local_width, 1)
    scale_ffn, unit_ffn = local_norm(middle_all)
    normed_ffn = to_gathered((unit_ffn * ffn_gain).astype(jnp.bfloat16))
    gate = wide_dot(normed_ffn, gate_all)
    up_proj = wide_dot(normed_ffn, up_all)
    sigmoid_gate = jax.nn.sigmoid(gate)
    activated = gate * sigmoid_gate
    mixed = (activated * up_proj).astype(jnp.bfloat16)
    block_out = (middle + share_rows(to_natural(wide_dot(mixed, down_all)))).astype(jnp.bfloat16)
    grad_flat = grad_output.reshape(flat, local_width)
    grad_full = full_rows(grad_flat)
    grad_full_gathered = to_gathered(grad_full)
    grad_mixed = wide_dot(grad_full_gathered, down_all.T)
    down_grad = wide_dot(mixed.T, grad_full_gathered)
    grad_gate = (grad_mixed * up_proj * sigmoid_gate * (1.0 + gate * (1.0 - sigmoid_gate))).astype(
        jnp.bfloat16
    )
    grad_up = (grad_mixed * activated).astype(jnp.bfloat16)
    gate_grad = wide_dot(normed_ffn.T, grad_gate)
    up_grad = wide_dot(normed_ffn.T, grad_up)
    ffn_pieces = (gate_grad, up_grad, down_grad.T)
    ffn_partial = start_sum_over_ctx(ffn_pieces)
    grad_normed_ffn = to_natural(
        add_rows_direct(wide_dot(grad_gate, gate_all.T) + wide_dot(grad_up, up_all.T))
    )
    back_ffn = local_back(grad_normed_ffn, unit_ffn, scale_ffn, ffn_gain)
    ffn_part = lax.dynamic_slice_in_dim(jnp.sum(grad_normed_ffn * unit_ffn, axis=0), offset, local_width)
    grad_middle_full = grad_full.astype(jnp.float32) + back_ffn
    grad_middle_all = to_gathered(grad_middle_full.astype(jnp.bfloat16))
    grad_attn = wide_dot(grad_middle_all, output_all.T).reshape(seqs, rows, kv_heads, group, HD)
    output_grad = wide_dot(attn_out.T, grad_middle_all)
    delta = jnp.transpose(
        jnp.sum(grad_attn * attn_heads.astype(jnp.float32), axis=-1), (0, 2, 3, 1)
    )
    grad_attn_low = grad_attn.astype(jnp.bfloat16)

    def revisit(grad_query_sum, pieces, start):
        key_piece, value_piece = pieces
        count = key_piece.shape[1]
        score, mask, keys = scores_at(key_piece, start)
        values = value_piece.reshape(seqs, count, kv_heads, HD)
        prob = jnp.where(mask, jnp.exp(score - log_total[..., None]), 0.0)
        grad_prob = jnp.einsum(
            "bqkgd,bskd->bkgqs", grad_attn_low, values, preferred_element_type=jnp.float32
        )
        grad_score = (prob * (grad_prob - delta[..., None]) * factor).astype(jnp.bfloat16)
        grad_query_sum = grad_query_sum + jnp.einsum(
            "bkgqs,bskd->bqkgd", grad_score, keys, preferred_element_type=jnp.float32
        )
        key_term = jnp.einsum(
            "bkgqs,bqkgd->bskd", grad_score, query_rot, preferred_element_type=jnp.float32
        )
        value_term = jnp.einsum(
            "bkgqs,bqkgd->bskd",
            prob.astype(jnp.bfloat16),
            grad_attn_low,
            preferred_element_type=jnp.float32,
        )
        return (
            grad_query_sum,
            jnp.concatenate(
                [
                    key_term.reshape(seqs, count, kv_heads * HD),
                    value_term.reshape(seqs, count, kv_heads * HD),
                ],
                2,
            ),
        )

    whole = key_every.shape[1]
    step = min(whole, 512)

    def back_turn(grad_query_sum, index):
        start = index * step
        pieces = (
            lax.dynamic_slice_in_dim(key_every, start, step, 1),
            lax.dynamic_slice_in_dim(value_every, start, step, 1),
        )
        return revisit(grad_query_sum, pieces, start)

    grad_query_rot, key_terms = lax.scan(
        back_turn,
        jnp.zeros((seqs, rows, kv_heads, group, HD), jnp.float32),
        jnp.arange(whole // step, dtype=jnp.int32),
    )
    key_terms = jnp.transpose(key_terms, (1, 0, 2, 3)).reshape(seqs, whole, 2 * kv_heads * HD)
    key_terms, ffn_partial = lax.optimization_barrier((key_terms, ffn_partial))
    ffn_summed = finish_sum_over_ctx(ffn_partial, ffn_pieces)
    owned = (
        ctx_scatter(key_terms.astype(jnp.bfloat16), 1, AXIS_STAGES)
        .astype(jnp.float32)
        .reshape(flat, 2 * kv_heads * HD)
    )
    grad_key_rot = owned[:, : kv_heads * HD].reshape(flat, kv_heads, HD)
    grad_value_low = owned[:, kv_heads * HD :].astype(jnp.bfloat16)
    grad_query_rot = grad_query_rot.reshape(flat, heads, HD)
    grad_query_unit = grad_query_rot * cosine - rotate_half(grad_query_rot * sine)
    grad_key_unit = grad_key_rot * cosine - rotate_half(grad_key_rot * sine)
    query_gain_part = jnp.sum(grad_query_unit * query_unit, axis=(0, 1))
    key_gain_part = jnp.sum(grad_key_unit * key_unit, axis=(0, 1))
    grad_query = (
        head_back(grad_query_unit, query_unit, query_scale, query_gain)
        .astype(jnp.bfloat16)
        .reshape(flat, heads * HD)
    )
    grad_key = (
        head_back(grad_key_unit, key_unit, key_scale, key_gain)
        .astype(jnp.bfloat16)
        .reshape(flat, kv_heads * HD)
    )
    query_grad = wide_dot(normed_attn.T, grad_query)
    key_grad = wide_dot(normed_attn.T, grad_key)
    value_grad = wide_dot(normed_attn.T, grad_value_low)
    grad_normed_attn = to_natural(add_rows_direct(
        wide_dot(grad_query, query_all.T)
        + wide_dot(grad_key, key_all_w.T)
        + wide_dot(grad_value_low, value_all_w.T)
    ))
    back_attn = local_back(grad_normed_attn, unit_attn, scale_attn, attn_gain)
    attn_part = lax.dynamic_slice_in_dim(jnp.sum(grad_normed_attn * unit_attn, axis=0), offset, local_width)
    input_grad = lax.dynamic_slice_in_dim(grad_middle_full + back_attn, offset, local_width, 1)
    attn_pieces = (query_grad, key_grad, value_grad, output_grad.T)
    attn_partial = start_sum_over_ctx(attn_pieces, AXIS_STAGES[:2])
    attn_placed = lax.dynamic_update_slice_in_dim(
        jnp.zeros((width,), jnp.float32), attn_part, offset, 0
    )
    ffn_placed = lax.dynamic_update_slice_in_dim(
        jnp.zeros((width,), jnp.float32), ffn_part, offset, 0
    )
    gains = (attn_placed, query_gain_part, key_gain_part, ffn_placed)
    for names in (SHARD,) + tuple(reversed(CTX_AXES)):
        gains = lax.psum(gains, names)
    attn_partial, gains = lax.optimization_barrier((attn_partial, gains))
    query_grad, key_grad, value_grad, output_grad = finish_sum_over_ctx(
        attn_partial, attn_pieces, AXIS_STAGES[2:]
    )
    gate_grad, up_grad, down_grad = ffn_summed
    output_grad = output_grad.T
    down_grad = down_grad.T
    attn_gain_grad, query_gain_grad, key_gain_grad, ffn_gain_grad = gains
    block_out = block_out.reshape(seqs, rows, local_width)
    input_grad = input_grad.reshape(seqs, rows, local_width)
    return (
        block_out,
        input_grad,
        attn_gain_grad,
        query_gain_grad,
        key_gain_grad,
        ffn_gain_grad,
        query_grad,
        key_grad,
        value_grad,
        output_grad,
        gate_grad,
        up_grad,
        down_grad,
    )


def solution(mesh):
    ctx_size, shard_size = mesh.devices.shape
    fine = Mesh(mesh.devices.reshape(2, 4, ctx_size // 8, 2, shard_size // 2), EVERY)
    ctx = CTX_AXES
    in_specs = (
        P(None, ctx, SHARD),
        P(),
        P(),
        P(),
        P(),
        P(),
        P(ctx, SHARD),
        P(ctx, SHARD),
        P(ctx, SHARD),
        P(SHARD, ctx),
        P(ctx, SHARD),
        P(ctx, SHARD),
        P(SHARD, ctx),
        P(None, ctx, SHARD),
    )
    out_specs = (
        P(None, ctx, SHARD),
        P(None, ctx, SHARD),
        P(),
        P(),
        P(),
        P(),
        P(ctx, SHARD),
        P(ctx, SHARD),
        P(ctx, SHARD),
        P(SHARD, ctx),
        P(ctx, SHARD),
        P(ctx, SHARD),
        P(SHARD, ctx),
    )
    return jax.shard_map(
        per_device, mesh=fine, in_specs=in_specs, out_specs=out_specs, check_vma=False
    )
```

```python
import math

import jax
import jax.numpy as jnp
from jax import lax
from jax.sharding import Mesh, PartitionSpec as P

HD = 64
BLK = 64


EPSILON = 1e-05
ROPE_BASE = 1000000.0


def wide_dot(left, right):
    return jnp.dot(left, right, preferred_element_type=jnp.float32)


def token_positions(block_pairs, row_index):
    owner = row_index // (2 * BLK)
    half = row_index // BLK % 2
    devices = jnp.arange(block_pairs.shape[0], dtype=jnp.int32)
    chosen = jnp.where(half[:, None] == 0, block_pairs[None, :, 0], block_pairs[None, :, 1])
    number = jnp.sum(jnp.where(owner[:, None] == devices[None, :], chosen, 0), axis=1)
    return number * BLK + row_index % BLK


def rope_tables(positions):
    index = jnp.arange(HD // 2, dtype=jnp.float32)
    inverse = jnp.exp(index * (-2.0 * math.log(ROPE_BASE) / HD))
    angle = positions.astype(jnp.float32)[:, None] * inverse[None, :]
    cosine = jnp.cos(angle)
    sine = jnp.sin(angle)
    return (
        jnp.concatenate([cosine, cosine], 1)[:, None, :],
        jnp.concatenate([sine, sine], 1)[:, None, :],
    )


def rotate_half(values):
    middle = values.shape[-1] // 2
    return jnp.concatenate([-values[..., middle:], values[..., :middle]], -1)


def head_norm(values):
    scale = lax.rsqrt(jnp.mean(values * values, axis=-1, keepdims=True) + EPSILON)
    return (scale, values * scale)


def head_back(grad_normed, unit, scale, gain):
    scaled = grad_normed * gain
    inner = jnp.mean(scaled * unit, axis=-1, keepdims=True)
    return scale * (scaled - unit * inner)


CTX_AXES = ("cx", "cy", "cz")
SHARD = ("sx", "sc")
EVERY = CTX_AXES + SHARD


GATHER_STAGES = (("cx",), ("cy", "cz"))
SCATTER_STAGES = tuple(reversed(GATHER_STAGES))
GATHERED_ORDER = tuple(name for stage in reversed(GATHER_STAGES) for name in stage)
SCATTER_ORDER = tuple(name for stage in SCATTER_STAGES for name in stage)


def ctx_gather(local, axis):
    for names in GATHER_STAGES:
        local = lax.all_gather(local, names, axis=axis, tiled=True)
    return local


def pair_scatter(partial_value, axis, name):
    half = partial_value.shape[axis] // 2
    me = lax.axis_index(name)
    keep = lax.dynamic_slice_in_dim(partial_value, me * half, half, axis)
    send = lax.dynamic_slice_in_dim(partial_value, (1 - me) * half, half, axis)
    got = lax.ppermute(send, name, perm=[(0, 1), (1, 0)])
    return (keep.astype(jnp.float32) + got.astype(jnp.float32)).astype(partial_value.dtype)


def ctx_scatter(partial_value, axis, stages=SCATTER_STAGES):
    for names in stages:
        if len(names) == 1 and lax.axis_size(names[0]) == 2:
            partial_value = pair_scatter(partial_value, axis, names[0])
        else:
            partial_value = lax.psum_scatter(partial_value, names, scatter_dimension=axis, tiled=True)
    return partial_value


def reorder_blocks(values, axis, source, target):
    sizes = [lax.axis_size(name) for name in source]
    shape = values.shape
    block = shape[axis] // math.prod(sizes)
    split = values.reshape(shape[:axis] + tuple(sizes) + (block,) + shape[axis + 1 :])
    order = list(range(axis)) + [axis + source.index(name) for name in target]
    order += list(range(axis + len(source), split.ndim))
    return jnp.transpose(split, order).reshape(shape)


def natural_row(index, rows):
    device = index // rows
    place = {}
    for name in reversed(GATHERED_ORDER):
        size = lax.axis_size(name)
        place[name] = device % size
        device = device // size
    natural = 0
    for name in CTX_AXES:
        natural = natural * lax.axis_size(name) + place[name]
    return natural * rows + index % rows


AXIS_STAGES = tuple((name,) for name in SCATTER_ORDER)


def start_sum_over_ctx(pieces, stages=SCATTER_STAGES[:1]):
    joined = jnp.concatenate(pieces, axis=1).astype(jnp.bfloat16)
    return ctx_scatter(joined, 0, stages)


def finish_sum_over_ctx(partial_value, pieces, stages=SCATTER_STAGES[1:]):
    widths = [piece.shape[1] for piece in pieces]
    cuts = [sum(widths[:i]) for i in range(len(widths) + 1)]
    summed = ctx_scatter(partial_value, 0, stages).astype(jnp.float32)
    return [summed[:, cuts[i] : cuts[i + 1]] for i in range(len(pieces))]


def sum_over_ctx(pieces, stages=SCATTER_STAGES):
    return finish_sum_over_ctx(start_sum_over_ctx(pieces, stages[:1]), pieces, stages[1:])


def rows_total(partial_value):
    return lax.psum(partial_value, SHARD)


def full_rows(local):
    return lax.all_gather(local, SHARD, axis=1, tiled=True)


def share_rows(partial_value):
    shards = lax.axis_size(SHARD)
    rows, cols = partial_value.shape
    blocks = partial_value.astype(jnp.bfloat16).reshape(rows, shards, cols // shards)
    blocks = lax.all_to_all(blocks, SHARD, 1, 1, tiled=True)
    return jnp.sum(blocks.astype(jnp.float32), axis=1)


def add_rows(partial_value):
    pieces = lax.all_gather(partial_value.astype(jnp.bfloat16), SHARD, axis=0)
    return jnp.sum(pieces.astype(jnp.float32), axis=0)


def add_rows_direct(partial_value):
    owned = share_rows(partial_value)
    shards = lax.axis_size(SHARD)
    copies = jnp.broadcast_to(owned[None], (shards,) + owned.shape)
    blocks = lax.all_to_all(copies, SHARD, 0, 0, tiled=True)
    return jnp.transpose(blocks, (1, 0, 2)).reshape(owned.shape[0], shards * owned.shape[1])


def local_norm(values):
    scale = lax.rsqrt(jnp.mean(values * values, axis=1, keepdims=True) + EPSILON)
    return (scale, values * scale)


def local_back(grad_normed, unit, scale, gain):
    scaled = grad_normed * gain
    inner = jnp.mean(scaled * unit, axis=1, keepdims=True)
    return scale * (scaled - unit * inner)


def row_norm(values, width):
    total = rows_total(jnp.sum(values * values, axis=1))
    scale = lax.rsqrt(total / width + EPSILON)[:, None]
    return (scale, values * scale)


def norm_back(grad_normed, unit, scale, gain, width):
    scaled = grad_normed * gain
    inner = rows_total(jnp.sum(scaled * unit, axis=1)) / width
    return (scale * (scaled - unit * inner[:, None]), jnp.sum(grad_normed * unit, axis=0))


def over_blocks(step_fn, carry, arrays):
    whole = arrays[0].shape[1]
    step = min(whole, 2048)

    def turn(index, state):
        start = index * step
        pieces = tuple((lax.dynamic_slice_in_dim(array, start, step, 1) for array in arrays))
        return step_fn(state, pieces, start)

    return lax.fori_loop(0, whole // step, turn, carry)


def per_device(
    block_in,
    block_pairs,
    attn_gain,
    query_gain,
    key_gain,
    ffn_gain,
    w_query,
    w_key,
    w_value,
    w_output,
    w_gate,
    w_up,
    w_down,
    grad_output,
):
    seqs, rows, local_width = block_in.shape
    flat = seqs * rows
    width = local_width * lax.axis_size(SHARD)
    offset = lax.axis_index(SHARD) * local_width
    pieces = (w_query, w_key, w_value, w_gate, w_up, w_output.T, w_down.T)
    widths = [piece.shape[1] for piece in pieces]
    cuts = [sum(widths[:i]) for i in range(len(widths) + 1)]
    every_weight = ctx_gather(jnp.concatenate(pieces, axis=1), 0)

    def to_gathered(values):
        return reorder_blocks(values, 1, CTX_AXES, GATHERED_ORDER)

    def to_natural(values):
        return reorder_blocks(values, 1, GATHERED_ORDER, CTX_AXES)
    gathered = [every_weight[:, cuts[i] : cuts[i + 1]] for i in range(len(pieces))]
    query_all, key_all_w, value_all_w, gate_all, up_all, output_all, down_all = gathered
    output_all = output_all.T
    down_all = down_all.T
    heads = query_all.shape[1] // HD
    kv_heads = key_all_w.shape[1] // HD
    group = heads // kv_heads
    factor = 1.0 / math.sqrt(HD)
    pos_query = token_positions(
        block_pairs, lax.axis_index(CTX_AXES) * rows + jnp.arange(rows, dtype=jnp.int32)
    )
    cosine_one, sine_one = rope_tables(pos_query)
    cosine = jnp.tile(cosine_one, (seqs, 1, 1))
    sine = jnp.tile(sine_one, (seqs, 1, 1))
    attn_slice = lax.dynamic_slice_in_dim(attn_gain, offset, local_width)
    ffn_slice = lax.dynamic_slice_in_dim(ffn_gain, offset, local_width)
    input_all = full_rows(block_in.reshape(flat, local_width)).astype(jnp.float32)
    scale_attn, unit_attn = local_norm(input_all)
    normed_attn = to_gathered((unit_attn * attn_gain).astype(jnp.bfloat16))
    query_raw = wide_dot(normed_attn, query_all).reshape(flat, heads, HD)
    key_raw = wide_dot(normed_attn, key_all_w).reshape(flat, kv_heads, HD)
    value_rows = (
        wide_dot(normed_attn, value_all_w).astype(jnp.bfloat16).reshape(seqs, rows, kv_heads * HD)
    )
    query_scale, query_unit = head_norm(query_raw)
    key_scale, key_unit = head_norm(key_raw)
    query_norm = query_unit * query_gain
    key_norm = key_unit * key_gain
    query_rot = (
        (query_norm * cosine + rotate_half(query_norm) * sine)
        .astype(jnp.bfloat16)
        .reshape(seqs, rows, kv_heads, group, HD)
    )
    key_rot = (
        (key_norm * cosine + rotate_half(key_norm) * sine)
        .astype(jnp.bfloat16)
        .reshape(seqs, rows, kv_heads * HD)
    )

    def scores_at(key_piece, start):
        count = key_piece.shape[1]
        pos_key = token_positions(
            block_pairs, natural_row(start + jnp.arange(count, dtype=jnp.int32), rows)
        )
        keys = key_piece.reshape(seqs, count, kv_heads, HD)
        score = (
            jnp.einsum("bqkgd,bskd->bkgqs", query_rot, keys, preferred_element_type=jnp.float32)
            * factor
        )
        mask = pos_key[None, None, None, None, :] <= pos_query[None, None, None, :, None]
        return (score, mask, keys)

    def attend(carry, pieces, start):
        key_piece, value_piece = pieces
        count = key_piece.shape[1]
        score, mask, keys = scores_at(key_piece, start)
        weights = jnp.where(mask, jnp.exp(score), 0.0)
        total, summed = carry
        values = value_piece.reshape(seqs, count, kv_heads, HD)
        summed = summed + jnp.einsum(
            "bkgqs,bskd->bqkgd",
            weights.astype(jnp.bfloat16),
            values,
            preferred_element_type=jnp.float32,
        )
        return (total + jnp.sum(weights, axis=-1), summed)

    start_carry = (
        jnp.zeros((seqs, kv_heads, group, rows), jnp.float32),
        jnp.zeros((seqs, rows, kv_heads, group, HD), jnp.float32),
    )
    key_value = ctx_gather(jnp.concatenate([key_rot, value_rows], axis=2), 1)
    key_every = key_value[:, :, : kv_heads * HD]
    value_every = key_value[:, :, kv_heads * HD :]
    total, summed = over_blocks(attend, start_carry, (key_every, value_every))
    log_total = jnp.log(total)
    attn_heads = (summed / jnp.transpose(total, (0, 3, 1, 2))[..., None]).astype(jnp.bfloat16)
    attn_out = attn_heads.reshape(flat, heads * HD)
    middle_all = input_all + to_natural(add_rows(wide_dot(attn_out, output_all)))
    middle = lax.dynamic_slice_in_dim(middle_all, offset, local_width, 1)
    scale_ffn, unit_ffn = local_norm(middle_all)
    normed_ffn = to_gathered((unit_ffn * ffn_gain).astype(jnp.bfloat16))
    gate = wide_dot(normed_ffn, gate_all)
    up_proj = wide_dot(normed_ffn, up_all)
    sigmoid_gate = jax.nn.sigmoid(gate)
    activated = gate * sigmoid_gate
    mixed = (activated * up_proj).astype(jnp.bfloat16)
    block_out = (middle + share_rows(to_natural(wide_dot(mixed, down_all)))).astype(jnp.bfloat16)
    grad_flat = grad_output.reshape(flat, local_width)
    grad_full = full_rows(grad_flat)
    grad_full_gathered = to_gathered(grad_full)
    grad_mixed = wide_dot(grad_full_gathered, down_all.T)
    down_grad = wide_dot(mixed.T, grad_full_gathered)
    grad_gate = (grad_mixed * up_proj * sigmoid_gate * (1.0 + gate * (1.0 - sigmoid_gate))).astype(
        jnp.bfloat16
    )
    grad_up = (grad_mixed * activated).astype(jnp.bfloat16)
    gate_grad = wide_dot(normed_ffn.T, grad_gate)
    up_grad = wide_dot(normed_ffn.T, grad_up)
    ffn_pieces = (gate_grad, up_grad, down_grad.T)
    ffn_partial = start_sum_over_ctx(ffn_pieces)
    grad_normed_ffn = to_natural(
        add_rows_direct(wide_dot(grad_gate, gate_all.T) + wide_dot(grad_up, up_all.T))
    )
    back_ffn = local_back(grad_normed_ffn, unit_ffn, scale_ffn, ffn_gain)
    ffn_part = lax.dynamic_slice_in_dim(jnp.sum(grad_normed_ffn * unit_ffn, axis=0), offset, local_width)
    grad_middle_full = grad_full.astype(jnp.float32) + back_ffn
    grad_middle_all = to_gathered(grad_middle_full.astype(jnp.bfloat16))
    grad_attn = wide_dot(grad_middle_all, output_all.T).reshape(seqs, rows, kv_heads, group, HD)
    output_grad = wide_dot(attn_out.T, grad_middle_all)
    delta = jnp.transpose(
        jnp.sum(grad_attn * attn_heads.astype(jnp.float32), axis=-1), (0, 2, 3, 1)
    )
    grad_attn_low = grad_attn.astype(jnp.bfloat16)

    def revisit(grad_query_sum, pieces, start):
        key_piece, value_piece = pieces
        count = key_piece.shape[1]
        score, mask, keys = scores_at(key_piece, start)
        values = value_piece.reshape(seqs, count, kv_heads, HD)
        prob = jnp.where(mask, jnp.exp(score - log_total[..., None]), 0.0)
        grad_prob = jnp.einsum(
            "bqkgd,bskd->bkgqs", grad_attn_low, values, preferred_element_type=jnp.float32
        )
        grad_score = (prob * (grad_prob - delta[..., None]) * factor).astype(jnp.bfloat16)
        grad_query_sum = grad_query_sum + jnp.einsum(
            "bkgqs,bskd->bqkgd", grad_score, keys, preferred_element_type=jnp.float32
        )
        key_term = jnp.einsum(
            "bkgqs,bqkgd->bskd", grad_score, query_rot, preferred_element_type=jnp.float32
        )
        value_term = jnp.einsum(
            "bkgqs,bqkgd->bskd",
            prob.astype(jnp.bfloat16),
            grad_attn_low,
            preferred_element_type=jnp.float32,
        )
        return (
            grad_query_sum,
            jnp.concatenate(
                [
                    key_term.reshape(seqs, count, kv_heads * HD),
                    value_term.reshape(seqs, count, kv_heads * HD),
                ],
                2,
            ),
        )

    whole = key_every.shape[1]
    step = min(whole, 2048)

    def back_turn(grad_query_sum, index):
        start = index * step
        pieces = (
            lax.dynamic_slice_in_dim(key_every, start, step, 1),
            lax.dynamic_slice_in_dim(value_every, start, step, 1),
        )
        return revisit(grad_query_sum, pieces, start)

    grad_query_rot, key_terms = lax.scan(
        back_turn,
        jnp.zeros((seqs, rows, kv_heads, group, HD), jnp.float32),
        jnp.arange(whole // step, dtype=jnp.int32),
    )
    key_terms = jnp.transpose(key_terms, (1, 0, 2, 3)).reshape(seqs, whole, 2 * kv_heads * HD)
    key_terms, ffn_partial = lax.optimization_barrier((key_terms, ffn_partial))
    ffn_summed = finish_sum_over_ctx(ffn_partial, ffn_pieces)
    owned = (
        ctx_scatter(key_terms.astype(jnp.bfloat16), 1, AXIS_STAGES)
        .astype(jnp.float32)
        .reshape(flat, 2 * kv_heads * HD)
    )
    grad_key_rot = owned[:, : kv_heads * HD].reshape(flat, kv_heads, HD)
    grad_value_low = owned[:, kv_heads * HD :].astype(jnp.bfloat16)
    grad_query_rot = grad_query_rot.reshape(flat, heads, HD)
    grad_query_unit = grad_query_rot * cosine - rotate_half(grad_query_rot * sine)
    grad_key_unit = grad_key_rot * cosine - rotate_half(grad_key_rot * sine)
    query_gain_part = jnp.sum(grad_query_unit * query_unit, axis=(0, 1))
    key_gain_part = jnp.sum(grad_key_unit * key_unit, axis=(0, 1))
    grad_query = (
        head_back(grad_query_unit, query_unit, query_scale, query_gain)
        .astype(jnp.bfloat16)
        .reshape(flat, heads * HD)
    )
    grad_key = (
        head_back(grad_key_unit, key_unit, key_scale, key_gain)
        .astype(jnp.bfloat16)
        .reshape(flat, kv_heads * HD)
    )
    query_grad = wide_dot(normed_attn.T, grad_query)
    key_grad = wide_dot(normed_attn.T, grad_key)
    value_grad = wide_dot(normed_attn.T, grad_value_low)
    grad_normed_attn = to_natural(add_rows_direct(
        wide_dot(grad_query, query_all.T)
        + wide_dot(grad_key, key_all_w.T)
        + wide_dot(grad_value_low, value_all_w.T)
    ))
    back_attn = local_back(grad_normed_attn, unit_attn, scale_attn, attn_gain)
    attn_part = lax.dynamic_slice_in_dim(jnp.sum(grad_normed_attn * unit_attn, axis=0), offset, local_width)
    input_grad = lax.dynamic_slice_in_dim(grad_middle_full + back_attn, offset, local_width, 1)
    attn_pieces = (query_grad, key_grad, value_grad, output_grad.T)
    attn_partial = start_sum_over_ctx(attn_pieces, AXIS_STAGES[:2])
    attn_placed = lax.dynamic_update_slice_in_dim(
        jnp.zeros((width,), jnp.float32), attn_part, offset, 0
    )
    ffn_placed = lax.dynamic_update_slice_in_dim(
        jnp.zeros((width,), jnp.float32), ffn_part, offset, 0
    )
    gains = (attn_placed, query_gain_part, key_gain_part, ffn_placed)
    for names in (SHARD,) + tuple(reversed(CTX_AXES)):
        gains = lax.psum(gains, names)
    attn_partial, gains = lax.optimization_barrier((attn_partial, gains))
    query_grad, key_grad, value_grad, output_grad = finish_sum_over_ctx(
        attn_partial, attn_pieces, AXIS_STAGES[2:]
    )
    gate_grad, up_grad, down_grad = ffn_summed
    output_grad = output_grad.T
    down_grad = down_grad.T
    attn_gain_grad, query_gain_grad, key_gain_grad, ffn_gain_grad = gains
    block_out = block_out.reshape(seqs, rows, local_width)
    input_grad = input_grad.reshape(seqs, rows, local_width)
    return (
        block_out,
        input_grad,
        attn_gain_grad,
        query_gain_grad,
        key_gain_grad,
        ffn_gain_grad,
        query_grad,
        key_grad,
        value_grad,
        output_grad,
        gate_grad,
        up_grad,
        down_grad,
    )


def solution(mesh):
    ctx_size, shard_size = mesh.devices.shape
    fine = Mesh(mesh.devices.reshape(2, 4, ctx_size // 8, 2, shard_size // 2), EVERY)
    ctx = CTX_AXES
    in_specs = (
        P(None, ctx, SHARD),
        P(),
        P(),
        P(),
        P(),
        P(),
        P(ctx, SHARD),
        P(ctx, SHARD),
        P(ctx, SHARD),
        P(SHARD, ctx),
        P(ctx, SHARD),
        P(ctx, SHARD),
        P(SHARD, ctx),
        P(None, ctx, SHARD),
    )
    out_specs = (
        P(None, ctx, SHARD),
        P(None, ctx, SHARD),
        P(),
        P(),
        P(),
        P(),
        P(ctx, SHARD),
        P(ctx, SHARD),
        P(ctx, SHARD),
        P(SHARD, ctx),
        P(ctx, SHARD),
        P(ctx, SHARD),
        P(SHARD, ctx),
    )
    return jax.shard_map(
        per_device, mesh=fine, in_specs=in_specs, out_specs=out_specs, check_vma=False
    )
```

```python
import math

import jax
import jax.numpy as jnp
from jax import lax
from jax.sharding import Mesh, PartitionSpec as P

HD = 64
BLK = 64


EPSILON = 1e-05
ROPE_BASE = 1000000.0


def wide_dot(left, right):
    return jnp.dot(left, right, preferred_element_type=jnp.float32)


def token_positions(block_pairs, row_index):
    owner = row_index // (2 * BLK)
    half = row_index // BLK % 2
    devices = jnp.arange(block_pairs.shape[0], dtype=jnp.int32)
    chosen = jnp.where(half[:, None] == 0, block_pairs[None, :, 0], block_pairs[None, :, 1])
    number = jnp.sum(jnp.where(owner[:, None] == devices[None, :], chosen, 0), axis=1)
    return number * BLK + row_index % BLK


def rope_tables(positions):
    index = jnp.arange(HD // 2, dtype=jnp.float32)
    inverse = jnp.exp(index * (-2.0 * math.log(ROPE_BASE) / HD))
    angle = positions.astype(jnp.float32)[:, None] * inverse[None, :]
    cosine = jnp.cos(angle)
    sine = jnp.sin(angle)
    return (
        jnp.concatenate([cosine, cosine], 1)[:, None, :],
        jnp.concatenate([sine, sine], 1)[:, None, :],
    )


def rotate_half(values):
    middle = values.shape[-1] // 2
    return jnp.concatenate([-values[..., middle:], values[..., :middle]], -1)


def head_norm(values):
    scale = lax.rsqrt(jnp.mean(values * values, axis=-1, keepdims=True) + EPSILON)
    return (scale, values * scale)


def head_back(grad_normed, unit, scale, gain):
    scaled = grad_normed * gain
    inner = jnp.mean(scaled * unit, axis=-1, keepdims=True)
    return scale * (scaled - unit * inner)


CTX_AXES = ("cx", "cy", "cz")
SHARD = ("sx", "sc")
EVERY = CTX_AXES + SHARD


GATHER_STAGES = (("cx",), ("cy", "cz"))
SCATTER_STAGES = tuple(reversed(GATHER_STAGES))
GATHERED_ORDER = tuple(name for stage in reversed(GATHER_STAGES) for name in stage)
SCATTER_ORDER = tuple(name for stage in SCATTER_STAGES for name in stage)


def ctx_gather(local, axis):
    for names in GATHER_STAGES:
        local = lax.all_gather(local, names, axis=axis, tiled=True)
    return local


def pair_scatter(partial_value, axis, name):
    half = partial_value.shape[axis] // 2
    me = lax.axis_index(name)
    keep = lax.dynamic_slice_in_dim(partial_value, me * half, half, axis)
    send = lax.dynamic_slice_in_dim(partial_value, (1 - me) * half, half, axis)
    got = lax.ppermute(send, name, perm=[(0, 1), (1, 0)])
    return (keep.astype(jnp.float32) + got.astype(jnp.float32)).astype(partial_value.dtype)


def ctx_scatter(partial_value, axis, stages=SCATTER_STAGES):
    for names in stages:
        if len(names) == 1 and lax.axis_size(names[0]) == 2:
            partial_value = pair_scatter(partial_value, axis, names[0])
        else:
            partial_value = lax.psum_scatter(partial_value, names, scatter_dimension=axis, tiled=True)
    return partial_value


def reorder_blocks(values, axis, source, target):
    sizes = [lax.axis_size(name) for name in source]
    shape = values.shape
    block = shape[axis] // math.prod(sizes)
    split = values.reshape(shape[:axis] + tuple(sizes) + (block,) + shape[axis + 1 :])
    order = list(range(axis)) + [axis + source.index(name) for name in target]
    order += list(range(axis + len(source), split.ndim))
    return jnp.transpose(split, order).reshape(shape)


def natural_row(index, rows):
    device = index // rows
    place = {}
    for name in reversed(GATHERED_ORDER):
        size = lax.axis_size(name)
        place[name] = device % size
        device = device // size
    natural = 0
    for name in CTX_AXES:
        natural = natural * lax.axis_size(name) + place[name]
    return natural * rows + index % rows


AXIS_STAGES = tuple((name,) for name in SCATTER_ORDER)


def start_sum_over_ctx(pieces, stages=SCATTER_STAGES[:1]):
    joined = jnp.concatenate(pieces, axis=1).astype(jnp.bfloat16)
    return ctx_scatter(joined, 0, stages)


def finish_sum_over_ctx(partial_value, pieces, stages=SCATTER_STAGES[1:]):
    widths = [piece.shape[1] for piece in pieces]
    cuts = [sum(widths[:i]) for i in range(len(widths) + 1)]
    summed = ctx_scatter(partial_value, 0, stages).astype(jnp.float32)
    return [summed[:, cuts[i] : cuts[i + 1]] for i in range(len(pieces))]


def sum_over_ctx(pieces, stages=SCATTER_STAGES):
    return finish_sum_over_ctx(start_sum_over_ctx(pieces, stages[:1]), pieces, stages[1:])


def rows_total(partial_value):
    return lax.psum(partial_value, SHARD)


def full_rows(local):
    return lax.all_gather(local, SHARD, axis=1, tiled=True)


def share_rows(partial_value):
    shards = lax.axis_size(SHARD)
    rows, cols = partial_value.shape
    blocks = partial_value.astype(jnp.bfloat16).reshape(rows, shards, cols // shards)
    blocks = lax.all_to_all(blocks, SHARD, 1, 1, tiled=True)
    return jnp.sum(blocks.astype(jnp.float32), axis=1)


def add_rows(partial_value):
    pieces = lax.all_gather(partial_value.astype(jnp.bfloat16), SHARD, axis=0)
    return jnp.sum(pieces.astype(jnp.float32), axis=0)


def add_rows_direct(partial_value):
    owned = share_rows(partial_value)
    shards = lax.axis_size(SHARD)
    copies = jnp.broadcast_to(owned[None], (shards,) + owned.shape)
    blocks = lax.all_to_all(copies, SHARD, 0, 0, tiled=True)
    return jnp.transpose(blocks, (1, 0, 2)).reshape(owned.shape[0], shards * owned.shape[1])


def local_norm(values):
    scale = lax.rsqrt(jnp.mean(values * values, axis=1, keepdims=True) + EPSILON)
    return (scale, values * scale)


def local_back(grad_normed, unit, scale, gain):
    scaled = grad_normed * gain
    inner = jnp.mean(scaled * unit, axis=1, keepdims=True)
    return scale * (scaled - unit * inner)


def row_norm(values, width):
    total = rows_total(jnp.sum(values * values, axis=1))
    scale = lax.rsqrt(total / width + EPSILON)[:, None]
    return (scale, values * scale)


def norm_back(grad_normed, unit, scale, gain, width):
    scaled = grad_normed * gain
    inner = rows_total(jnp.sum(scaled * unit, axis=1)) / width
    return (scale * (scaled - unit * inner[:, None]), jnp.sum(grad_normed * unit, axis=0))


def over_blocks(step_fn, carry, arrays):
    whole = arrays[0].shape[1]
    step = min(whole, 4096)

    def turn(index, state):
        start = index * step
        pieces = tuple((lax.dynamic_slice_in_dim(array, start, step, 1) for array in arrays))
        return step_fn(state, pieces, start)

    return lax.fori_loop(0, whole // step, turn, carry)


def per_device(
    block_in,
    block_pairs,
    attn_gain,
    query_gain,
    key_gain,
    ffn_gain,
    w_query,
    w_key,
    w_value,
    w_output,
    w_gate,
    w_up,
    w_down,
    grad_output,
):
    seqs, rows, local_width = block_in.shape
    flat = seqs * rows
    width = local_width * lax.axis_size(SHARD)
    offset = lax.axis_index(SHARD) * local_width
    pieces = (w_query, w_key, w_value, w_gate, w_up, w_output.T, w_down.T)
    widths = [piece.shape[1] for piece in pieces]
    cuts = [sum(widths[:i]) for i in range(len(widths) + 1)]
    every_weight = ctx_gather(jnp.concatenate(pieces, axis=1), 0)

    def to_gathered(values):
        return reorder_blocks(values, 1, CTX_AXES, GATHERED_ORDER)

    def to_natural(values):
        return reorder_blocks(values, 1, GATHERED_ORDER, CTX_AXES)
    gathered = [every_weight[:, cuts[i] : cuts[i + 1]] for i in range(len(pieces))]
    query_all, key_all_w, value_all_w, gate_all, up_all, output_all, down_all = gathered
    output_all = output_all.T
    down_all = down_all.T
    heads = query_all.shape[1] // HD
    kv_heads = key_all_w.shape[1] // HD
    group = heads // kv_heads
    factor = 1.0 / math.sqrt(HD)
    pos_query = token_positions(
        block_pairs, lax.axis_index(CTX_AXES) * rows + jnp.arange(rows, dtype=jnp.int32)
    )
    cosine_one, sine_one = rope_tables(pos_query)
    cosine = jnp.tile(cosine_one, (seqs, 1, 1))
    sine = jnp.tile(sine_one, (seqs, 1, 1))
    attn_slice = lax.dynamic_slice_in_dim(attn_gain, offset, local_width)
    ffn_slice = lax.dynamic_slice_in_dim(ffn_gain, offset, local_width)
    input_all = full_rows(block_in.reshape(flat, local_width)).astype(jnp.float32)
    scale_attn, unit_attn = local_norm(input_all)
    normed_attn = to_gathered((unit_attn * attn_gain).astype(jnp.bfloat16))
    query_raw = wide_dot(normed_attn, query_all).reshape(flat, heads, HD)
    key_raw = wide_dot(normed_attn, key_all_w).reshape(flat, kv_heads, HD)
    value_rows = (
        wide_dot(normed_attn, value_all_w).astype(jnp.bfloat16).reshape(seqs, rows, kv_heads * HD)
    )
    query_scale, query_unit = head_norm(query_raw)
    key_scale, key_unit = head_norm(key_raw)
    query_norm = query_unit * query_gain
    key_norm = key_unit * key_gain
    query_rot = (
        (query_norm * cosine + rotate_half(query_norm) * sine)
        .astype(jnp.bfloat16)
        .reshape(seqs, rows, kv_heads, group, HD)
    )
    key_rot = (
        (key_norm * cosine + rotate_half(key_norm) * sine)
        .astype(jnp.bfloat16)
        .reshape(seqs, rows, kv_heads * HD)
    )

    def scores_at(key_piece, start):
        count = key_piece.shape[1]
        pos_key = token_positions(
            block_pairs, natural_row(start + jnp.arange(count, dtype=jnp.int32), rows)
        )
        keys = key_piece.reshape(seqs, count, kv_heads, HD)
        score = (
            jnp.einsum("bqkgd,bskd->bkgqs", query_rot, keys, preferred_element_type=jnp.float32)
            * factor
        )
        mask = pos_key[None, None, None, None, :] <= pos_query[None, None, None, :, None]
        return (score, mask, keys)

    def attend(carry, pieces, start):
        key_piece, value_piece = pieces
        count = key_piece.shape[1]
        score, mask, keys = scores_at(key_piece, start)
        weights = jnp.where(mask, jnp.exp(score), 0.0)
        total, summed = carry
        values = value_piece.reshape(seqs, count, kv_heads, HD)
        summed = summed + jnp.einsum(
            "bkgqs,bskd->bqkgd",
            weights.astype(jnp.bfloat16),
            values,
            preferred_element_type=jnp.float32,
        )
        return (total + jnp.sum(weights, axis=-1), summed)

    start_carry = (
        jnp.zeros((seqs, kv_heads, group, rows), jnp.float32),
        jnp.zeros((seqs, rows, kv_heads, group, HD), jnp.float32),
    )
    key_value = ctx_gather(jnp.concatenate([key_rot, value_rows], axis=2), 1)
    key_every = key_value[:, :, : kv_heads * HD]
    value_every = key_value[:, :, kv_heads * HD :]
    total, summed = over_blocks(attend, start_carry, (key_every, value_every))
    log_total = jnp.log(total)
    attn_heads = (summed / jnp.transpose(total, (0, 3, 1, 2))[..., None]).astype(jnp.bfloat16)
    attn_out = attn_heads.reshape(flat, heads * HD)
    middle_all = input_all + to_natural(add_rows(wide_dot(attn_out, output_all)))
    middle = lax.dynamic_slice_in_dim(middle_all, offset, local_width, 1)
    scale_ffn, unit_ffn = local_norm(middle_all)
    normed_ffn = to_gathered((unit_ffn * ffn_gain).astype(jnp.bfloat16))
    gate = wide_dot(normed_ffn, gate_all)
    up_proj = wide_dot(normed_ffn, up_all)
    sigmoid_gate = jax.nn.sigmoid(gate)
    activated = gate * sigmoid_gate
    mixed = (activated * up_proj).astype(jnp.bfloat16)
    block_out = (middle + share_rows(to_natural(wide_dot(mixed, down_all)))).astype(jnp.bfloat16)
    grad_flat = grad_output.reshape(flat, local_width)
    grad_full = full_rows(grad_flat)
    grad_full_gathered = to_gathered(grad_full)
    grad_mixed = wide_dot(grad_full_gathered, down_all.T)
    down_grad = wide_dot(mixed.T, grad_full_gathered)
    grad_gate = (grad_mixed * up_proj * sigmoid_gate * (1.0 + gate * (1.0 - sigmoid_gate))).astype(
        jnp.bfloat16
    )
    grad_up = (grad_mixed * activated).astype(jnp.bfloat16)
    gate_grad = wide_dot(normed_ffn.T, grad_gate)
    up_grad = wide_dot(normed_ffn.T, grad_up)
    ffn_pieces = (gate_grad, up_grad, down_grad.T)
    ffn_partial = start_sum_over_ctx(ffn_pieces)
    grad_normed_ffn = to_natural(
        add_rows_direct(wide_dot(grad_gate, gate_all.T) + wide_dot(grad_up, up_all.T))
    )
    back_ffn = local_back(grad_normed_ffn, unit_ffn, scale_ffn, ffn_gain)
    ffn_part = lax.dynamic_slice_in_dim(jnp.sum(grad_normed_ffn * unit_ffn, axis=0), offset, local_width)
    grad_middle_full = grad_full.astype(jnp.float32) + back_ffn
    grad_middle_all = to_gathered(grad_middle_full.astype(jnp.bfloat16))
    grad_attn = wide_dot(grad_middle_all, output_all.T).reshape(seqs, rows, kv_heads, group, HD)
    output_grad = wide_dot(attn_out.T, grad_middle_all)
    delta = jnp.transpose(
        jnp.sum(grad_attn * attn_heads.astype(jnp.float32), axis=-1), (0, 2, 3, 1)
    )
    grad_attn_low = grad_attn.astype(jnp.bfloat16)

    def revisit(grad_query_sum, pieces, start):
        key_piece, value_piece = pieces
        count = key_piece.shape[1]
        score, mask, keys = scores_at(key_piece, start)
        values = value_piece.reshape(seqs, count, kv_heads, HD)
        prob = jnp.where(mask, jnp.exp(score - log_total[..., None]), 0.0)
        grad_prob = jnp.einsum(
            "bqkgd,bskd->bkgqs", grad_attn_low, values, preferred_element_type=jnp.float32
        )
        grad_score = (prob * (grad_prob - delta[..., None]) * factor).astype(jnp.bfloat16)
        grad_query_sum = grad_query_sum + jnp.einsum(
            "bkgqs,bskd->bqkgd", grad_score, keys, preferred_element_type=jnp.float32
        )
        key_term = jnp.einsum(
            "bkgqs,bqkgd->bskd", grad_score, query_rot, preferred_element_type=jnp.float32
        )
        value_term = jnp.einsum(
            "bkgqs,bqkgd->bskd",
            prob.astype(jnp.bfloat16),
            grad_attn_low,
            preferred_element_type=jnp.float32,
        )
        return (
            grad_query_sum,
            jnp.concatenate(
                [
                    key_term.reshape(seqs, count, kv_heads * HD),
                    value_term.reshape(seqs, count, kv_heads * HD),
                ],
                2,
            ),
        )

    whole = key_every.shape[1]
    step = min(whole, 4096)

    def back_turn(grad_query_sum, index):
        start = index * step
        pieces = (
            lax.dynamic_slice_in_dim(key_every, start, step, 1),
            lax.dynamic_slice_in_dim(value_every, start, step, 1),
        )
        return revisit(grad_query_sum, pieces, start)

    grad_query_rot, key_terms = lax.scan(
        back_turn,
        jnp.zeros((seqs, rows, kv_heads, group, HD), jnp.float32),
        jnp.arange(whole // step, dtype=jnp.int32),
    )
    key_terms = jnp.transpose(key_terms, (1, 0, 2, 3)).reshape(seqs, whole, 2 * kv_heads * HD)
    key_terms, ffn_partial = lax.optimization_barrier((key_terms, ffn_partial))
    ffn_summed = finish_sum_over_ctx(ffn_partial, ffn_pieces)
    owned = (
        ctx_scatter(key_terms.astype(jnp.bfloat16), 1, AXIS_STAGES)
        .astype(jnp.float32)
        .reshape(flat, 2 * kv_heads * HD)
    )
    grad_key_rot = owned[:, : kv_heads * HD].reshape(flat, kv_heads, HD)
    grad_value_low = owned[:, kv_heads * HD :].astype(jnp.bfloat16)
    grad_query_rot = grad_query_rot.reshape(flat, heads, HD)
    grad_query_unit = grad_query_rot * cosine - rotate_half(grad_query_rot * sine)
    grad_key_unit = grad_key_rot * cosine - rotate_half(grad_key_rot * sine)
    query_gain_part = jnp.sum(grad_query_unit * query_unit, axis=(0, 1))
    key_gain_part = jnp.sum(grad_key_unit * key_unit, axis=(0, 1))
    grad_query = (
        head_back(grad_query_unit, query_unit, query_scale, query_gain)
        .astype(jnp.bfloat16)
        .reshape(flat, heads * HD)
    )
    grad_key = (
        head_back(grad_key_unit, key_unit, key_scale, key_gain)
        .astype(jnp.bfloat16)
        .reshape(flat, kv_heads * HD)
    )
    query_grad = wide_dot(normed_attn.T, grad_query)
    key_grad = wide_dot(normed_attn.T, grad_key)
    value_grad = wide_dot(normed_attn.T, grad_value_low)
    grad_normed_attn = to_natural(add_rows_direct(
        wide_dot(grad_query, query_all.T)
        + wide_dot(grad_key, key_all_w.T)
        + wide_dot(grad_value_low, value_all_w.T)
    ))
    back_attn = local_back(grad_normed_attn, unit_attn, scale_attn, attn_gain)
    attn_part = lax.dynamic_slice_in_dim(jnp.sum(grad_normed_attn * unit_attn, axis=0), offset, local_width)
    input_grad = lax.dynamic_slice_in_dim(grad_middle_full + back_attn, offset, local_width, 1)
    attn_pieces = (query_grad, key_grad, value_grad, output_grad.T)
    attn_partial = start_sum_over_ctx(attn_pieces, AXIS_STAGES[:2])
    attn_placed = lax.dynamic_update_slice_in_dim(
        jnp.zeros((width,), jnp.float32), attn_part, offset, 0
    )
    ffn_placed = lax.dynamic_update_slice_in_dim(
        jnp.zeros((width,), jnp.float32), ffn_part, offset, 0
    )
    gains = (attn_placed, query_gain_part, key_gain_part, ffn_placed)
    for names in (SHARD,) + tuple(reversed(CTX_AXES)):
        gains = lax.psum(gains, names)
    attn_partial, gains = lax.optimization_barrier((attn_partial, gains))
    query_grad, key_grad, value_grad, output_grad = finish_sum_over_ctx(
        attn_partial, attn_pieces, AXIS_STAGES[2:]
    )
    gate_grad, up_grad, down_grad = ffn_summed
    output_grad = output_grad.T
    down_grad = down_grad.T
    attn_gain_grad, query_gain_grad, key_gain_grad, ffn_gain_grad = gains
    block_out = block_out.reshape(seqs, rows, local_width)
    input_grad = input_grad.reshape(seqs, rows, local_width)
    return (
        block_out,
        input_grad,
        attn_gain_grad,
        query_gain_grad,
        key_gain_grad,
        ffn_gain_grad,
        query_grad,
        key_grad,
        value_grad,
        output_grad,
        gate_grad,
        up_grad,
        down_grad,
    )


def solution(mesh):
    ctx_size, shard_size = mesh.devices.shape
    fine = Mesh(mesh.devices.reshape(2, 4, ctx_size // 8, 2, shard_size // 2), EVERY)
    ctx = CTX_AXES
    in_specs = (
        P(None, ctx, SHARD),
        P(),
        P(),
        P(),
        P(),
        P(),
        P(ctx, SHARD),
        P(ctx, SHARD),
        P(ctx, SHARD),
        P(SHARD, ctx),
        P(ctx, SHARD),
        P(ctx, SHARD),
        P(SHARD, ctx),
        P(None, ctx, SHARD),
    )
    out_specs = (
        P(None, ctx, SHARD),
        P(None, ctx, SHARD),
        P(),
        P(),
        P(),
        P(),
        P(ctx, SHARD),
        P(ctx, SHARD),
        P(ctx, SHARD),
        P(SHARD, ctx),
        P(ctx, SHARD),
        P(ctx, SHARD),
        P(SHARD, ctx),
    )
    return jax.shard_map(
        per_device, mesh=fine, in_specs=in_specs, out_specs=out_specs, check_vma=False
    )
```
